32 devices in a mesh: pipe: 8 (over z, x), fsdp: 4 (over y, core).
Axes of the slice: x: 2, y: 2, z: 4, core: 2. Of those that a mesh axis runs over, the one named last changes fastest.
Arguments:
- frames_in: bfloat16 [64, 384, 768], P(('pipe', 'fsdp')), may hold values from -6 to 6
- attn_in: bfloat16 [2, 768, 2304], P(None, 'fsdp'), may hold values from -0.21875 to 0.21875
- q_bias: bfloat16 [2, 768], P(None, 'fsdp'), may hold values from -1.796875 to 1.796875
- attn_out: bfloat16 [2, 768, 768], P(None, 'fsdp'), may hold values from -2.5 to 2.5
- out_bias: bfloat16 [2, 768], P(None, 'fsdp'), may hold values from -1.796875 to 1.796875
- norm1_gain: bfloat16 [2, 768], P(None, 'fsdp'), may hold values from 0.5 to 1.5
- norm1_bias: bfloat16 [2, 768], P(None, 'fsdp'), may hold values from -1.796875 to 1.796875
- ffn_up: bfloat16 [2, 768, 3072], P(None, 'fsdp'), may hold values from -0.21875 to 0.21875
- up_bias: bfloat16 [2, 3072], P(None, 'fsdp'), may hold values from -1.796875 to 1.796875
- ffn_down: bfloat16 [2, 3072, 768], P(None, 'fsdp'), may hold values from -0.21875 to 0.21875
- down_bias: bfloat16 [2, 768], P(None, 'fsdp'), may hold values from -1.796875 to 1.796875
- norm2_gain: bfloat16 [2, 768], P(None, 'fsdp'), may hold values from 0.5 to 1.5
- norm2_bias: bfloat16 [2, 768], P(None, 'fsdp'), may hold values from -1.796875 to 1.796875
- subnet: int32 [4, 4], replicated, may hold values from 0 to 2, as said below
- out_cotangent: bfloat16 [64, 384, 768], P(('pipe', 'fsdp')), may hold values from -6 to 6
Outputs:
- layer_out: bfloat16 [64, 384, 768], P(('pipe', 'fsdp'))
- input_grad: bfloat16 [64, 384, 768], P(('pipe', 'fsdp'))
- grad_attn_in: float32 [2, 768, 2304], P(None, 'fsdp')
- grad_q_bias: float32 [2, 768], P(None, 'fsdp')
- grad_attn_out: float32 [2, 768, 768], P(None, 'fsdp')
- grad_out_bias: float32 [2, 768], P(None, 'fsdp')
- grad_norm1_gain: float32 [2, 768], P(None, 'fsdp')
- grad_norm1_bias: float32 [2, 768], P(None, 'fsdp')
- grad_ffn_up: float32 [2, 768, 3072], P(None, 'fsdp')
- grad_up_bias: float32 [2, 3072], P(None, 'fsdp')
- grad_ffn_down: float32 [2, 3072, 768], P(None, 'fsdp')
- grad_down_bias: float32 [2, 768], P(None, 'fsdp')
- grad_norm2_gain: float32 [2, 768], P(None, 'fsdp')
- grad_norm2_bias: float32 [2, 768], P(None, 'fsdp')
The draws below stay inside these ranges and needn't reach their ends.
Inputs may be any that keep to these rules, and one draw needn't show every extreme that they name: `subnet`: rows 0, 1 and 2 hold indices of width, head count and feed-forward ratio; row 3 holds the skip flag. Exactly one micro-batch has skip flag 1, and some micro-batch with skip flag 0 has index 2 in rows 0, 1 and 2.
All inputs are finite; a program needn't handle non-finite values.
Results may differ from the reference program's by a relative error of at most 0.02.
Values may be sent and summed in bfloat16 or wider, within the bound.
A program may use at most 256 MiB of HBM per device.

```python
import jax
import jax.numpy as jnp
from jax import lax

D = 768
FF = 3072
HEADS = 12
HEAD_DIM = 64
FRAMES = 384
ITEMS_DEV = 2
MICRO = 4
ITEMS = 64


def draw_subnet(key, part):
    draw_order = jax.random.permutation(jax.random.fold_in(key, 11), MICRO)
    pick_codes = jax.random.randint(jax.random.fold_in(key, 12), (3, MICRO), 0, 3)
    pick_codes = jnp.where(draw_order[None, :] == 1, 2, pick_codes)
    skip_flags = (draw_order == 0).astype(jnp.int32)
    return jnp.concatenate([pick_codes, skip_flags[None, :]], axis=0).astype(jnp.int32)


def shard_levels(stream_key, dims, cuts, least, high):
    def one(axis_at, parts):
        steps = jax.random.uniform(jax.random.fold_in(jax.random.fold_in(stream_key, 6), axis_at), (parts,), jnp.float32, least / len(cuts), high / len(cuts))
        return jnp.repeat(jnp.exp(steps), dims[axis_at] // parts).reshape((-1,) + (1,) * (len(dims) - axis_at - 1))

    factor_of = one(*cuts[0])
    for cut in cuts[1:]:
        factor_of = factor_of * one(*cut)
    return factor_of


def noise(own_key, shape, deviation, bound, cuts=(), kind=jnp.bfloat16):
    factor_of = shard_levels(own_key, shape, cuts, -0.22, 0.18) if cuts else 1.0
    values = jax.random.normal(own_key, shape, jnp.float32) * deviation * factor_of
    return jnp.minimum(jnp.maximum(values, -bound), bound).astype(kind)


def setup_inputs(seed: int = 0) -> dict:
    key_of = jax.random.split(jax.random.key(seed), 16)
    return {
        "frames_in": noise(key_of[0], (ITEMS, FRAMES, D), 1.0, 6.0, ((0, 32),)),
        "attn_in": noise(key_of[1], (2, D, 3 * D), D ** -0.5, 0.21875, ((1, 4),)),
        "q_bias": noise(key_of[2], (2, D), 0.3, 1.796875, ((1, 4),)),
        "attn_out": noise(key_of[3], (2, D, D), (max(D // 128, 1)) ** -0.5, 2.5, ((1, 4),)),
        "out_bias": noise(key_of[4], (2, D), 0.3, 1.796875, ((1, 4),)),
        "norm1_gain": jnp.clip(1.0 + 0.1 * jax.random.normal(key_of[5], (2, D), jnp.float32), 0.5, 1.5).astype(jnp.bfloat16),
        "norm1_bias": noise(key_of[6], (2, D), 0.3, 1.796875, ((1, 4),)),
        "ffn_up": noise(key_of[7], (2, D, FF), D ** -0.5, 0.21875, ((1, 4),)),
        "up_bias": noise(key_of[8], (2, FF), 0.3, 1.796875, ((1, 4),)),
        "ffn_down": noise(key_of[9], (2, FF, D), (FF // 4) ** -0.5, 0.21875, ((1, 4),)),
        "down_bias": noise(key_of[10], (2, D), 0.3, 1.796875, ((1, 4),)),
        "norm2_gain": jnp.clip(1.0 + 0.1 * jax.random.normal(key_of[11], (2, D), jnp.float32), 0.5, 1.5).astype(jnp.bfloat16),
        "norm2_bias": noise(key_of[12], (2, D), 0.3, 1.796875, ((1, 4),)),
        "subnet": draw_subnet(jax.random.fold_in(key_of[15], 71), 0),
        "out_cotangent": noise(key_of[14], (ITEMS, FRAMES, D), 1.0, 6.0, ((0, 32),)),
    }


@jax.custom_vjp
def low(v):
    return lax.optimization_barrier(v.astype(jnp.bfloat16)).astype(jnp.float32)

@jax.custom_vjp
def low_back(v):
    return v

def low_keep(v):
    return (low(v), None)

def low_pass(kept, grad):
    return (grad,)

def back_keep(v):
    return (v, None)

def back_low(kept, grad):
    return (low(grad),)
low.defvjp(low_keep, low_pass)
low_back.defvjp(back_keep, back_low)
EPSILON = 1e-05
PRECISE = lax.Precision.HIGHEST

def matmul_high(left, right):
    return jnp.dot(left, right, precision=PRECISE, preferred_element_type=jnp.float32)

def masks_from_codes(subnet_codes, model_width, ff_width):
    width_now = model_width * (4 + subnet_codes[0]) // 6
    active = HEAD_DIM * (HEADS * (4 + subnet_codes[1]) // 6)
    unit_count = width_now * (6 + subnet_codes[2]) // 2
    lane_ids = jnp.arange(model_width, dtype=jnp.int32)
    chan_mask = (lane_ids < width_now).astype(jnp.float32)
    head_lanes = (lane_ids < active).astype(jnp.float32)
    head_mask = jnp.concatenate([head_lanes, head_lanes, head_lanes])
    unit_mask = (jnp.arange(ff_width, dtype=jnp.int32) < unit_count).astype(jnp.float32)
    return (chan_mask, head_mask, unit_mask, width_now.astype(jnp.float32))

def norm_rows(rows_in, gain_vec, shift_vec, chan_mask, width_count):
    mean_val = lax.optimization_barrier(jnp.sum(rows_in * chan_mask, axis=-1, keepdims=True)) / width_count
    centered = (rows_in - mean_val) * chan_mask
    variance = lax.optimization_barrier(jnp.sum(centered * centered, axis=-1, keepdims=True)) / width_count
    return (centered * lax.rsqrt(variance + EPSILON) * gain_vec + shift_vec) * chan_mask

def layer_ref(layer_in, weights, mask_set):
    w_qkv, b_q, w_out, b_out, gain_first, bias_first, w_up, b_up, w_down, b_down, gain_second, bias_second = weights
    chan_mask, head_mask, unit_mask, width_count = mask_set
    frames = layer_in.shape[0]
    model_width = layer_in.shape[1]
    masked_in = layer_in * chan_mask
    bias_all = jnp.concatenate([b_q, jnp.zeros((2 * model_width,), jnp.float32)])
    proj_qkv = low(low_back((matmul_high(masked_in, w_qkv) + bias_all) * head_mask))
    split_heads = proj_qkv.reshape(frames, 3, HEADS, model_width // HEADS)
    query_rows = split_heads[:, 0]
    keys_rows = split_heads[:, 1]
    value_rows = split_heads[:, 2]
    scores = low_back(jnp.einsum('qhd,khd->hqk', query_rows, keys_rows, precision=PRECISE) * HEAD_DIM ** (-0.5))
    probs_all = jax.nn.softmax(scores, axis=-1)
    mixed_heads = jnp.einsum('hqk,khd->qhd', low(probs_all), value_rows, precision=PRECISE).reshape(frames, model_width)
    mixed_heads = low(low_back(mixed_heads))
    attn_branch = low_back((matmul_high(mixed_heads, w_out) + b_out) * chan_mask)
    first_norm = norm_rows(masked_in + attn_branch, gain_first, bias_first, chan_mask, width_count)
    hidden = low_back((matmul_high(low(first_norm), w_up) + b_up) * unit_mask)
    activated = low(jax.nn.gelu(hidden, approximate=False))
    ffn_branch = low_back((matmul_high(activated, w_down) + b_down) * chan_mask)
    return norm_rows(first_norm + ffn_branch, gain_second, bias_second, chan_mask, width_count)

def reference(frames_in, attn_in, q_bias, attn_out, out_bias, norm1_gain, norm1_bias, ffn_up, up_bias, ffn_down, down_bias, norm2_gain, norm2_bias, subnet, out_cotangent):
    weights = tuple((weight_part.astype(jnp.float32) for weight_part in (attn_in, q_bias, attn_out, out_bias, norm1_gain, norm1_bias, ffn_up, up_bias, ffn_down, down_bias, norm2_gain, norm2_bias)))
    item_total = frames_in.shape[0]
    model_width = frames_in.shape[2]
    ff_width = ffn_up.shape[2]
    item_ids = jnp.arange(item_total, dtype=jnp.int32)
    micro_ids = 2 * item_ids // item_total * ITEMS_DEV + item_ids % ITEMS_DEV
    item_codes = subnet[:, micro_ids].T

    def forward(rows_all, stacked):

        def one_item(item_pair):
            item_rows, item_code = item_pair
            mask_set = masks_from_codes(item_code, model_width, ff_width)
            layer_zero = tuple((weight_part[0] for weight_part in stacked))
            layer_one = tuple((weight_part[1] for weight_part in stacked))
            first_in = low_back(item_rows)
            middle = low(low_back(layer_ref(first_in, layer_zero, mask_set)))
            final_out = layer_ref(middle, layer_one, mask_set)
            return jnp.where(item_code[3] == 1, middle, final_out)
        return lax.map(jax.checkpoint(one_item), (rows_all, item_codes))
    result, pullback = jax.vjp(forward, frames_in.astype(jnp.float32), weights)
    d_rows, d_stacked = pullback(out_cotangent.astype(jnp.float32))
    return (result.astype(jnp.bfloat16), d_rows.astype(jnp.bfloat16), d_stacked[0], d_stacked[1], d_stacked[2], d_stacked[3], d_stacked[4], d_stacked[5], d_stacked[6], d_stacked[7], d_stacked[8], d_stacked[9], d_stacked[10], d_stacked[11])
```

```python
import functools

import jax
import jax.numpy as jnp
from jax import lax
from jax.experimental import pallas as pl
from jax.experimental.pallas import tpu as pltpu
from jax.sharding import PartitionSpec as P

HEADS = 12
HEAD_DIM = 64
EPSILON = 1e-05
LANES = 128
UNIT_CHUNK = 512
BF = jnp.bfloat16
F32 = jnp.float32

ROW_QB, ROW_OB, ROW_G1, ROW_B1, ROW_DB, ROW_G2, ROW_B2, ROW_UB = 0, 1, 2, 3, 4, 5, 6, 7

def dot_nn(a, b):
    return lax.dot_general(a, b, (((1,), (0,)), ((), ())), preferred_element_type=F32)


def dot_nt(a, b):
    return lax.dot_general(a, b, (((1,), (1,)), ((), ())), preferred_element_type=F32)


def dot_tn(a, b):
    return lax.dot_general(a, b, (((0,), (0,)), ((), ())), preferred_element_type=F32)


def lane_mask(width, count):
    return (lax.broadcasted_iota(jnp.int32, (1, width), 1) < count).astype(F32)


def normed(rows, cm, inv_w):
    mean = jnp.sum(rows * cm, axis=-1, keepdims=True) * inv_w
    centered = (rows - mean) * cm
    var = jnp.sum(centered * centered, axis=-1, keepdims=True) * inv_w
    rstd = lax.rsqrt(var + EPSILON)
    return centered * rstd, rstd


def norm_back(dy, xhat, rstd, gain, cm, inv_w):
    dym = dy * cm
    dg = jnp.sum(dym * xhat, axis=0, keepdims=True)
    ds = jnp.sum(dym, axis=0, keepdims=True)
    dx = dym * gain
    m1 = jnp.sum(dx, axis=-1, keepdims=True) * inv_w
    m2 = jnp.sum(dx * xhat, axis=-1, keepdims=True) * inv_w
    return cm * (rstd * (dx - m1 - xhat * m2)), dg, ds


class Attn:
    def __init__(self, layer, refs, w, sems):
        w_in, w_out = refs
        d = w.shape[1]
        self.copies = [
            pltpu.make_async_copy(w_in.at[layer, :, pl.ds(b * d, d)], w.at[b], sems.at[b]) for b in range(3)
        ] + [pltpu.make_async_copy(w_out.at[layer], w.at[3], sems.at[3])]

    def start(self, order):
        for b in order:
            self.copies[b].start()

    def wait(self, b):
        self.copies[b].wait()


class Ffn:
    def __init__(self, layer, refs, w_up, w_down, sems):
        up, down = refs
        d = w_up.shape[0]
        self.blocks = w_up.shape[1] // d
        self.first = [b * d // UNIT_CHUNK for b in range(self.blocks)]
        self.copies = [(
            pltpu.make_async_copy(up.at[layer, :, pl.ds(b * d, d)], w_up.at[:, pl.ds(b * d, d)], sems.at[b, 0]),
            pltpu.make_async_copy(down.at[layer, pl.ds(b * d, d)], w_down.at[pl.ds(b * d, d)], sems.at[b, 1]),
        ) for b in range(self.blocks)]

    def start(self):
        for pair in self.copies:
            for copy in pair:
                copy.start()

    def wait(self, b):
        for copy in self.copies[b]:
            copy.wait()

    def before(self, c):
        for b in range(self.blocks):
            @pl.when(c == self.first[b])
            def _(b=b):
                self.wait(b)

    def drain(self, counts):
        most = jnp.maximum(counts[0], counts[1])
        for b in range(self.blocks):
            @pl.when(most <= self.first[b])
            def _(b=b):
                self.wait(b)


class Table:
    def __init__(self, subnet, items, width):
        segment = lax.axis_index("pipe") // (lax.axis_size("pipe") // 2)
        codes = [[subnet[k, segment * items + i] for k in range(4)] for i in range(items)]
        widths = [width * (4 + k) // 6 for k in range(3)]
        self.w = [width * (4 + c[0]) // 6 for c in codes]
        self.inv = [
            jnp.where(c[0] == 0, 1.0 / widths[0], jnp.where(c[0] == 1, 1.0 / widths[1], 1.0 / widths[2])) for c in codes]
        self.a = [HEAD_DIM * (HEADS * (4 + c[1]) // 6) for c in codes]
        self.u = [w * (6 + c[2]) // 2 for w, c in zip(self.w, codes)]
        self.skip = [c[3] for c in codes]
        self.pairs = [(a + LANES - 1) // LANES for a in self.a]
        self.chunks = [(u + UNIT_CHUNK - 1) // UNIT_CHUNK for u in self.u]


def fetch(src, dst, sem):
    copy = pltpu.make_async_copy(src, dst, sem)
    copy.start()
    return copy


def pick(i, values):
    return values[i] if isinstance(i, int) else jnp.where(i == 0, values[0], values[1])


def rows_of(i, frames):
    if isinstance(i, int):
        return pl.ds(i * frames, frames)
    return pl.ds(pl.multiple_of(i * frames, frames), frames)


def over_both(counts, body):
    n0, n1 = counts
    low, high = jnp.minimum(n0, n1), jnp.maximum(n0, n1)
    longer = (n1 > n0).astype(jnp.int32)

    def both(c, _):
        body((0, 1), c)
        return 0

    def one(c, _):
        body((longer,), c)
        return 0

    lax.fori_loop(0, low, both, 0)
    lax.fori_loop(low, high, one, 0)


def mask_rows(x, items, frames, tab):
    for i in range(items):
        rr = rows_of(i, frames)
        x[rr, :] = jnp.where(lane_mask(x.shape[1], tab.w[i]) > 0, x[rr, :], jnp.zeros((), x.dtype))


def half_mask(h):
    low = lax.broadcasted_iota(jnp.int32, (1, LANES), 1) < HEAD_DIM
    return low if h == 0 else jnp.logical_not(low)


def only(h, x):
    return jnp.where(half_mask(h), x, jnp.zeros_like(x))


def attn_fwd_kernel(layer, items, frames, subnet, vec, x_any, *rest):
    qkv_o, pt_o, ob_o, r1_o, w, x, qkv, pt, ob, r1, wsem, sem, ptsem = rest[2:]
    width = x.shape[1]
    tab = Table(subnet, items, width)
    load = fetch(x_any, x, sem.at[0])
    p = Attn(layer, rest[:2], w, wsem)
    p.start((0, 1, 2, 3))
    cms = [lane_mask(width, n) for n in tab.w]
    hms = [lane_mask(width, n) for n in tab.a]
    load.wait()
    if layer == 0:
        mask_rows(x, items, frames, tab)
    outs = []
    for j in range(3):
        p.wait(j)
        accs = [dot_nn(x[rows_of(i, frames), :], w[j]) for i in range(items)]
        for i, acc in enumerate(accs):
            if j == 0:
                acc = acc + vec[ROW_QB:ROW_QB + 1, :]
            qkv[j, rows_of(i, frames), :] = (acc * hms[i]).astype(BF)
        outs.append(fetch(qkv.at[j], qkv_o.at[j], sem.at[1 + j]))

    def pair(its, c):
        lanes = pl.ds(pl.multiple_of(c * LANES, LANES), LANES)
        vts, ss = [], []
        for i in its:
            rr = rows_of(i, frames)
            q = qkv[0, rr, lanes] * jnp.asarray(HEAD_DIM ** -0.5, BF)
            k = qkv[1, rr, lanes]
            vts.append(qkv[2, rr, lanes].T)
            ss += [dot_nt(only(h, k), q) for h in (0, 1)]
        es = [jnp.exp(s - jnp.max(s, axis=0, keepdims=True)) for s in ss]
        pbs = [(e * (1.0 / jnp.sum(e, axis=0, keepdims=True))).astype(BF) for e in es]
        for n, i in enumerate(its):
            mixed = []
            for h in (0, 1):
                pt[i, 2 * c + h] = pbs[2 * n + h]
                mixed.append(dot_nn(vts[n][h * HEAD_DIM:(h + 1) * HEAD_DIM], pbs[2 * n + h]))
            ob[rows_of(i, frames), lanes] = jnp.concatenate(mixed, axis=0).T.astype(BF)
            fetch(pt.at[i, pl.ds(2 * c, 2)], pt_o.at[i, pl.ds(2 * c, 2)], ptsem.at[i, c])

    over_both(tab.pairs, pair)
    for i in range(items):
        def blank(c, _, i=i):
            ob[rows_of(i, frames), pl.ds(pl.multiple_of(c * LANES, LANES), LANES)] = jnp.zeros((frames, LANES), BF)
            return 0

        lax.fori_loop(tab.pairs[i], width // LANES, blank, 0)
    outs.append(fetch(ob, ob_o, sem.at[4]))
    p.wait(3)
    accs = [dot_nn(ob[rows_of(i, frames), :], w[3]) for i in range(items)]
    for i, acc in enumerate(accs):
        rr = rows_of(i, frames)
        r1[rr, :] = x[rr, :].astype(F32) + (acc + vec[ROW_OB:ROW_OB + 1, :]) * cms[i]
    outs.append(fetch(r1, r1_o, sem.at[5]))
    for i in range(items):
        def drain(c, _, i=i):
            pltpu.make_async_copy(pt.at[i, pl.ds(2 * c, 2)], pt_o.at[i, pl.ds(2 * c, 2)], ptsem.at[i, c]).wait()
            return 0

        lax.fori_loop(0, tab.pairs[i], drain, 0)
    for o in outs:
        o.wait()


def ffn_fwd_kernel(layer, items, frames, last, subnet, vec, ub, r1_any, x_any, *rest):
    n1b_o, g_o, gp_o, r2_o, out_o, w_up, w_down, r1, x, n1b, g, gp, acc, out, wsem, sem, gsem = rest[2:]
    width, units = w_up.shape
    tab = Table(subnet, items, width)
    nblk, nch = units // width, units // UNIT_CHUNK
    loads = [fetch(r1_any, r1, sem.at[0])]
    p = Ffn(layer, rest[:2], w_up, w_down, wsem)
    p.start()
    if last:
        loads.append(fetch(x_any, x, sem.at[1]))
    cms = [lane_mask(width, n) for n in tab.w]
    loads[0].wait()
    for i in range(items):
        rr = rows_of(i, frames)
        xhat, _ = normed(r1[rr, :], cms[i], tab.inv[i])
        n1 = (xhat * vec[ROW_G1:ROW_G1 + 1, :] + vec[ROW_B1:ROW_B1 + 1, :]) * cms[i]
        n1b[rr, :] = n1.astype(BF)
        acc[rr, :] = n1 + vec[ROW_DB:ROW_DB + 1, :] * cms[i]
    outs = [fetch(n1b, n1b_o, sem.at[2])]

    def store_chunk(i, c):
        cols = pl.ds(pl.multiple_of(c * UNIT_CHUNK, UNIT_CHUNK), UNIT_CHUNK)
        rr = rows_of(i, frames)
        return [
            pltpu.make_async_copy(a.at[rr, cols], b.at[rr, cols], gsem.at[k, i, c])
            for k, (a, b) in enumerate(((g, g_o), (gp, gp_o)))
        ]

    def chunk(its, c):
        p.before(c)
        cols = pl.ds(pl.multiple_of(c * UNIT_CHUNK, UNIT_CHUNK), UNIT_CHUNK)
        ids = lax.broadcasted_iota(jnp.int32, (1, UNIT_CHUNK), 1) + c * UNIT_CHUNK
        us = [dot_nn(n1b[rows_of(i, frames), :], w_up[:, cols]) for i in its]
        gbs = []
        for i, u in zip(its, us):
            fm = (ids < pick(i, tab.u)).astype(F32)
            u = (u + ub[0:1, cols]) * fm
            half = 0.5 * (1.0 + lax.erf(u * (0.5 ** 0.5)))
            gb = (u * half).astype(BF)
            g[rows_of(i, frames), cols] = gb
            gp[rows_of(i, frames), cols] = ((half + u * (jnp.exp(u * u * -0.5) * 0.3989422804014327)) * fm).astype(BF)
            gbs.append(gb)
        for i, gb in zip(its, gbs):
            acc[rows_of(i, frames), :] += dot_nn(gb, w_down[cols, :]) * lane_mask(width, pick(i, tab.w))
        for i in its:
            for copy in store_chunk(i, c):
                copy.start()

    over_both(tab.chunks, chunk)
    p.drain(tab.chunks)
    for i in range(items):
        def blank(c, _, i=i):
            cols = pl.ds(pl.multiple_of(c * UNIT_CHUNK, UNIT_CHUNK), UNIT_CHUNK)
            g[rows_of(i, frames), cols] = jnp.zeros((frames, UNIT_CHUNK), BF)
            gp[rows_of(i, frames), cols] = jnp.zeros((frames, UNIT_CHUNK), BF)
            for copy in store_chunk(i, c):
                copy.start()
            return 0

        lax.fori_loop(tab.chunks[i], nch, blank, 0)
    outs.append(fetch(acc, r2_o, sem.at[3]))
    if last:
        loads[1].wait()
    for i in range(items):
        rr = rows_of(i, frames)
        xhat, _ = normed(acc[rr, :], cms[i], tab.inv[i])
        y = ((xhat * vec[ROW_G2:ROW_G2 + 1, :] + vec[ROW_B2:ROW_B2 + 1, :]) * cms[i]).astype(BF)
        if last:
            y = jnp.where(tab.skip[i] == 1, x[rr, :], y)
        out[rr, :] = y
    outs.append(fetch(out, out_o, sem.at[4]))
    for i in range(items):
        for c in range(nch):
            for copy in store_chunk(i, c):
                copy.wait()
    for o in outs:
        o.wait()


class Quarters:
    def __init__(self, stage, out, sems, first):
        self.stage, self.out, self.sems, self.first = stage, out, sems, first

    def copy(self, y, b):
        return pltpu.make_async_copy(self.stage.at[y, b], self.out.at[y, self.first + b], self.sems.at[y, b])

    def start(self, y, b):
        self.copy(y, b).start()

    def wait(self):
        for y in range(self.stage.shape[0]):
            for b in range(self.stage.shape[1]):
                self.copy(y, b).wait()


def ffn_bwd_kernel(layer, items, frames, last, first, subnet, vec, cot_any, dxn_any, r2_any, r1_any, gp_any, g_any, n1b_any,
                   *rest):
    (da_o, dr1_o, sums, grads, w_up, w_down, cot, dxn, r2, r1, gp, g, n1b, du, df, acc, da, stage, wsem, sem,
     gsem, qsem) = rest[(2 if last else 3):]
    width, units = w_up.shape
    tab = Table(subnet, items, width)
    nblk, nch = units // width, units // UNIT_CHUNK
    loads = [fetch(r2_any, r2, sem.at[0]), fetch(cot_any, cot, sem.at[1])]
    if not last:
        loads.append(fetch(dxn_any, dxn, sem.at[2]))
    p = Ffn(layer, rest[:2], w_up, w_down, wsem)
    p.start()

    def load_gp(c):
        cols = pl.ds(pl.multiple_of(c * UNIT_CHUNK, UNIT_CHUNK), UNIT_CHUNK)
        return pltpu.make_async_copy(gp_any.at[:, cols], gp.at[:, cols], gsem.at[c])

    for c in range(nch):
        load_gp(c).start()
    later = [fetch(r1_any, r1, sem.at[3]), fetch(n1b_any, n1b, sem.at[4]), fetch(g_any, g, sem.at[5])]
    sums[...] = jnp.zeros_like(sums)
    for o in loads:
        o.wait()
    for i in range(items):
        rr = rows_of(i, frames)
        cm = lane_mask(width, tab.w[i])
        if last:
            dy = jnp.where(tab.skip[i] == 1, 0.0, cot[rr, :].astype(F32))
        else:
            dy = jnp.where(tab.skip[i] == 1, cot[rr, :], dxn[rr, :]).astype(F32)
        xhat, rstd = normed(r2[rr, :], cm, tab.inv[i])
        dr2, dg, ds = norm_back(dy, xhat, rstd, vec[ROW_G2:ROW_G2 + 1, :], cm, tab.inv[i])
        dfb = dr2.astype(BF)
        df[rr, :] = dfb
        acc[rr, :] = dr2
        sums[ROW_G2:ROW_G2 + 1, 0:width] += dg
        sums[ROW_B2:ROW_B2 + 1, 0:width] += ds
        sums[ROW_DB:ROW_DB + 1, 0:width] += jnp.sum(dfb.astype(F32), axis=0, keepdims=True)

    def chunk(its, c):
        p.before(c)
        load_gp(c).wait()
        cols = pl.ds(pl.multiple_of(c * UNIT_CHUNK, UNIT_CHUNK), UNIT_CHUNK)
        dgs = [dot_nt(df[rows_of(i, frames), :], w_down[cols, :]) for i in its]
        dubs = []
        for i, dg in zip(its, dgs):
            dub = (dg * gp[rows_of(i, frames), cols].astype(F32)).astype(BF)
            du[rows_of(i, frames), cols] = dub
            sums[ROW_UB:ROW_UB + 1, cols] += jnp.sum(dub.astype(F32), axis=0, keepdims=True)
            dubs.append(dub)
        for i, dub in zip(its, dubs):
            acc[rows_of(i, frames), :] += dot_nt(dub, w_up[:, cols])

    over_both(tab.chunks, chunk)
    p.drain(tab.chunks)

    def drain(c, _):
        load_gp(c).wait()
        return 0

    lax.fori_loop(jnp.maximum(tab.chunks[0], tab.chunks[1]), nch, drain, 0)
    for i in range(items):
        def blank(c, _, i=i):
            cols = pl.ds(pl.multiple_of(c * UNIT_CHUNK, UNIT_CHUNK), UNIT_CHUNK)
            du[rows_of(i, frames), cols] = jnp.zeros((frames, UNIT_CHUNK), BF)
            return 0

        lax.fori_loop(tab.chunks[i], nch, blank, 0)
    for o in later:
        o.wait()
    quarters = Quarters(stage, grads, qsem, first)
    rows = stage.shape[3]

    def down_step(f, _):
        y, par = f // 2, f % 2
        for s in range(nblk // 2):
            lanes = pl.ds(pl.multiple_of(f * width + s * 2 * rows, LANES), 2 * rows)
            res = dot_tn(g[:, lanes], df[...]).astype(BF)
            for t in (0, 1):
                stage[y, nblk + 2 * s + t, par] = res[t * rows:(t + 1) * rows]

        @pl.when(par == 1)
        def _():
            for b in range(nblk):
                quarters.start(y, nblk + b)
        return 0

    lax.fori_loop(0, 4, down_step, 0)
    for i in range(items):
        rr = rows_of(i, frames)
        cm = lane_mask(width, tab.w[i])
        xhat, rstd = normed(r1[rr, :], cm, tab.inv[i])
        d1, dg, ds = norm_back(acc[rr, :], xhat, rstd, vec[ROW_G1:ROW_G1 + 1, :], cm, tab.inv[i])
        acc[rr, :] = d1
        dab = d1.astype(BF)
        da[rr, :] = dab
        sums[ROW_G1:ROW_G1 + 1, 0:width] += dg
        sums[ROW_B1:ROW_B1 + 1, 0:width] += ds
        sums[ROW_OB:ROW_OB + 1, 0:width] += jnp.sum(dab.astype(F32), axis=0, keepdims=True)
    outs = [fetch(acc, dr1_o, sem.at[6]), fetch(da, da_o, sem.at[7])]

    def up_step(j, _):
        cols = pl.ds(pl.multiple_of(j * width, LANES), width)
        for y in (0, 1):
            res = dot_tn(n1b[:, y * 2 * rows:(y + 1) * 2 * rows], du[:, cols]).astype(BF)
            for t in (0, 1):
                stage[y, j, t] = res[t * rows:(t + 1) * rows]
            quarters.start(y, j)
        return 0

    lax.fori_loop(0, nblk, up_step, 0)
    quarters.wait()
    for o in outs:
        o.wait()


def attn_bwd_kernel(layer, items, frames, first, subnet, da_any, dr1_any, qkv_any, pt_any, x_any, ob_any, *rest):
    dx_o, sums, grads, w, da, dr1, qkv, pt, x, ob, do, dqkv, dx, stage, wsem, sem, ptsem, qsem = rest[3:]
    width = da.shape[1]
    tab = Table(subnet, items, width)
    loads = [fetch(da_any, da, sem.at[0])]
    p = Attn(layer, rest[:2], w, wsem)
    p.start((3, 0, 1, 2))
    loads.append(fetch(qkv_any, qkv, sem.at[1]))

    def load_pt(i, c):
        return pltpu.make_async_copy(pt_any.at[i, pl.ds(2 * c, 2)], pt.at[i, pl.ds(2 * c, 2)], ptsem.at[i, c])

    npair = width // LANES

    def begin(c, _):
        for i in range(items):
            @pl.when(c < tab.pairs[i])
            def _(i=i):
                load_pt(i, c).start()
        return 0

    lax.fori_loop(0, npair, begin, 0)
    later = [fetch(ob_any, ob, sem.at[2]), fetch(dr1_any, dr1, sem.at[3]), fetch(x_any, x, sem.at[4])]
    sums[...] = jnp.zeros_like(sums)
    loads[0].wait()
    p.wait(3)
    dos = [dot_nt(da[rows_of(i, frames), :], w[3]) for i in range(items)]
    for i, d in enumerate(dos):
        do[rows_of(i, frames), :] = d.astype(BF)
    loads[1].wait()
    scale = HEAD_DIM ** -0.5

    def pair(its, c):
        lanes = pl.ds(pl.multiple_of(c * LANES, LANES), LANES)
        ids = lax.broadcasted_iota(jnp.int32, (1, LANES), 1) + c * LANES
        for i in its:
            load_pt(i, c).wait()
        rr = [rows_of(i, frames) for i in its]
        q = [qkv[0, r, lanes] for r in rr]
        k = [qkv[1, r, lanes] for r in rr]
        v = [qkv[2, r, lanes] for r in rr]
        dob = [do[r, lanes] for r in rr]
        kt = [a.T for a in k]
        heads = [(n, h) for n in range(len(its)) for h in (0, 1)]
        pbs = [pt[its[n], 2 * c + h] for n, h in heads]
        dps = [dot_nt(only(h, v[n]), dob[n]) for n, h in heads]
        dvs = [dot_nn(pb, dob[n]) for pb, (n, h) in zip(pbs, heads)]
        tmps = [pb.astype(F32) * dp for pb, dp in zip(pbs, dps)]
        dss = [(t - pb.astype(F32) * jnp.sum(t, axis=0, keepdims=True)).astype(BF) for t, pb in zip(tmps, pbs)]
        dks = [dot_nn(ds, q[n]) for ds, (n, h) in zip(dss, heads)]
        dqs = [dot_nn(kt[n][h * HEAD_DIM:(h + 1) * HEAD_DIM], ds) for ds, (n, h) in zip(dss, heads)]
        for n, i in enumerate(its):
            hm = (ids < pick(i, tab.a)).astype(F32)
            dq = (jnp.concatenate(dqs[2 * n:2 * n + 2], axis=0).T * (hm * scale)).astype(BF)
            dqkv[0, rr[n], lanes] = dq
            dqkv[1, rr[n], lanes] = (jnp.where(half_mask(0), dks[2 * n], dks[2 * n + 1]) * (hm * scale)).astype(BF)
            dqkv[2, rr[n], lanes] = (jnp.where(half_mask(0), dvs[2 * n], dvs[2 * n + 1]) * hm).astype(BF)
            sums[ROW_QB:ROW_QB + 1, lanes] += jnp.sum(dq.astype(F32), axis=0, keepdims=True)

    over_both(tab.pairs, pair)
    for i in range(items):
        def blank(c, _, i=i):
            lanes = pl.ds(pl.multiple_of(c * LANES, LANES), LANES)
            for j in range(3):
                dqkv[j, rows_of(i, frames), lanes] = jnp.zeros((frames, LANES), BF)
            return 0

        lax.fori_loop(tab.pairs[i], npair, blank, 0)
    for o in later:
        o.wait()
    if layer == 0:
        mask_rows(x, items, frames, tab)
    quarters = Quarters(stage, grads, qsem, first)
    rows = stage.shape[3]

    def step(lhs, rhs, b):
        for y in (0, 1):
            res = dot_tn(lhs[:, y * 2 * rows:(y + 1) * 2 * rows], rhs).astype(BF)
            for t in (0, 1):
                stage[y, b, t] = res[t * rows:(t + 1) * rows]
            quarters.start(y, b)

    def in_step(j, _):
        step(x, dqkv[j], j)
        return 0

    lax.fori_loop(0, 3, in_step, 0)
    step(ob, da[...], 3)
    for j in range(3):
        p.wait(j)

    def back_step(j, _):
        adds = [dot_nt(dqkv[j, rows_of(i, frames), :], w[j]) for i in range(items)]
        for i, add in enumerate(adds):
            dr1[rows_of(i, frames), :] += add
        return 0

    lax.fori_loop(0, 3, back_step, 0)
    for i in range(items):
        rr = rows_of(i, frames)
        dx[rr, :] = (dr1[rr, :] * lane_mask(width, tab.w[i])).astype(BF)
    out = fetch(dx, dx_o, sem.at[5])
    quarters.wait()
    out.wait()


ANY = pl.BlockSpec(memory_space=pl.ANY)
VM = pl.BlockSpec(memory_space=pltpu.VMEM)
SM = pl.BlockSpec(memory_space=pltpu.SMEM)
PARAMS = dict(vmem_limit_bytes=58 * 2 ** 20)


def cost(flops, nbytes):
    return pl.CostEstimate(flops=int(flops), bytes_accessed=int(nbytes), transcendentals=0)


def sds(shape, dtype):
    return jax.ShapeDtypeStruct(shape, dtype)


def run(kernel, name, subnet, vmem, hbm, outs, vmem_outs, scratch, sems, flops, nbytes, alias=None):
    return pl.pallas_call(
        kernel,
        out_shape=tuple(outs),
        in_specs=[SM] + [VM] * len(vmem) + [ANY] * len(hbm),
        out_specs=tuple(VM if k in vmem_outs else ANY for k in range(len(outs))),
        scratch_shapes=[pltpu.VMEM(s, d) for s, d in scratch] + [pltpu.SemaphoreType.DMA(s) for s in sems],
        input_output_aliases={} if alias is None else {len(vmem) + len(hbm): alias},
        compiler_params=pltpu.CompilerParams(**PARAMS),
        cost_estimate=cost(flops, nbytes),
        name=name,
    )(subnet, *vmem, *hbm)


def attn_fwd(layer, subnet, x, vec, weights, items):
    n, d = x.shape
    t = n // items
    return run(
        functools.partial(attn_fwd_kernel, layer, items, t), "attn_fwd", subnet, (vec,), (x, *weights),
        [sds((3, n, d), BF), sds((items, HEADS, t, t), BF), sds((n, d), BF), sds((n, d), F32)], (),
        [((4, d, d), BF), ((n, d), BF), ((3, n, d), BF), ((items, HEADS, t, t), BF), ((n, d), BF), ((n, d), F32)],
        [(4,), (6,), (items, d // LANES)],
        8 * n * d * d + 16 * t * n * d, 8 * d * d + n * d * 24)


def ffn_fwd(layer, last, subnet, r1, x, vec, ub, weights, ff, items):
    n, d = x.shape
    return run(
        functools.partial(ffn_fwd_kernel, layer, items, n // items, last), "ffn_fwd", subnet, (vec, ub),
        (r1, x, *weights),
        [sds((n, d), BF), sds((n, ff), BF), sds((n, ff), BF), sds((n, d), F32), sds((n, d), BF)], (),
        [((d, ff), BF), ((ff, d), BF), ((n, d), F32), ((n, d), BF), ((n, d), BF), ((n, ff), BF), ((n, ff), BF),
         ((n, d), F32), ((n, d), BF)],
        [(ff // d, 2), (5,), (2, items, ff // UNIT_CHUNK)],
        6 * n * d * ff, 4 * d * ff + n * d * 30)


def ffn_bwd(layer, last, first, blocks, subnet, cot, dxn, r2, r1, gp, g, n1b, vec, weights, grads, items):
    n, d = cot.shape
    ff = gp.shape[1]
    q, nb = d // 4, ff // d
    more = () if grads is None else (grads,)
    return run(
        functools.partial(ffn_bwd_kernel, layer, items, n // items, last, first), "ffn_bwd", subnet, (vec,),
        (cot, dxn, r2, r1, gp, g, n1b, *weights, *more),
        [sds((n, d), BF), sds((n, d), F32), sds((8, ff), F32), sds((2, blocks, 2, q, d), BF)], (2,),
        [((d, ff), BF), ((ff, d), BF), ((n, d), BF), ((n, d), BF), ((n, d), F32), ((n, d), F32), ((n, ff), BF),
         ((n, ff), BF), ((n, d), BF), ((n, ff), BF), ((n, d), BF), ((n, d), F32), ((n, d), BF),
         ((2, 2 * nb, 2, q, d), BF)],
        [(nb, 2), (8,), (ff // UNIT_CHUNK,), (2, 2 * nb)],
        10 * n * d * ff, 8 * d * ff + n * d * 40, None if grads is None else 3)


def attn_bwd(layer, first, subnet, da, dr1, qkv, pt, x, ob, weights, grads, items):
    n, d = da.shape
    t = n // items
    q = d // 4
    return run(
        functools.partial(attn_bwd_kernel, layer, items, t, first), "attn_bwd", subnet, (),
        (da, dr1, qkv, pt, x, ob, *weights, grads),
        [sds((n, d), BF), sds((8, d), F32), sds(grads.shape, BF)], (1,),
        [((4, d, d), BF), ((n, d), BF), ((n, d), F32), ((3, n, d), BF), ((items, HEADS, t, t), BF), ((n, d), BF),
         ((n, d), BF), ((n, d), BF), ((3, n, d), BF), ((n, d), BF), ((2, 4, 2, q, d), BF)],
        [(4,), (6,), (items, d // LANES), (2, 4)],
        16 * n * d * d + 32 * t * n * d, 16 * d * d + n * d * 30, 2)


MESH = pl.DeviceIdType.MESH


def flip(axis, bit):
    return {axis: jnp.bitwise_xor(lax.axis_index(axis), 1 << bit)}


def greet(partners):
    barrier = pltpu.get_barrier_semaphore()
    for who in partners:
        pl.semaphore_signal(barrier, inc=1, device_id=who, device_id_type=MESH)
    pl.semaphore_wait(barrier, len(partners))


def gather_kernel(layers, w_in, w_out, w_up, w_down, *rest):
    smalls, full, vec, ub = rest[:8], rest[8:12], rest[12], rest[13]
    every, own, send_sem, recv_sem, local_sem = rest[14], rest[15:19], rest[19], rest[20], rest[21]
    shards = (w_in, w_out, w_up, w_down)
    f = lax.axis_index("fsdp")
    pipe = lax.axis_index("pipe")
    part = 2 * (pipe % 2) + (pipe // 2) % 2
    core, far, xnb, znb = flip("fsdp", 0), flip("fsdp", 1), flip("pipe", 0), flip("pipe", 1)
    rows, width = w_out.shape[1:]
    piece = rows // 4
    half = rows // 2
    count = [0]

    def at(ref, k, layer, row, nrows, col, ncols, quarter):
        base = 0 if quarter is None else pl.multiple_of(quarter * shards[k].shape[1], 8)
        return ref.at[layer, pl.ds(pl.multiple_of(base + row, 8), nrows), pl.ds(col, ncols)]

    def regions(chunk, ab, k):
        kind = chunk[1]
        if kind == 0:
            if ab == 0:
                return [(0, piece * k, piece, 0, 2 * width)]
            return [(0, piece * k, piece, 2 * width, width), (1, piece * k, piece, 0, width)]
        row = (kind - 1) * half
        if ab == 0:
            return [(2, row, half, pl.multiple_of(k * width, LANES), width)]
        return [(3, k * rows + row, half, 0, width)]

    def remote(src, dst, who):
        n = count[0]
        count[0] += 1
        return pltpu.make_async_remote_copy(
            src_ref=src, dst_ref=dst, send_sem=send_sem.at[n], recv_sem=recv_sem.at[n], device_id=who, device_id_type=MESH)

    def move(chunk, ab, k, quarter, who, own=False):
        out = []
        for w, row, nr, col, nc in regions(chunk, ab, k):
            src = at(shards[w], w, chunk[0], row, nr, col, nc, None) if own else at(full[w], w, chunk[0], row, nr, col, nc, quarter)
            out.append(remote(src, at(full[w], w, chunk[0], row, nr, col, nc, quarter), who))
        return out

    def place(ref, w, l):
        n = shards[w].shape[1]
        return ref.at[l, pl.ds(pl.multiple_of(f * n, 8), n)]

    order = [(w, l) for l in range(layers) for w in range(4)]
    loads = [pltpu.make_async_copy(shards[w].at[l], own[w].at[l], local_sem.at[0, w, l]) for w, l in order]
    stores = [pltpu.make_async_copy(own[w].at[l], place(full[w], w, l), local_sem.at[1, w, l]) for w, l in order]
    every[f] = jnp.zeros(every.shape[1:], F32)
    for k, ref in enumerate(smalls):
        for l in range(layers):
            every[f, l, k:k + 1, 0:ref.shape[1]] = ref[l:l + 1, :].astype(F32)
    greet((core, far, xnb, znb))
    chunks = [(l, kind) for l in range(layers) for kind in range(3)]
    started, arrived = [], []

    def start(copies):
        for c in copies:
            c.start()
        started.extend(copies)
        return copies

    def landed(copies):
        for c in copies:
            c.wait_recv()
        arrived.extend(copies)

    q2 = jnp.bitwise_xor(f, 2)
    small_far = start([remote(every.at[f], every.at[f], far)])
    small_core = start([remote(every.at[f], every.at[f], core)])
    y_copies, s2, s3 = {}, {}, {}
    tail = []

    def own_core(l):
        for w in range(4):
            tail.extend(start([remote(shards[w].at[l], place(full[w], w, l), core)]))

    k1, k2, k3 = (jnp.bitwise_xor(part, m) for m in (1, 2, 3))
    n_ch = len(chunks)
    direct = {n: (None, 1, 0)[n % 3] for n in range(n_ch)}
    for t in range(n_ch + 3):
        if t < n_ch:
            y_copies[t] = [start(move(chunks[t], ab, part, f, far, own=True)) for ab in (0, 1)]
            if direct[t] is not None:
                y_copies[t].append(start(move(chunks[t], direct[t], k3, f, far, own=True)))
        if t == 0:
            landed(small_far)
            small_core2 = start([remote(every.at[q2], every.at[q2], core)])
            for c in loads:
                c.start()
        if t < layers:
            own_core(t)
        if t == 1:
            for c, d in zip(loads, stores):
                c.wait()
                d.start()
        n = t - 1
        if 0 <= n < n_ch:
            ch = chunks[n]
            for ab in (0, 1):
                landed(y_copies[n][ab])
            s2[n] = {}
            for ab in (0, 1):
                s2[n]["x", ab] = start(move(ch, ab, part, q2, xnb))
                s2[n]["z", ab] = start(move(ch, ab, part, q2, znb))
            for ab in (0, 1):
                tail.extend(start(move(ch, ab, part, q2, core)))
        n = t - 2
        if 0 <= n < n_ch:
            ch = chunks[n]
            landed(s2[n]["x", 0])
            landed(s2[n]["z", 1])
            s3[n] = {}
            if direct[n] != 0:
                s3[n][0] = start(move(ch, 0, k2, q2, znb))
            if direct[n] != 1:
                s3[n][1] = start(move(ch, 1, k1, q2, xnb))
            if direct[n] is not None:
                landed(y_copies[n][2])
                tail.extend(start(move(ch, direct[n], k3, q2, core)))
            tail.extend(start(move(ch, 0, k2, q2, core)))
            tail.extend(start(move(ch, 1, k1, q2, core)))
        n = t - 3
        if 0 <= n < n_ch:
            ch = chunks[n]
            landed(s2[n]["x", 1])
            landed(s2[n]["z", 0])
            tail.extend(start(move(ch, 1, k2, q2, core)))
            tail.extend(start(move(ch, 0, k1, q2, core)))
            for ab, copies in s3[n].items():
                landed(copies)
                tail.extend(start(move(ch, ab, k3, q2, core)))
    landed(small_core)
    landed(small_core2)
    for q in range(4):
        for l in range(layers):
            vec[l, 0:7, q * rows:(q + 1) * rows] = every[q, l, 0:7, 0:rows]
            ub[l, :, q * width:(q + 1) * width] = every[q, l, 7:8, :]
    landed(tail)
    for c in started:
        c.wait_send()
    for c in stores:
        c.wait()


def gather(w_in, w_out, w_up, w_down, smalls):
    layers = w_in.shape[0]
    weights = (w_in, w_out, w_up, w_down)
    width = w_out.shape[2]
    n = 160
    dma = pltpu.SemaphoreType.DMA
    return pl.pallas_call(
        functools.partial(gather_kernel, layers),
        out_shape=tuple(sds((layers, 4 * w.shape[1], w.shape[2]), BF) for w in weights)
        + (sds((layers, 8, width), F32), sds((layers, 1, 4 * width), F32)),
        in_specs=[ANY] * 4 + [VM] * 8,
        out_specs=(ANY,) * 4 + (VM, VM),
        scratch_shapes=[pltpu.VMEM((4, layers, 8, width), F32)] + [pltpu.VMEM(w.shape, BF) for w in weights]
        + [dma((n,)), dma((n,)), dma((2, 4, layers))],
        compiler_params=pltpu.CompilerParams(collective_id=0, has_side_effects=True),
        name="gather",
    )(*weights, *smalls)


def reduce_kernel(first, count, bits, layers, g, *rest):
    parts, (out, small_out, loc, rc, ry, rx, rz, fin, srecv, ss, rs, ls, os_, s_send, s_recv) = rest[:2 * layers], rest[2 * layers:]
    f = lax.axis_index("fsdp")
    pipe = lax.axis_index("pipe")
    c, y, x, z = f % 2, f // 2, pipe % 2, (pipe // 2) % 2
    rows = g.shape[3]
    half, quarter = rows // 2, rows // 4
    who = [flip("fsdp", 0), flip("fsdp", 1)] + [flip("pipe", b) for b in range(bits)]
    mine_half = pl.ds(pl.multiple_of(x * half, 16), half)
    their_half = pl.ds(pl.multiple_of((1 - x) * half, 16), half)
    mine = pl.ds(pl.multiple_of(x * half + z * quarter, 16), quarter)
    theirs = pl.ds(pl.multiple_of(x * half + (1 - z) * quarter, 16), quarter)

    def remote(k, p, src, dst, partner):
        return pltpu.make_async_remote_copy(
            src_ref=src, dst_ref=dst, send_sem=ss.at[k, p], recv_sem=rs.at[k, p], device_id=who[partner], device_id_type=MESH)

    def load(p):
        return pltpu.make_async_copy(g.at[:, first + p, c], loc.at[p], ls.at[p])

    def store(p):
        return pltpu.make_async_copy(fin.at[p], out.at[p], os_.at[p])

    moves = [
        lambda p: remote(0, p, g.at[:, first + p, 1 - c], rc.at[p], 0),
        lambda p: remote(1, p, loc.at[p, 1 - y], ry.at[p], 1),
        lambda p: remote(2, p, loc.at[p, y, their_half], rx.at[p], 2),
        lambda p: remote(3, p, loc.at[p, y, theirs], rz.at[0, p], 3),
    ]
    for b in range(2, bits):
        moves.append(lambda p, b=b: remote(2 + b, p, fin.at[p, mine], rz.at[b - 1, p], 2 + b))
    n_red = len(moves)
    moves.append(lambda p: remote(n_red, p, fin.at[p, mine], fin.at[p, mine], 3))
    moves.append(lambda p: remote(n_red + 1, p, fin.at[p, mine_half], fin.at[p, mine_half], 2))

    def add(a, b):
        return (a.astype(F32) + b.astype(F32)).astype(BF)

    def arrive(k, p):
        moves[k](p).wait()
        if k == 0:
            load(p).wait()
            loc[p] = add(loc[p], rc[p])
        elif k == 1:
            loc[p, y] = add(loc[p, y], ry[p])
        elif k == 2:
            loc[p, y, mine_half] = add(loc[p, y, mine_half], rx[p])
        elif k == 3:
            fin[p, mine] = add(loc[p, y, mine], rz[0, p])
        elif k < n_red:
            fin[p, mine] = add(fin[p, mine], rz[k - 3, p])

    greet(who)
    for l in range(layers):
        attn_sums, ffn_sums = parts[2 * l], parts[2 * l + 1]
        small_out[l] = ffn_sums[...]
        small_out[l, 0:1, 0:attn_sums.shape[1]] = attn_sums[0:1, :]
    n_small = len(who)

    def small_move(k):
        return pltpu.make_async_remote_copy(
            src_ref=small_out, dst_ref=srecv.at[k], send_sem=s_send.at[k], recv_sem=s_recv.at[k], device_id=who[k],
            device_id_type=MESH)

    moves[0](0).start()
    load(0).start()
    total = len(moves)

    def tick(t, _):
        @pl.when(t + 1 < count)
        def _():
            moves[0](t + 1).start()
            load(t + 1).start()

        for k in range(total):
            p = t - k

            @pl.when(jnp.logical_and(p >= 0, p < count))
            def _(k=k, p=p):
                arrive(k, p)
                if k + 1 < total:
                    moves[k + 1](p).start()
                else:
                    store(p).start()

        for k in range(n_small + 1):
            @pl.when(t == k)
            def _(k=k):
                if k > 0:
                    small_move(k - 1).wait()
                    small_out[...] = small_out[...] + srecv[k - 1]
                if k < n_small:
                    small_move(k).start()
        return 0

    lax.fori_loop(0, count + total - 1, tick, 0)

    def drain(p, _):
        store(p).wait()
        return 0

    lax.fori_loop(0, count, drain, 0)


def reduce_blocks(g, smalls, first, count, cid):
    bits = 0
    while (1 << bits) < lax.axis_size("pipe"):
        bits += 1
    rows, d = g.shape[3:]
    small = (len(smalls) // 2,) + smalls[1].shape
    n_moves = 2 + bits + 2
    vm = pltpu.VMEM
    dma = pltpu.SemaphoreType.DMA
    return pl.pallas_call(
        functools.partial(reduce_kernel, first, count, bits, len(smalls) // 2),
        out_shape=(sds((count, rows, d), BF), sds(small, F32)),
        in_specs=[ANY] + [VM] * len(smalls),
        out_specs=(ANY, VM),
        scratch_shapes=[
            vm((count, 2, rows, d), BF), vm((count, 2, rows, d), BF), vm((count, rows, d), BF),
            vm((count, rows // 2, d), BF), vm((bits - 1, count, rows // 4, d), BF), vm((count, rows, d), BF),
            vm((2 + bits,) + small, F32),
            dma((n_moves, count)), dma((n_moves, count)), dma((count,)), dma((count,)), dma((2 + bits,)), dma((2 + bits,)),
        ],
        compiler_params=pltpu.CompilerParams(collective_id=cid, has_side_effects=True, vmem_limit_bytes=60 * 2 ** 20),
        name="reduce",
    )(g, *smalls)


def finish_kernel(layers, red, total, g_in, g_out, g_up, g_down, *rest):
    vecs, (bf, f32, sem_in, sem_out) = rest[:8], rest[8:]
    f = lax.axis_index("fsdp")
    blocks = bf.shape[0]
    rows, d = bf.shape[1:]
    per = blocks // layers
    nb = (per - 4) // 2

    def target(l, k):
        if k < nb:
            return g_up.at[l, :, pl.ds(k * d, d)]
        if k < 2 * nb:
            return g_down.at[l, pl.ds((k - nb) * rows, rows)]
        if k < 2 * nb + 3:
            return g_in.at[l, :, pl.ds((k - 2 * nb) * d, d)]
        return g_out.at[l]

    loads = [pltpu.make_async_copy(red.at[p], bf.at[p], sem_in.at[p]) for p in range(blocks)]
    stores = [pltpu.make_async_copy(f32.at[p], target(p // per, p % per), sem_out.at[p]) for p in range(blocks)]
    for c in loads:
        c.start()
    for q in range(4):
        @pl.when(f == q)
        def _(q=q):
            for l in range(layers):
                for k in range(7):
                    vecs[k][l:l + 1, :] = total[l, k:k + 1, q * rows:(q + 1) * rows]
                vecs[7][l:l + 1, :] = total[l, 7:8, q * d:(q + 1) * d]
    for p in range(blocks):
        loads[p].wait()
        f32[p] = bf[p].astype(F32)
        stores[p].start()
    for c in stores:
        c.wait()


def finish(red, total):
    blocks, rows, d = red.shape
    layers = total.shape[0]
    nb = (blocks // layers - 4) // 2
    return pl.pallas_call(
        functools.partial(finish_kernel, layers),
        out_shape=(sds((layers, rows, 3 * d), F32), sds((layers, rows, d), F32), sds((layers, rows, nb * d), F32),
                   sds((layers, nb * rows, d), F32)) + (sds((layers, rows), F32),) * 7 + (sds((layers, d), F32),),
        in_specs=[ANY, VM],
        out_specs=(ANY,) * 4 + (VM,) * 8,
        scratch_shapes=[pltpu.VMEM(red.shape, BF), pltpu.VMEM(red.shape, F32), pltpu.SemaphoreType.DMA((blocks,)),
                        pltpu.SemaphoreType.DMA((blocks,))],
        compiler_params=pltpu.CompilerParams(**PARAMS),
        name="finish",
    )(red, total)


def local(
    frames_in, attn_in, q_bias, attn_out, out_bias, norm1_gain, norm1_bias, ffn_up, up_bias, ffn_down, down_bias,
    norm2_gain, norm2_bias, subnet, out_cotangent,
):
    items, frames, width = frames_in.shape
    ff = ffn_up.shape[2]
    layers = attn_in.shape[0]
    nb = ff // width
    *weights, vec, ub = gather(
        attn_in, attn_out, ffn_up, ffn_down,
        (q_bias, out_bias, norm1_gain, norm1_bias, down_bias, norm2_gain, norm2_bias, up_bias))
    w_att, w_ffn = weights[:2], weights[2:]

    n = items * frames
    cur = frames_in.reshape(n, width)
    kept = []
    for l in range(layers):
        qkv, pt, ob, r1 = attn_fwd(l, subnet, cur, vec[l], w_att, items)
        n1b, g, gp, r2, out = ffn_fwd(l, l == layers - 1, subnet, r1, cur, vec[l], ub[l], w_ffn, ff, items)
        kept.append((cur, qkv, pt, ob, r1, n1b, g, gp, r2))
        cur = out
    layer_out = cur.reshape(frames_in.shape)

    blocks = 2 * nb + 4
    grads = None
    sums = [None] * layers
    cot = out_cotangent.reshape(n, width)
    dx = cot
    for l in reversed(range(layers)):
        x, qkv, pt, ob, r1, n1b, g, gp, r2 = kept[l]
        da, dr1, s1, grads = ffn_bwd(
            l, l == layers - 1, l * blocks, layers * blocks, subnet, cot, dx, r2, r1, gp, g, n1b, vec[l], w_ffn, grads, items)
        dx, s2, grads = attn_bwd(l, l * blocks + 2 * nb, subnet, da, dr1, qkv, pt, x, ob, w_att, grads, items)
        sums[l] = (s2, s1)
    dx = dx.reshape(frames_in.shape)

    red, total = reduce_blocks(grads, [a for pair in sums for a in pair], 0, layers * blocks, 1)
    g_in, g_out, g_up, g_down, g_qb, g_ob, g_g1, g_b1, g_db, g_g2, g_b2, g_ub = finish(red, total)
    return (layer_out, dx, g_in, g_qb, g_out, g_ob, g_g1, g_b1, g_up, g_ub, g_down, g_db, g_g2, g_b2)


def solution(mesh):
    rows3 = P(None, "fsdp", None)
    rows2 = P(None, "fsdp")
    item = P(("pipe", "fsdp"), None, None)
    weights = (rows3, rows2, rows3, rows2, rows2, rows2, rows3, rows2, rows3, rows2, rows2, rows2)
    return jax.shard_map(
        local, mesh=mesh, in_specs=(item,) + weights + (P(), item), out_specs=(item, item) + weights, check_vma=False,
    )
```

```python
import functools

import jax
import jax.numpy as jnp
from jax import lax
from jax.experimental import pallas as pl
from jax.experimental.pallas import tpu as pltpu
from jax.sharding import PartitionSpec as P

HEADS = 12
HEAD_DIM = 64
EPSILON = 1e-05
LANES = 128
UNIT_CHUNK = 512
BF = jnp.bfloat16
F32 = jnp.float32

ROW_QB, ROW_OB, ROW_G1, ROW_B1, ROW_DB, ROW_G2, ROW_B2, ROW_UB = 0, 1, 2, 3, 4, 5, 6, 7

def dot_nn(a, b):
    return lax.dot_general(a, b, (((1,), (0,)), ((), ())), preferred_element_type=F32)


def dot_nt(a, b):
    return lax.dot_general(a, b, (((1,), (1,)), ((), ())), preferred_element_type=F32)


def dot_tn(a, b):
    return lax.dot_general(a, b, (((0,), (0,)), ((), ())), preferred_element_type=F32)


def lane_mask(width, count):
    return (lax.broadcasted_iota(jnp.int32, (1, width), 1) < count).astype(F32)


def normed(rows, cm, inv_w):
    mean = jnp.sum(rows * cm, axis=-1, keepdims=True) * inv_w
    centered = (rows - mean) * cm
    var = jnp.sum(centered * centered, axis=-1, keepdims=True) * inv_w
    rstd = lax.rsqrt(var + EPSILON)
    return centered * rstd, rstd


def norm_back(dy, xhat, rstd, gain, cm, inv_w):
    dym = dy * cm
    dg = jnp.sum(dym * xhat, axis=0, keepdims=True)
    ds = jnp.sum(dym, axis=0, keepdims=True)
    dx = dym * gain
    m1 = jnp.sum(dx, axis=-1, keepdims=True) * inv_w
    m2 = jnp.sum(dx * xhat, axis=-1, keepdims=True) * inv_w
    return cm * (rstd * (dx - m1 - xhat * m2)), dg, ds


class Attn:
    def __init__(self, layer, refs, w, sems):
        w_in, w_out = refs
        d = w.shape[1]
        self.copies = [
            pltpu.make_async_copy(w_in.at[layer, :, pl.ds(b * d, d)], w.at[b], sems.at[b]) for b in range(3)
        ] + [pltpu.make_async_copy(w_out.at[layer], w.at[3], sems.at[3])]

    def start(self, order):
        for b in order:
            self.copies[b].start()

    def wait(self, b):
        self.copies[b].wait()


class Ffn:
    def __init__(self, layer, refs, w_up, w_down, sems):
        up, down = refs
        d = w_up.shape[0]
        self.blocks = w_up.shape[1] // d
        self.first = [b * d // UNIT_CHUNK for b in range(self.blocks)]
        self.copies = [(
            pltpu.make_async_copy(up.at[layer, :, pl.ds(b * d, d)], w_up.at[:, pl.ds(b * d, d)], sems.at[b, 0]),
            pltpu.make_async_copy(down.at[layer, pl.ds(b * d, d)], w_down.at[pl.ds(b * d, d)], sems.at[b, 1]),
        ) for b in range(self.blocks)]

    def start(self):
        for pair in self.copies:
            for copy in pair:
                copy.start()

    def wait(self, b):
        for copy in self.copies[b]:
            copy.wait()

    def before(self, c):
        for b in range(self.blocks):
            @pl.when(c == self.first[b])
            def _(b=b):
                self.wait(b)

    def drain(self, counts):
        most = jnp.maximum(counts[0], counts[1])
        for b in range(self.blocks):
            @pl.when(most <= self.first[b])
            def _(b=b):
                self.wait(b)


class Table:
    def __init__(self, subnet, items, width):
        segment = lax.axis_index("pipe") // (lax.axis_size("pipe") // 2)
        codes = [[subnet[k, segment * items + i] for k in range(4)] for i in range(items)]
        widths = [width * (4 + k) // 6 for k in range(3)]
        self.w = [width * (4 + c[0]) // 6 for c in codes]
        self.inv = [
            jnp.where(c[0] == 0, 1.0 / widths[0], jnp.where(c[0] == 1, 1.0 / widths[1], 1.0 / widths[2])) for c in codes]
        self.a = [HEAD_DIM * (HEADS * (4 + c[1]) // 6) for c in codes]
        self.u = [w * (6 + c[2]) // 2 for w, c in zip(self.w, codes)]
        self.skip = [c[3] for c in codes]
        self.pairs = [(a + LANES - 1) // LANES for a in self.a]
        self.chunks = [(u + UNIT_CHUNK - 1) // UNIT_CHUNK for u in self.u]


def fetch(src, dst, sem):
    copy = pltpu.make_async_copy(src, dst, sem)
    copy.start()
    return copy


def pick(i, values):
    return values[i] if isinstance(i, int) else jnp.where(i == 0, values[0], values[1])


def rows_of(i, frames):
    if isinstance(i, int):
        return pl.ds(i * frames, frames)
    return pl.ds(pl.multiple_of(i * frames, frames), frames)


def over_both(counts, body):
    n0, n1 = counts
    low, high = jnp.minimum(n0, n1), jnp.maximum(n0, n1)
    longer = (n1 > n0).astype(jnp.int32)

    def both(c, _):
        body((0, 1), c)
        return 0

    def one(c, _):
        body((longer,), c)
        return 0

    lax.fori_loop(0, low, both, 0)
    lax.fori_loop(low, high, one, 0)


def mask_rows(x, items, frames, tab):
    for i in range(items):
        rr = rows_of(i, frames)
        x[rr, :] = jnp.where(lane_mask(x.shape[1], tab.w[i]) > 0, x[rr, :], jnp.zeros((), x.dtype))


def half_mask(h):
    low = lax.broadcasted_iota(jnp.int32, (1, LANES), 1) < HEAD_DIM
    return low if h == 0 else jnp.logical_not(low)


def only(h, x):
    return jnp.where(half_mask(h), x, jnp.zeros_like(x))


def attn_fwd_kernel(layer, items, frames, subnet, vec, x_any, *rest):
    qkv_o, pt_o, ob_o, r1_o, w, x, qkv, pt, ob, r1, wsem, sem, ptsem = rest[2:]
    width = x.shape[1]
    tab = Table(subnet, items, width)
    load = fetch(x_any, x, sem.at[0])
    p = Attn(layer, rest[:2], w, wsem)
    p.start((0, 1, 2, 3))
    cms = [lane_mask(width, n) for n in tab.w]
    hms = [lane_mask(width, n) for n in tab.a]
    load.wait()
    if layer == 0:
        mask_rows(x, items, frames, tab)
    outs = []
    for j in range(3):
        p.wait(j)
        accs = [dot_nn(x[rows_of(i, frames), :], w[j]) for i in range(items)]
        for i, acc in enumerate(accs):
            if j == 0:
                acc = acc + vec[ROW_QB:ROW_QB + 1, :]
            qkv[j, rows_of(i, frames), :] = (acc * hms[i]).astype(BF)
        outs.append(fetch(qkv.at[j], qkv_o.at[j], sem.at[1 + j]))

    def pair(its, c):
        lanes = pl.ds(pl.multiple_of(c * LANES, LANES), LANES)
        vts, ss = [], []
        for i in its:
            rr = rows_of(i, frames)
            q = qkv[0, rr, lanes] * jnp.asarray(HEAD_DIM ** -0.5, BF)
            k = qkv[1, rr, lanes]
            vts.append(qkv[2, rr, lanes].T)
            ss += [dot_nt(only(h, k), q) for h in (0, 1)]
        es = [jnp.exp(s - jnp.max(s, axis=0, keepdims=True)) for s in ss]
        pbs = [(e * (1.0 / jnp.sum(e, axis=0, keepdims=True))).astype(BF) for e in es]
        for n, i in enumerate(its):
            mixed = []
            for h in (0, 1):
                pt[i, 2 * c + h] = pbs[2 * n + h]
                mixed.append(dot_nn(vts[n][h * HEAD_DIM:(h + 1) * HEAD_DIM], pbs[2 * n + h]))
            ob[rows_of(i, frames), lanes] = jnp.concatenate(mixed, axis=0).T.astype(BF)
            fetch(pt.at[i, pl.ds(2 * c, 2)], pt_o.at[i, pl.ds(2 * c, 2)], ptsem.at[i, c])

    over_both(tab.pairs, pair)
    for i in range(items):
        def blank(c, _, i=i):
            ob[rows_of(i, frames), pl.ds(pl.multiple_of(c * LANES, LANES), LANES)] = jnp.zeros((frames, LANES), BF)
            return 0

        lax.fori_loop(tab.pairs[i], width // LANES, blank, 0)
    outs.append(fetch(ob, ob_o, sem.at[4]))
    p.wait(3)
    accs = [dot_nn(ob[rows_of(i, frames), :], w[3]) for i in range(items)]
    for i, acc in enumerate(accs):
        rr = rows_of(i, frames)
        r1[rr, :] = x[rr, :].astype(F32) + (acc + vec[ROW_OB:ROW_OB + 1, :]) * cms[i]
    outs.append(fetch(r1, r1_o, sem.at[5]))
    for i in range(items):
        def drain(c, _, i=i):
            pltpu.make_async_copy(pt.at[i, pl.ds(2 * c, 2)], pt_o.at[i, pl.ds(2 * c, 2)], ptsem.at[i, c]).wait()
            return 0

        lax.fori_loop(0, tab.pairs[i], drain, 0)
    for o in outs:
        o.wait()


def ffn_fwd_kernel(layer, items, frames, last, subnet, vec, ub, r1_any, x_any, *rest):
    n1b_o, g_o, gp_o, r2_o, out_o, w_up, w_down, r1, x, n1b, g, gp, acc, out, wsem, sem, gsem = rest[2:]
    width, units = w_up.shape
    tab = Table(subnet, items, width)
    nblk, nch = units // width, units // UNIT_CHUNK
    loads = [fetch(r1_any, r1, sem.at[0])]
    p = Ffn(layer, rest[:2], w_up, w_down, wsem)
    p.start()
    if last:
        loads.append(fetch(x_any, x, sem.at[1]))
    cms = [lane_mask(width, n) for n in tab.w]
    loads[0].wait()
    for i in range(items):
        rr = rows_of(i, frames)
        xhat, _ = normed(r1[rr, :], cms[i], tab.inv[i])
        n1 = (xhat * vec[ROW_G1:ROW_G1 + 1, :] + vec[ROW_B1:ROW_B1 + 1, :]) * cms[i]
        n1b[rr, :] = n1.astype(BF)
        acc[rr, :] = n1 + vec[ROW_DB:ROW_DB + 1, :] * cms[i]
    outs = [fetch(n1b, n1b_o, sem.at[2])]

    def store_chunk(i, c):
        cols = pl.ds(pl.multiple_of(c * UNIT_CHUNK, UNIT_CHUNK), UNIT_CHUNK)
        rr = rows_of(i, frames)
        return [
            pltpu.make_async_copy(a.at[rr, cols], b.at[rr, cols], gsem.at[k, i, c])
            for k, (a, b) in enumerate(((g, g_o), (gp, gp_o)))
        ]

    def chunk(its, c):
        p.before(c)
        cols = pl.ds(pl.multiple_of(c * UNIT_CHUNK, UNIT_CHUNK), UNIT_CHUNK)
        ids = lax.broadcasted_iota(jnp.int32, (1, UNIT_CHUNK), 1) + c * UNIT_CHUNK
        us = [dot_nn(n1b[rows_of(i, frames), :], w_up[:, cols]) for i in its]
        gbs = []
        for i, u in zip(its, us):
            fm = (ids < pick(i, tab.u)).astype(F32)
            u = (u + ub[0:1, cols]) * fm
            half = 0.5 * (1.0 + lax.erf(u * (0.5 ** 0.5)))
            gb = (u * half).astype(BF)
            g[rows_of(i, frames), cols] = gb
            gp[rows_of(i, frames), cols] = ((half + u * (jnp.exp(u * u * -0.5) * 0.3989422804014327)) * fm).astype(BF)
            gbs.append(gb)
        for i, gb in zip(its, gbs):
            acc[rows_of(i, frames), :] += dot_nn(gb, w_down[cols, :]) * lane_mask(width, pick(i, tab.w))
        for i in its:
            for copy in store_chunk(i, c):
                copy.start()

    over_both(tab.chunks, chunk)
    p.drain(tab.chunks)
    for i in range(items):
        def blank(c, _, i=i):
            cols = pl.ds(pl.multiple_of(c * UNIT_CHUNK, UNIT_CHUNK), UNIT_CHUNK)
            g[rows_of(i, frames), cols] = jnp.zeros((frames, UNIT_CHUNK), BF)
            gp[rows_of(i, frames), cols] = jnp.zeros((frames, UNIT_CHUNK), BF)
            for copy in store_chunk(i, c):
                copy.start()
            return 0

        lax.fori_loop(tab.chunks[i], nch, blank, 0)
    outs.append(fetch(acc, r2_o, sem.at[3]))
    if last:
        loads[1].wait()
    for i in range(items):
        rr = rows_of(i, frames)
        xhat, _ = normed(acc[rr, :], cms[i], tab.inv[i])
        y = ((xhat * vec[ROW_G2:ROW_G2 + 1, :] + vec[ROW_B2:ROW_B2 + 1, :]) * cms[i]).astype(BF)
        if last:
            y = jnp.where(tab.skip[i] == 1, x[rr, :], y)
        out[rr, :] = y
    outs.append(fetch(out, out_o, sem.at[4]))
    for i in range(items):
        for c in range(nch):
            for copy in store_chunk(i, c):
                copy.wait()
    for o in outs:
        o.wait()


class Quarters:
    def __init__(self, stage, out, sems, first):
        self.stage, self.out, self.sems, self.first = stage, out, sems, first

    def copy(self, y, b):
        return pltpu.make_async_copy(self.stage.at[y, b], self.out.at[y, self.first + b], self.sems.at[y, b])

    def start(self, y, b):
        self.copy(y, b).start()

    def wait(self):
        for y in range(self.stage.shape[0]):
            for b in range(self.stage.shape[1]):
                self.copy(y, b).wait()


def ffn_bwd_kernel(layer, items, frames, last, first, subnet, vec, cot_any, dxn_any, r2_any, r1_any, gp_any, g_any, n1b_any,
                   *rest):
    (da_o, dr1_o, sums, grads, w_up, w_down, cot, dxn, r2, r1, gp, g, n1b, du, df, acc, da, stage, wsem, sem,
     gsem, qsem) = rest[(2 if last else 3):]
    width, units = w_up.shape
    tab = Table(subnet, items, width)
    nblk, nch = units // width, units // UNIT_CHUNK
    loads = [fetch(r2_any, r2, sem.at[0]), fetch(cot_any, cot, sem.at[1])]
    if not last:
        loads.append(fetch(dxn_any, dxn, sem.at[2]))
    p = Ffn(layer, rest[:2], w_up, w_down, wsem)
    p.start()

    def load_gp(c):
        cols = pl.ds(pl.multiple_of(c * UNIT_CHUNK, UNIT_CHUNK), UNIT_CHUNK)
        return pltpu.make_async_copy(gp_any.at[:, cols], gp.at[:, cols], gsem.at[c])

    for c in range(nch):
        load_gp(c).start()
    later = [fetch(r1_any, r1, sem.at[3]), fetch(n1b_any, n1b, sem.at[4]), fetch(g_any, g, sem.at[5])]
    sums[...] = jnp.zeros_like(sums)
    for o in loads:
        o.wait()
    for i in range(items):
        rr = rows_of(i, frames)
        cm = lane_mask(width, tab.w[i])
        if last:
            dy = jnp.where(tab.skip[i] == 1, 0.0, cot[rr, :].astype(F32))
        else:
            dy = jnp.where(tab.skip[i] == 1, cot[rr, :], dxn[rr, :]).astype(F32)
        xhat, rstd = normed(r2[rr, :], cm, tab.inv[i])
        dr2, dg, ds = norm_back(dy, xhat, rstd, vec[ROW_G2:ROW_G2 + 1, :], cm, tab.inv[i])
        dfb = dr2.astype(BF)
        df[rr, :] = dfb
        acc[rr, :] = dr2
        sums[ROW_G2:ROW_G2 + 1, 0:width] += dg
        sums[ROW_B2:ROW_B2 + 1, 0:width] += ds
        sums[ROW_DB:ROW_DB + 1, 0:width] += jnp.sum(dfb.astype(F32), axis=0, keepdims=True)

    def chunk(its, c):
        p.before(c)
        load_gp(c).wait()
        cols = pl.ds(pl.multiple_of(c * UNIT_CHUNK, UNIT_CHUNK), UNIT_CHUNK)
        dgs = [dot_nt(df[rows_of(i, frames), :], w_down[cols, :]) for i in its]
        dubs = []
        for i, dg in zip(its, dgs):
            dub = (dg * gp[rows_of(i, frames), cols].astype(F32)).astype(BF)
            du[rows_of(i, frames), cols] = dub
            sums[ROW_UB:ROW_UB + 1, cols] += jnp.sum(dub.astype(F32), axis=0, keepdims=True)
            dubs.append(dub)
        for i, dub in zip(its, dubs):
            acc[rows_of(i, frames), :] += dot_nt(dub, w_up[:, cols])

    over_both(tab.chunks, chunk)
    p.drain(tab.chunks)

    def drain(c, _):
        load_gp(c).wait()
        return 0

    lax.fori_loop(jnp.maximum(tab.chunks[0], tab.chunks[1]), nch, drain, 0)
    for i in range(items):
        def blank(c, _, i=i):
            cols = pl.ds(pl.multiple_of(c * UNIT_CHUNK, UNIT_CHUNK), UNIT_CHUNK)
            du[rows_of(i, frames), cols] = jnp.zeros((frames, UNIT_CHUNK), BF)
            return 0

        lax.fori_loop(tab.chunks[i], nch, blank, 0)
    for o in later:
        o.wait()
    quarters = Quarters(stage, grads, qsem, first)
    rows = stage.shape[3]

    def down_step(f, _):
        y, par = f // 2, f % 2
        for s in range(nblk // 2):
            lanes = pl.ds(pl.multiple_of(f * width + s * 2 * rows, LANES), 2 * rows)
            res = dot_tn(g[:, lanes], df[...]).astype(BF)
            for t in (0, 1):
                stage[y, 2 * s + t, par] = res[t * rows:(t + 1) * rows]

        @pl.when(par == 1)
        def _():
            for b in range(nblk):
                quarters.start(y, b)
        return 0

    lax.fori_loop(0, 4, down_step, 0)
    for i in range(items):
        rr = rows_of(i, frames)
        cm = lane_mask(width, tab.w[i])
        xhat, rstd = normed(r1[rr, :], cm, tab.inv[i])
        d1, dg, ds = norm_back(acc[rr, :], xhat, rstd, vec[ROW_G1:ROW_G1 + 1, :], cm, tab.inv[i])
        acc[rr, :] = d1
        dab = d1.astype(BF)
        da[rr, :] = dab
        sums[ROW_G1:ROW_G1 + 1, 0:width] += dg
        sums[ROW_B1:ROW_B1 + 1, 0:width] += ds
        sums[ROW_OB:ROW_OB + 1, 0:width] += jnp.sum(dab.astype(F32), axis=0, keepdims=True)
    outs = [fetch(acc, dr1_o, sem.at[6]), fetch(da, da_o, sem.at[7])]

    def up_step(j, _):
        cols = pl.ds(pl.multiple_of(j * width, LANES), width)
        for y in (0, 1):
            res = dot_tn(n1b[:, y * 2 * rows:(y + 1) * 2 * rows], du[:, cols]).astype(BF)
            for t in (0, 1):
                stage[y, nblk + j, t] = res[t * rows:(t + 1) * rows]
            quarters.start(y, nblk + j)
        return 0

    lax.fori_loop(0, nblk, up_step, 0)
    quarters.wait()
    for o in outs:
        o.wait()


def attn_bwd_kernel(layer, items, frames, first, subnet, da_any, dr1_any, qkv_any, pt_any, x_any, ob_any, *rest):
    dx_o, sums, grads, w, da, dr1, qkv, pt, x, ob, do, dqkv, dx, stage, wsem, sem, ptsem, qsem = rest[3:]
    width = da.shape[1]
    tab = Table(subnet, items, width)
    loads = [fetch(da_any, da, sem.at[0])]
    p = Attn(layer, rest[:2], w, wsem)
    p.start((3, 0, 1, 2))
    loads.append(fetch(qkv_any, qkv, sem.at[1]))

    def load_pt(i, c):
        return pltpu.make_async_copy(pt_any.at[i, pl.ds(2 * c, 2)], pt.at[i, pl.ds(2 * c, 2)], ptsem.at[i, c])

    npair = width // LANES

    def begin(c, _):
        for i in range(items):
            @pl.when(c < tab.pairs[i])
            def _(i=i):
                load_pt(i, c).start()
        return 0

    lax.fori_loop(0, npair, begin, 0)
    later = [fetch(ob_any, ob, sem.at[2]), fetch(dr1_any, dr1, sem.at[3]), fetch(x_any, x, sem.at[4])]
    sums[...] = jnp.zeros_like(sums)
    loads[0].wait()
    p.wait(3)
    dos = [dot_nt(da[rows_of(i, frames), :], w[3]) for i in range(items)]
    for i, d in enumerate(dos):
        do[rows_of(i, frames), :] = d.astype(BF)
    loads[1].wait()
    scale = HEAD_DIM ** -0.5

    def pair(its, c):
        lanes = pl.ds(pl.multiple_of(c * LANES, LANES), LANES)
        ids = lax.broadcasted_iota(jnp.int32, (1, LANES), 1) + c * LANES
        for i in its:
            load_pt(i, c).wait()
        rr = [rows_of(i, frames) for i in its]
        q = [qkv[0, r, lanes] for r in rr]
        k = [qkv[1, r, lanes] for r in rr]
        v = [qkv[2, r, lanes] for r in rr]
        dob = [do[r, lanes] for r in rr]
        kt = [a.T for a in k]
        heads = [(n, h) for n in range(len(its)) for h in (0, 1)]
        pbs = [pt[its[n], 2 * c + h] for n, h in heads]
        dps = [dot_nt(only(h, v[n]), dob[n]) for n, h in heads]
        dvs = [dot_nn(pb, dob[n]) for pb, (n, h) in zip(pbs, heads)]
        tmps = [pb.astype(F32) * dp for pb, dp in zip(pbs, dps)]
        dss = [(t - pb.astype(F32) * jnp.sum(t, axis=0, keepdims=True)).astype(BF) for t, pb in zip(tmps, pbs)]
        dks = [dot_nn(ds, q[n]) for ds, (n, h) in zip(dss, heads)]
        dqs = [dot_nn(kt[n][h * HEAD_DIM:(h + 1) * HEAD_DIM], ds) for ds, (n, h) in zip(dss, heads)]
        for n, i in enumerate(its):
            hm = (ids < pick(i, tab.a)).astype(F32)
            dq = (jnp.concatenate(dqs[2 * n:2 * n + 2], axis=0).T * (hm * scale)).astype(BF)
            dqkv[0, rr[n], lanes] = dq
            dqkv[1, rr[n], lanes] = (jnp.where(half_mask(0), dks[2 * n], dks[2 * n + 1]) * (hm * scale)).astype(BF)
            dqkv[2, rr[n], lanes] = (jnp.where(half_mask(0), dvs[2 * n], dvs[2 * n + 1]) * hm).astype(BF)
            sums[ROW_QB:ROW_QB + 1, lanes] += jnp.sum(dq.astype(F32), axis=0, keepdims=True)

    over_both(tab.pairs, pair)
    for i in range(items):
        def blank(c, _, i=i):
            lanes = pl.ds(pl.multiple_of(c * LANES, LANES), LANES)
            for j in range(3):
                dqkv[j, rows_of(i, frames), lanes] = jnp.zeros((frames, LANES), BF)
            return 0

        lax.fori_loop(tab.pairs[i], npair, blank, 0)
    for o in later:
        o.wait()
    if layer == 0:
        mask_rows(x, items, frames, tab)
    quarters = Quarters(stage, grads, qsem, first)
    rows = stage.shape[3]

    def step(lhs, rhs, b):
        for y in (0, 1):
            res = dot_tn(lhs[:, y * 2 * rows:(y + 1) * 2 * rows], rhs).astype(BF)
            for t in (0, 1):
                stage[y, b, t] = res[t * rows:(t + 1) * rows]
            quarters.start(y, b)

    def in_step(j, _):
        step(x, dqkv[j], j)
        return 0

    lax.fori_loop(0, 3, in_step, 0)
    step(ob, da[...], 3)
    for j in range(3):
        p.wait(j)

    def back_step(j, _):
        adds = [dot_nt(dqkv[j, rows_of(i, frames), :], w[j]) for i in range(items)]
        for i, add in enumerate(adds):
            dr1[rows_of(i, frames), :] += add
        return 0

    lax.fori_loop(0, 3, back_step, 0)
    for i in range(items):
        rr = rows_of(i, frames)
        dx[rr, :] = (dr1[rr, :] * lane_mask(width, tab.w[i])).astype(BF)
    out = fetch(dx, dx_o, sem.at[5])
    quarters.wait()
    out.wait()


ANY = pl.BlockSpec(memory_space=pl.ANY)
VM = pl.BlockSpec(memory_space=pltpu.VMEM)
SM = pl.BlockSpec(memory_space=pltpu.SMEM)
PARAMS = dict(vmem_limit_bytes=58 * 2 ** 20)


def cost(flops, nbytes):
    return pl.CostEstimate(flops=int(flops), bytes_accessed=int(nbytes), transcendentals=0)


def sds(shape, dtype):
    return jax.ShapeDtypeStruct(shape, dtype)


def run(kernel, name, subnet, vmem, hbm, outs, vmem_outs, scratch, sems, flops, nbytes, alias=None):
    return pl.pallas_call(
        kernel,
        out_shape=tuple(outs),
        in_specs=[SM] + [VM] * len(vmem) + [ANY] * len(hbm),
        out_specs=tuple(VM if k in vmem_outs else ANY for k in range(len(outs))),
        scratch_shapes=[pltpu.VMEM(s, d) for s, d in scratch] + [pltpu.SemaphoreType.DMA(s) for s in sems],
        input_output_aliases={} if alias is None else {len(vmem) + len(hbm): alias},
        compiler_params=pltpu.CompilerParams(**PARAMS),
        cost_estimate=cost(flops, nbytes),
        name=name,
    )(subnet, *vmem, *hbm)


def attn_fwd(layer, subnet, x, vec, weights, items):
    n, d = x.shape
    t = n // items
    return run(
        functools.partial(attn_fwd_kernel, layer, items, t), "attn_fwd", subnet, (vec,), (x, *weights),
        [sds((3, n, d), BF), sds((items, HEADS, t, t), BF), sds((n, d), BF), sds((n, d), F32)], (),
        [((4, d, d), BF), ((n, d), BF), ((3, n, d), BF), ((items, HEADS, t, t), BF), ((n, d), BF), ((n, d), F32)],
        [(4,), (6,), (items, d // LANES)],
        8 * n * d * d + 16 * t * n * d, 8 * d * d + n * d * 24)


def ffn_fwd(layer, last, subnet, r1, x, vec, ub, weights, ff, items):
    n, d = x.shape
    return run(
        functools.partial(ffn_fwd_kernel, layer, items, n // items, last), "ffn_fwd", subnet, (vec, ub),
        (r1, x, *weights),
        [sds((n, d), BF), sds((n, ff), BF), sds((n, ff), BF), sds((n, d), F32), sds((n, d), BF)], (),
        [((d, ff), BF), ((ff, d), BF), ((n, d), F32), ((n, d), BF), ((n, d), BF), ((n, ff), BF), ((n, ff), BF),
         ((n, d), F32), ((n, d), BF)],
        [(ff // d, 2), (5,), (2, items, ff // UNIT_CHUNK)],
        6 * n * d * ff, 4 * d * ff + n * d * 30)


def ffn_bwd(layer, last, first, blocks, subnet, cot, dxn, r2, r1, gp, g, n1b, vec, weights, grads, items):
    n, d = cot.shape
    ff = gp.shape[1]
    q, nb = d // 4, ff // d
    more = () if grads is None else (grads,)
    return run(
        functools.partial(ffn_bwd_kernel, layer, items, n // items, last, first), "ffn_bwd", subnet, (vec,),
        (cot, dxn, r2, r1, gp, g, n1b, *weights, *more),
        [sds((n, d), BF), sds((n, d), F32), sds((8, ff), F32), sds((2, blocks, 2, q, d), BF)], (2,),
        [((d, ff), BF), ((ff, d), BF), ((n, d), BF), ((n, d), BF), ((n, d), F32), ((n, d), F32), ((n, ff), BF),
         ((n, ff), BF), ((n, d), BF), ((n, ff), BF), ((n, d), BF), ((n, d), F32), ((n, d), BF),
         ((2, 2 * nb, 2, q, d), BF)],
        [(nb, 2), (8,), (ff // UNIT_CHUNK,), (2, 2 * nb)],
        10 * n * d * ff, 8 * d * ff + n * d * 40, None if grads is None else 3)


def attn_bwd(layer, first, subnet, da, dr1, qkv, pt, x, ob, weights, grads, items):
    n, d = da.shape
    t = n // items
    q = d // 4
    return run(
        functools.partial(attn_bwd_kernel, layer, items, t, first), "attn_bwd", subnet, (),
        (da, dr1, qkv, pt, x, ob, *weights, grads),
        [sds((n, d), BF), sds((8, d), F32), sds(grads.shape, BF)], (1,),
        [((4, d, d), BF), ((n, d), BF), ((n, d), F32), ((3, n, d), BF), ((items, HEADS, t, t), BF), ((n, d), BF),
         ((n, d), BF), ((n, d), BF), ((3, n, d), BF), ((n, d), BF), ((2, 4, 2, q, d), BF)],
        [(4,), (6,), (items, d // LANES), (2, 4)],
        16 * n * d * d + 32 * t * n * d, 16 * d * d + n * d * 30, 2)


MESH = pl.DeviceIdType.MESH


def flip(axis, bit):
    return {axis: jnp.bitwise_xor(lax.axis_index(axis), 1 << bit)}


def greet(partners):
    barrier = pltpu.get_barrier_semaphore()
    for who in partners:
        pl.semaphore_signal(barrier, inc=1, device_id=who, device_id_type=MESH)
    pl.semaphore_wait(barrier, len(partners))


def gather_kernel(layers, w_in, w_out, w_up, w_down, *rest):
    smalls, full, vec, ub = rest[:8], rest[8:12], rest[12], rest[13]
    every, own, send_sem, recv_sem, local_sem = rest[14], rest[15:19], rest[19], rest[20], rest[21]
    shards = (w_in, w_out, w_up, w_down)
    f = lax.axis_index("fsdp")
    pipe = lax.axis_index("pipe")
    part = 2 * (pipe % 2) + (pipe // 2) % 2
    core, far, xnb, znb = flip("fsdp", 0), flip("fsdp", 1), flip("pipe", 0), flip("pipe", 1)
    rows, width = w_out.shape[1:]
    piece = rows // 4
    half = rows // 2
    count = [0]

    def at(ref, k, layer, row, nrows, col, ncols, quarter):
        base = 0 if quarter is None else pl.multiple_of(quarter * shards[k].shape[1], 8)
        return ref.at[layer, pl.ds(pl.multiple_of(base + row, 8), nrows), pl.ds(col, ncols)]

    def regions(chunk, ab, k):
        kind = chunk[1]
        if kind == 0:
            if ab == 0:
                return [(0, piece * k, piece, 0, 2 * width)]
            return [(0, piece * k, piece, 2 * width, width), (1, piece * k, piece, 0, width)]
        row = (kind - 1) * half
        if ab == 0:
            return [(2, row, half, pl.multiple_of(k * width, LANES), width)]
        return [(3, k * rows + row, half, 0, width)]

    def remote(src, dst, who):
        n = count[0]
        count[0] += 1
        return pltpu.make_async_remote_copy(
            src_ref=src, dst_ref=dst, send_sem=send_sem.at[n], recv_sem=recv_sem.at[n], device_id=who, device_id_type=MESH)

    def move(chunk, ab, k, quarter, who, own=False):
        out = []
        for w, row, nr, col, nc in regions(chunk, ab, k):
            src = at(shards[w], w, chunk[0], row, nr, col, nc, None) if own else at(full[w], w, chunk[0], row, nr, col, nc, quarter)
            out.append(remote(src, at(full[w], w, chunk[0], row, nr, col, nc, quarter), who))
        return out

    def place(ref, w, l):
        n = shards[w].shape[1]
        return ref.at[l, pl.ds(pl.multiple_of(f * n, 8), n)]

    order = [(w, l) for l in range(layers) for w in range(4)]
    loads = [pltpu.make_async_copy(shards[w].at[l], own[w].at[l], local_sem.at[0, w, l]) for w, l in order]
    stores = [pltpu.make_async_copy(own[w].at[l], place(full[w], w, l), local_sem.at[1, w, l]) for w, l in order]
    every[f] = jnp.zeros(every.shape[1:], F32)
    for k, ref in enumerate(smalls):
        for l in range(layers):
            every[f, l, k:k + 1, 0:ref.shape[1]] = ref[l:l + 1, :].astype(F32)
    greet((core, far, xnb, znb))
    chunks = [(l, kind) for l in range(layers) for kind in range(3)]
    started, arrived = [], []

    def start(copies):
        for c in copies:
            c.start()
        started.extend(copies)
        return copies

    def landed(copies):
        for c in copies:
            c.wait_recv()
        arrived.extend(copies)

    q2 = jnp.bitwise_xor(f, 2)
    small_far = start([remote(every.at[f], every.at[f], far)])
    small_core = start([remote(every.at[f], every.at[f], core)])
    y_copies, s2, s3 = {}, {}, {}
    tail = []

    def own_core(l):
        for w in range(4):
            tail.extend(start([remote(shards[w].at[l], place(full[w], w, l), core)]))

    k1, k2, k3 = (jnp.bitwise_xor(part, m) for m in (1, 2, 3))
    n_ch = len(chunks)
    direct = {n: (None, 1, 0)[n % 3] for n in range(n_ch)}
    for t in range(n_ch + 3):
        if t < n_ch:
            y_copies[t] = [start(move(chunks[t], ab, part, f, far, own=True)) for ab in (0, 1)]
            if direct[t] is not None:
                y_copies[t].append(start(move(chunks[t], direct[t], k3, f, far, own=True)))
        if t == 0:
            landed(small_far)
            small_core2 = start([remote(every.at[q2], every.at[q2], core)])
            for c in loads:
                c.start()
        if t < layers:
            own_core(t)
        if t == 1:
            for c, d in zip(loads, stores):
                c.wait()
                d.start()
        n = t - 1
        if 0 <= n < n_ch:
            ch = chunks[n]
            for ab in (0, 1):
                landed(y_copies[n][ab])
            s2[n] = {}
            for ab in (0, 1):
                s2[n]["x", ab] = start(move(ch, ab, part, q2, xnb))
                s2[n]["z", ab] = start(move(ch, ab, part, q2, znb))
            for ab in (0, 1):
                tail.extend(start(move(ch, ab, part, q2, core)))
        n = t - 2
        if 0 <= n < n_ch:
            ch = chunks[n]
            landed(s2[n]["x", 0])
            landed(s2[n]["z", 1])
            s3[n] = {}
            if direct[n] != 0:
                s3[n][0] = start(move(ch, 0, k2, q2, znb))
            if direct[n] != 1:
                s3[n][1] = start(move(ch, 1, k1, q2, xnb))
            if direct[n] is not None:
                landed(y_copies[n][2])
                tail.extend(start(move(ch, direct[n], k3, q2, core)))
            tail.extend(start(move(ch, 0, k2, q2, core)))
            tail.extend(start(move(ch, 1, k1, q2, core)))
        n = t - 3
        if 0 <= n < n_ch:
            ch = chunks[n]
            landed(s2[n]["x", 1])
            landed(s2[n]["z", 0])
            tail.extend(start(move(ch, 1, k2, q2, core)))
            tail.extend(start(move(ch, 0, k1, q2, core)))
            for ab, copies in s3[n].items():
                landed(copies)
                tail.extend(start(move(ch, ab, k3, q2, core)))
    landed(small_core)
    landed(small_core2)
    for q in range(4):
        for l in range(layers):
            vec[l, 0:7, q * rows:(q + 1) * rows] = every[q, l, 0:7, 0:rows]
            ub[l, :, q * width:(q + 1) * width] = every[q, l, 7:8, :]
    landed(tail)
    for c in started:
        c.wait_send()
    for c in stores:
        c.wait()


def gather(w_in, w_out, w_up, w_down, smalls):
    layers = w_in.shape[0]
    weights = (w_in, w_out, w_up, w_down)
    width = w_out.shape[2]
    n = 160
    dma = pltpu.SemaphoreType.DMA
    return pl.pallas_call(
        functools.partial(gather_kernel, layers),
        out_shape=tuple(sds((layers, 4 * w.shape[1], w.shape[2]), BF) for w in weights)
        + (sds((layers, 8, width), F32), sds((layers, 1, 4 * width), F32)),
        in_specs=[ANY] * 4 + [VM] * 8,
        out_specs=(ANY,) * 4 + (VM, VM),
        scratch_shapes=[pltpu.VMEM((4, layers, 8, width), F32)] + [pltpu.VMEM(w.shape, BF) for w in weights]
        + [dma((n,)), dma((n,)), dma((2, 4, layers))],
        compiler_params=pltpu.CompilerParams(collective_id=0, has_side_effects=True),
        name="gather",
    )(*weights, *smalls)


class Reduce:
    LOC, RECV = 6, 4

    def __init__(self, count, bits, g, out, refs):
        self.count, self.bits, self.g, self.out = count, bits, g, out
        self.loc, self.rc, self.ry, self.rx, self.rz, self.fin, self.ss, self.rs, self.ls, self.os = refs
        f, pipe = lax.axis_index("fsdp"), lax.axis_index("pipe")
        self.c, self.y, x, z = f % 2, f // 2, pipe % 2, (pipe // 2) % 2
        rows = g.shape[3]
        half, quarter = rows // 2, rows // 4
        self.who = [flip("fsdp", 0), flip("fsdp", 1)] + [flip("pipe", b) for b in range(bits)]
        part = lambda at, n: pl.ds(pl.multiple_of(at, 16), n)
        self.my_half, self.their_half = part(x * half, half), part((1 - x) * half, half)
        self.mine, self.theirs = part(x * half + z * quarter, quarter), part(x * half + (1 - z) * quarter, quarter)
        self.n_red = 2 + bits
        self.total = self.n_red + 2
        self.slots = self.fin.shape[0]

    @staticmethod
    def scratch(bits, count, rows, d):
        vm, dma = pltpu.VMEM, pltpu.SemaphoreType.DMA
        n = bits + 4
        return [
            vm((Reduce.LOC, 2, rows, d), BF), vm((Reduce.RECV, 2, rows, d), BF), vm((Reduce.RECV, rows, d), BF),
            vm((Reduce.RECV, rows // 2, d), BF), vm((bits - 1, Reduce.RECV, rows // 4, d), BF), vm((n + 2, rows, d), BF),
            dma((n, count)), dma((n, count)), dma((count,)), dma((count,)),
        ]

    def load(self, p):
        return pltpu.make_async_copy(self.g.at[:, p, self.c], self.loc.at[p % self.LOC], self.ls.at[p])

    def store(self, p):
        return pltpu.make_async_copy(self.fin.at[p % self.slots], self.out.at[p], self.os.at[p])

    def move(self, k, p):
        loc, fin, r = self.loc.at[p % self.LOC], self.fin.at[p % self.slots], p % self.RECV
        if k == 0:
            src, dst, who = self.g.at[:, p, 1 - self.c], self.rc.at[r], 0
        elif k == 1:
            src, dst, who = loc.at[1 - self.y], self.ry.at[r], 1
        elif k == 2:
            src, dst, who = loc.at[self.y, self.their_half], self.rx.at[r], 2
        elif k == 3:
            src, dst, who = loc.at[self.y, self.theirs], self.rz.at[0, r], 3
        elif k < self.n_red:
            src, dst, who = fin.at[self.mine], self.rz.at[k - 3, r], k
        elif k == self.n_red:
            src, dst, who = fin.at[self.mine], fin.at[self.mine], 3
        else:
            src, dst, who = fin.at[self.my_half], fin.at[self.my_half], 2
        return pltpu.make_async_remote_copy(
            src_ref=src, dst_ref=dst, send_sem=self.ss.at[k, p], recv_sem=self.rs.at[k, p], device_id=self.who[who],
            device_id_type=MESH)

    def arrive(self, k, p):
        self.move(k, p).wait()
        s, f, r = p % self.LOC, p % self.slots, p % self.RECV
        if k == 0:
            self.load(p).wait()
            self.loc[s] = add_low(self.loc[s], self.rc[r])
        elif k == 1:
            self.loc[s, self.y] = add_low(self.loc[s, self.y], self.ry[r])
        elif k == 2:
            self.loc[s, self.y, self.my_half] = add_low(self.loc[s, self.y, self.my_half], self.rx[r])
        elif k == 3:
            self.fin[f, self.mine] = add_low(self.loc[s, self.y, self.mine], self.rz[0, r])
        elif k < self.n_red:
            self.fin[f, self.mine] = add_low(self.fin[f, self.mine], self.rz[k - 3, r])

    def begin(self):
        self.move(0, 0).start()
        self.load(0).start()

    def tick(self, t):
        @pl.when(t + 1 < self.count)
        def _():
            self.move(0, t + 1).start()
            self.load(t + 1).start()

        for k in range(self.total):
            p = t - k

            @pl.when(jnp.logical_and(p >= 0, p < self.count))
            def _(k=k, p=p):
                self.arrive(k, p)
                if k + 1 < self.total:
                    self.move(k + 1, p).start()
                else:
                    self.store(p).start()

        p = t - self.total

        @pl.when(jnp.logical_and(p >= 0, p < self.count))
        def _():
            self.store(p).wait()

    def ticks(self):
        return self.count + self.total


def add_low(a, b):
    return (a.astype(F32) + b.astype(F32)).astype(BF)


class SumAll:
    def __init__(self, who, total, recv, ss, rs):
        self.who, self.total, self.recv, self.ss, self.rs = who, total, recv, ss, rs

    def move(self, k):
        return pltpu.make_async_remote_copy(
            src_ref=self.total, dst_ref=self.recv.at[k], send_sem=self.ss.at[k], recv_sem=self.rs.at[k],
            device_id=self.who[k], device_id_type=MESH)

    def step(self, k):
        for j in range(len(self.who) + 1):
            @pl.when(k == j)
            def _(j=j):
                if j > 0:
                    self.move(j - 1).wait()
                    self.total[...] = self.total[...] + self.recv[j - 1]
                if j < len(self.who):
                    self.move(j).start()


def attn_back(layer, items, frames, tab, src, buf, weights, sems, first, grads, tick, t0, dx_out):
    qkv_any, pt_any, x_any, ob_any = src
    w, da, dr1, qkv, pt, x, ob, do, dqkv, dx, stage = buf
    wsem, sem, ptsem, qsem = sems
    width = da.shape[1]
    npair = width // LANES
    ring = pt.shape[0]
    p = Attn(layer, weights, w, wsem)
    p.start((3, 0, 1, 2))

    def block(ref, j):
        return ref.at[:, pl.ds(pl.multiple_of(j * width, LANES), width)]

    loads = [fetch(qkv_any.at[j], block(qkv, j), sem.at[3 + j]) for j in range(3)]

    def load_pt(c):
        return pltpu.make_async_copy(pt_any.at[:, pl.ds(2 * c, 2)], pt.at[c % ring], ptsem.at[c])

    for c in range(ring - 1):
        load_pt(c).start()
    later = [fetch(ob_any, ob, sem.at[0]), fetch(x_any, x, sem.at[1])]
    p.wait(3)
    dos = [dot_nt(da[rows_of(i, frames), :], w[3]) for i in range(items)]
    for i, d in enumerate(dos):
        do[rows_of(i, frames), :] = d.astype(BF)
    for o in loads:
        o.wait()
    scale = HEAD_DIM ** -0.5
    qsums = []

    def pair(c, _):
        @pl.when(c % 3 == 0)
        def _():
            tick(t0 + c // 3)

        lanes = pl.ds(pl.multiple_of(c * LANES, LANES), LANES)
        ids = lax.broadcasted_iota(jnp.int32, (1, LANES), 1) + c * LANES
        load_pt(c).wait()

        @pl.when(c + ring - 1 < npair)
        def _():
            load_pt(c + ring - 1).start()

        rr = [rows_of(i, frames) for i in range(items)]
        at = [pl.ds(pl.multiple_of(j * width + c * LANES, LANES), LANES) for j in range(3)]
        q = [qkv[r, at[0]] for r in rr]
        k = [qkv[r, at[1]] for r in rr]
        v = [qkv[r, at[2]] for r in rr]
        dob = [do[r, lanes] for r in rr]
        kt = [a.T for a in k]
        heads = [(n, h) for n in range(items) for h in (0, 1)]
        pbs = [pt[c % ring, n, h] for n, h in heads]
        dps = [dot_nt(only(h, v[n]), dob[n]) for n, h in heads]
        dvs = [dot_nn(pb, dob[n]) for pb, (n, h) in zip(pbs, heads)]
        tmps = [pb.astype(F32) * dp for pb, dp in zip(pbs, dps)]
        dss = [(t - pb.astype(F32) * jnp.sum(t, axis=0, keepdims=True)).astype(BF) for t, pb in zip(tmps, pbs)]
        dks = [dot_nn(ds, q[n]) for ds, (n, h) in zip(dss, heads)]
        dqs = [dot_nn(kt[n][h * HEAD_DIM:(h + 1) * HEAD_DIM], ds) for ds, (n, h) in zip(dss, heads)]
        for n in range(items):
            on = ids < tab.a[n]
            put = lambda v, s: jnp.where(on, v * s, 0.0).astype(BF)
            dqkv[rr[n], at[0]] = put(jnp.concatenate(dqs[2 * n:2 * n + 2], axis=0).T, scale)
            dqkv[rr[n], at[1]] = put(jnp.where(half_mask(0), dks[2 * n], dks[2 * n + 1]), scale)
            dqkv[rr[n], at[2]] = put(jnp.where(half_mask(0), dvs[2 * n], dvs[2 * n + 1]), 1.0)
        return 0

    lax.fori_loop(0, npair, pair, 0)
    t0 = t0 + (npair + 2) // 3
    tick(t0)
    q_sum = jnp.sum(dqkv[:, 0:width].astype(F32), axis=0, keepdims=True)
    for o in later:
        o.wait()
    if layer == 0:
        mask_rows(x, items, frames, tab)
    quarters = Quarters(stage, grads, qsem, first)
    rows = stage.shape[3]

    def step(lhs, rhs, b):
        for y in (0, 1):
            res = dot_tn(lhs[:, y * 2 * rows:(y + 1) * 2 * rows], rhs).astype(BF)
            for t in (0, 1):
                stage[y, b, t] = res[t * rows:(t + 1) * rows]
            quarters.start(y, b)

    def in_step(j, _):
        step(x, block(dqkv, j)[...], j)
        return 0

    lax.fori_loop(0, 3, in_step, 0)
    tick(t0 + 1)
    step(ob, da[...], 3)
    for j in range(3):
        p.wait(j)

    def back_step(j, _):
        adds = [dot_nt(block(dqkv, j)[rows_of(i, frames), :], w[j]) for i in range(items)]
        for i, add in enumerate(adds):
            dr1[rows_of(i, frames), :] += add
        return 0

    lax.fori_loop(0, 3, back_step, 0)
    for i in range(items):
        rr = rows_of(i, frames)
        dx[rr, :] = (dr1[rr, :] * lane_mask(width, tab.w[i])).astype(BF)
    if dx_out is not None:
        fetch(dx, dx_out, sem.at[2])
    quarters.wait()
    tick(t0 + 2)
    return t0 + 3, q_sum


def ffn_back(layer, items, frames, tab, vec, src, buf, weights, sems, first, grads, tick, t0, sums):
    cot_any, r2_any, r1_any, gp_any, g_any, n1b_any = src
    w_up, w_down, cot, dxn, r, du, g, n1b, df, acc, da, stage = buf
    wsem, sem, gsem, qsem = sems
    width, units = w_up.shape
    nblk, nch = units // width, units // UNIT_CHUNK
    p = Ffn(layer, weights, w_up, w_down, wsem)
    p.start()
    loads = [fetch(r2_any, r, sem.at[0]), fetch(cot_any, cot, sem.at[1])]

    def load_gp(c):
        cols = pl.ds(pl.multiple_of(c * UNIT_CHUNK, UNIT_CHUNK), UNIT_CHUNK)
        return pltpu.make_async_copy(gp_any.at[:, cols], du.at[:, cols], gsem.at[c])

    for c in range(nch):
        load_gp(c).start()
    later = [fetch(n1b_any, n1b, sem.at[3]), fetch(g_any, g, sem.at[4])]
    for o in loads:
        o.wait()
    for i in range(items):
        rr = rows_of(i, frames)
        cm = lane_mask(width, tab.w[i])
        dy = jnp.where(tab.skip[i] == 1, cot[rr, :], dxn[rr, :]).astype(F32)
        xhat, rstd = normed(r[rr, :], cm, tab.inv[i])
        dr2, dg, ds = norm_back(dy, xhat, rstd, vec[layer, ROW_G2:ROW_G2 + 1, :], cm, tab.inv[i])
        dfb = dr2.astype(BF)
        df[rr, :] = dfb
        acc[rr, :] = dr2
        sums[ROW_G2:ROW_G2 + 1, 0:width] += dg
        sums[ROW_B2:ROW_B2 + 1, 0:width] += ds
        sums[ROW_DB:ROW_DB + 1, 0:width] += jnp.sum(dfb.astype(F32), axis=0, keepdims=True)
    load_r1 = fetch(r1_any, r, sem.at[2])
    tick(t0)

    def chunk(c):
        p.before(c)
        load_gp(c).wait()
        cols = pl.ds(pl.multiple_of(c * UNIT_CHUNK, UNIT_CHUNK), UNIT_CHUNK)
        dgs = [dot_nt(df[rows_of(i, frames), :], w_down[cols, :]) for i in range(items)]
        dubs = []
        for i, dg in enumerate(dgs):
            dub = (dg * du[rows_of(i, frames), cols].astype(F32)).astype(BF)
            du[rows_of(i, frames), cols] = dub
            sums[ROW_UB:ROW_UB + 1, cols] += jnp.sum(dub.astype(F32), axis=0, keepdims=True)
            dubs.append(dub)
        for i, dub in enumerate(dubs):
            acc[rows_of(i, frames), :] += dot_nt(dub, w_up[:, cols])

    def one(c, _):
        @pl.when(jnp.logical_and(c % 3 == 0, c > 0))
        def _():
            tick(t0 + c // 3)

        chunk(c)
        return 0

    lax.fori_loop(0, nch, one, 0)
    t0 = t0 + (nch + 2) // 3
    tick(t0)
    for o in later:
        o.wait()
    rows = stage.shape[3]
    down = Quarters(stage, grads, qsem.at[0], first)
    up = Quarters(stage, grads, qsem.at[1], first + nblk)

    def down_step(f, _):
        y, par = f // 2, f % 2
        for s in range(nblk // 2):
            lanes = pl.ds(pl.multiple_of(f * width + s * 2 * rows, LANES), 2 * rows)
            res = dot_tn(g[:, lanes], df[...]).astype(BF)
            for t in (0, 1):
                stage[y, 2 * s + t, par] = res[t * rows:(t + 1) * rows]
        return 0

    lax.fori_loop(0, 4, down_step, 0)
    for y in (0, 1):
        for b in range(nblk):
            down.start(y, b)
    tick(t0 + 1)
    load_r1.wait()
    for i in range(items):
        rr = rows_of(i, frames)
        cm = lane_mask(width, tab.w[i])
        xhat, rstd = normed(r[rr, :], cm, tab.inv[i])
        d1, dg, ds = norm_back(acc[rr, :], xhat, rstd, vec[layer, ROW_G1:ROW_G1 + 1, :], cm, tab.inv[i])
        acc[rr, :] = d1
        dab = d1.astype(BF)
        da[rr, :] = dab
        sums[ROW_G1:ROW_G1 + 1, 0:width] += dg
        sums[ROW_B1:ROW_B1 + 1, 0:width] += ds
        sums[ROW_OB:ROW_OB + 1, 0:width] += jnp.sum(dab.astype(F32), axis=0, keepdims=True)
    down.wait()
    tick(t0 + 2)

    def up_step(j, _):
        cols = pl.ds(pl.multiple_of(j * width, LANES), width)
        for y in (0, 1):
            res = dot_tn(n1b[:, y * 2 * rows:(y + 1) * 2 * rows], du[:, cols]).astype(BF)
            for t in (0, 1):
                stage[y, j, t] = res[t * rows:(t + 1) * rows]
            up.start(y, j)
        return 0

    lax.fori_loop(0, nblk, up_step, 0)
    up.wait()
    tick(t0 + 3)
    return t0 + 4


def back_kernel(items, frames, bits, blocks, subnet, vec, s_top, da_any, dr1_any, cot_any, *rest):
    top, bottom, mid, weights = rest[:4], rest[4:8], rest[8:13], rest[13:17]
    (dx_o, grads, out, total, w_up, w, da, dr1, pt, x, ob, do, dx, r, du, g, stage, srecv) = rest[18:36]
    asem, bsem, fsem = rest[36:40], rest[40:44], rest[44:48]
    red = Reduce(2 * blocks, bits, grads, out, rest[48:58])
    s_send, s_recv, isem = rest[58:]
    width = da.shape[1]
    tab = Table(subnet, items, width)
    loads = [fetch(da_any, da, isem.at[0]), fetch(dr1_any, dr1, isem.at[1])]
    greet(red.who)
    red.begin()
    total[1] = s_top[...]
    total[0] = jnp.zeros(total.shape[1:], F32)
    nb = w_up.shape[1] // width
    w_att, w_ffn = weights[:2], weights[2:]
    for o in loads:
        o.wait()
    buf = (w, da, dr1, du, pt, x, ob, do, g, dx, stage)
    t, q_sum = attn_back(1, items, frames, tab, top, buf, w_att, asem, 2 * nb, grads, red.tick, 0, None)
    total[1, ROW_QB:ROW_QB + 1, 0:width] = q_sum
    w_down = w.reshape(nb * width, width)
    buf_f = (w_up, w_down, x, dx, r, du, g, ob, do, dr1, da, stage)
    t = ffn_back(0, items, frames, tab, vec, (cot_any,) + tuple(mid), buf_f, w_ffn, fsem, blocks, grads, red.tick, t, total.at[0])
    t, q_sum = attn_back(0, items, frames, tab, bottom, buf, w_att, bsem, blocks + 2 * nb, grads, red.tick, t, dx_o)
    total[0, ROW_QB:ROW_QB + 1, 0:width] = q_sum
    small = SumAll(red.who, total, srecv, s_send, s_recv)

    def rest_of(n, _):
        red.tick(n)
        small.step(n - t)
        return 0

    lax.fori_loop(t, red.ticks(), rest_of, 0)
    pltpu.make_async_copy(dx, dx_o, bsem[1].at[2]).wait()


def back(subnet, vec, s_top, da, dr1, cot, top, bottom, mid, weights, grads, items):
    bits = 0
    while (1 << bits) < lax.axis_size("pipe"):
        bits += 1
    n, d = cot.shape
    ff = mid[2].shape[1]
    t = n // items
    rows, nb = d // 4, ff // d
    blocks = 2 * nb + 4
    small = (2,) + s_top.shape
    vm, dma = pltpu.VMEM, pltpu.SemaphoreType.DMA
    square = vm((n, d), BF)
    hbm = (da, dr1, cot, *top, *bottom, *mid, *weights, grads)
    asems = [dma((4,)), dma((6,)), dma((d // LANES,)), dma((2, 4))]
    return pl.pallas_call(
        functools.partial(back_kernel, items, t, bits, blocks),
        out_shape=(sds((n, d), BF), sds(grads.shape, BF), sds((2 * blocks, rows, d), BF), sds(small, F32)),
        in_specs=[SM, VM, VM] + [ANY] * len(hbm),
        out_specs=(ANY, ANY, ANY, VM),
        scratch_shapes=[
            vm((d, ff), BF), vm((4, d, d), BF), square, vm((n, d), F32), vm((3, items, 2, t, t), BF),
            square, square, square, square, vm((n, d), F32), vm((n, ff), BF), vm((n, ff), BF),
            vm((2, 4, 2, rows, d), BF), vm((2 + bits,) + small, F32),
            *asems, *asems, dma((nb, 2)), dma((5,)), dma((ff // UNIT_CHUNK,)), dma((2, 2, nb)),
            *Reduce.scratch(bits, 2 * blocks, rows, d), dma((2 + bits,)), dma((2 + bits,)), dma((2,)),
        ],
        input_output_aliases={2 + len(hbm): 1},
        compiler_params=pltpu.CompilerParams(collective_id=1, has_side_effects=True, vmem_limit_bytes=60 * 2 ** 20),
        name="back",
    )(subnet, vec, s_top, *hbm)


def finish_kernel(layers, red, total, g_in, g_out, g_up, g_down, *rest):
    vecs, (bf, f32, sem_in, sem_out) = rest[:8], rest[8:]
    f = lax.axis_index("fsdp")
    blocks = bf.shape[0]
    rows, d = bf.shape[1:]
    per = blocks // layers
    nb = (per - 4) // 2

    def target(l, k):
        if k < nb:
            return g_down.at[l, pl.ds(k * rows, rows)]
        if k < 2 * nb:
            return g_up.at[l, :, pl.ds((k - nb) * d, d)]
        if k < 2 * nb + 3:
            return g_in.at[l, :, pl.ds((k - 2 * nb) * d, d)]
        return g_out.at[l]

    loads = [pltpu.make_async_copy(red.at[p], bf.at[p], sem_in.at[p]) for p in range(blocks)]
    stores = [pltpu.make_async_copy(f32.at[p], target(layers - 1 - p // per, p % per), sem_out.at[p]) for p in range(blocks)]
    for c in loads:
        c.start()
    for q in range(4):
        @pl.when(f == q)
        def _(q=q):
            for l in range(layers):
                for k in range(7):
                    vecs[k][l:l + 1, :] = total[l, k:k + 1, q * rows:(q + 1) * rows]
                vecs[7][l:l + 1, :] = total[l, 7:8, q * d:(q + 1) * d]
    for p in range(blocks):
        loads[p].wait()
        f32[p] = bf[p].astype(F32)
        stores[p].start()
    for c in stores:
        c.wait()


def finish(red, total):
    blocks, rows, d = red.shape
    layers = total.shape[0]
    nb = (blocks // layers - 4) // 2
    return pl.pallas_call(
        functools.partial(finish_kernel, layers),
        out_shape=(sds((layers, rows, 3 * d), F32), sds((layers, rows, d), F32), sds((layers, rows, nb * d), F32),
                   sds((layers, nb * rows, d), F32)) + (sds((layers, rows), F32),) * 7 + (sds((layers, d), F32),),
        in_specs=[ANY, VM],
        out_specs=(ANY,) * 4 + (VM,) * 8,
        scratch_shapes=[pltpu.VMEM(red.shape, BF), pltpu.VMEM(red.shape, F32), pltpu.SemaphoreType.DMA((blocks,)),
                        pltpu.SemaphoreType.DMA((blocks,))],
        compiler_params=pltpu.CompilerParams(**PARAMS),
        name="finish",
    )(red, total)


def local(
    frames_in, attn_in, q_bias, attn_out, out_bias, norm1_gain, norm1_bias, ffn_up, up_bias, ffn_down, down_bias,
    norm2_gain, norm2_bias, subnet, out_cotangent,
):
    items, frames, width = frames_in.shape
    ff = ffn_up.shape[2]
    layers = attn_in.shape[0]
    nb = ff // width
    *weights, vec, ub = gather(
        attn_in, attn_out, ffn_up, ffn_down,
        (q_bias, out_bias, norm1_gain, norm1_bias, down_bias, norm2_gain, norm2_bias, up_bias))
    w_att, w_ffn = weights[:2], weights[2:]

    n = items * frames
    cur = frames_in.reshape(n, width)
    kept = []
    for l in range(layers):
        qkv, pt, ob, r1 = attn_fwd(l, subnet, cur, vec[l], w_att, items)
        n1b, g, gp, r2, out = ffn_fwd(l, l == layers - 1, subnet, r1, cur, vec[l], ub[l], w_ffn, ff, items)
        kept.append((cur, qkv, pt, ob, r1, n1b, g, gp, r2))
        cur = out
    layer_out = cur.reshape(frames_in.shape)

    cot = out_cotangent.reshape(n, width)
    x1, qkv1, pt1, ob1, r1, n1b, g, gp, r2 = kept[1]
    da, dr1, s_top, grads = ffn_bwd(
        1, True, 0, 2 * (2 * nb + 4), subnet, cot, cot, r2, r1, gp, g, n1b, vec[1], w_ffn, None, items)
    x0, qkv0, pt0, ob0, r1, n1b, g, gp, r2 = kept[0]
    dx, _, red, total = back(
        subnet, vec, s_top, da, dr1, cot, (qkv1, pt1, x1, ob1), (qkv0, pt0, x0, ob0), (r2, r1, gp, g, n1b), weights, grads,
        items)
    dx = dx.reshape(frames_in.shape)
    g_in, g_out, g_up, g_down, g_qb, g_ob, g_g1, g_b1, g_db, g_g2, g_b2, g_ub = finish(red, total)
    return (layer_out, dx, g_in, g_qb, g_out, g_ob, g_g1, g_b1, g_up, g_ub, g_down, g_db, g_g2, g_b2)


def solution(mesh):
    rows3 = P(None, "fsdp", None)
    rows2 = P(None, "fsdp")
    item = P(("pipe", "fsdp"), None, None)
    weights = (rows3, rows2, rows3, rows2, rows2, rows2, rows3, rows2, rows3, rows2, rows2, rows2)
    return jax.shard_map(
        local, mesh=mesh, in_specs=(item,) + weights + (P(), item), out_specs=(item, item) + weights, check_vma=False,
    )
```

```python
import functools

import jax
import jax.numpy as jnp
from jax import lax
from jax.experimental import pallas as pl
from jax.experimental.pallas import tpu as pltpu
from jax.sharding import PartitionSpec as P

HEADS = 12
HEAD_DIM = 64
EPSILON = 1e-05
LANES = 128
UNIT_CHUNK = 512
BF = jnp.bfloat16
F32 = jnp.float32

ROW_QB, ROW_OB, ROW_G1, ROW_B1, ROW_DB, ROW_G2, ROW_B2, ROW_UB = 0, 1, 2, 3, 4, 5, 6, 7

def dot_nn(a, b):
    return lax.dot_general(a, b, (((1,), (0,)), ((), ())), preferred_element_type=F32)


def dot_nt(a, b):
    return lax.dot_general(a, b, (((1,), (1,)), ((), ())), preferred_element_type=F32)


def dot_tn(a, b):
    return lax.dot_general(a, b, (((0,), (0,)), ((), ())), preferred_element_type=F32)


def lane_mask(width, count):
    return (lax.broadcasted_iota(jnp.int32, (1, width), 1) < count).astype(F32)


def normed(rows, cm, inv_w):
    mean = jnp.sum(rows * cm, axis=-1, keepdims=True) * inv_w
    centered = (rows - mean) * cm
    var = jnp.sum(centered * centered, axis=-1, keepdims=True) * inv_w
    rstd = lax.rsqrt(var + EPSILON)
    return centered * rstd, rstd


def norm_back(dy, xhat, rstd, gain, cm, inv_w):
    dym = dy * cm
    dg = jnp.sum(dym * xhat, axis=0, keepdims=True)
    ds = jnp.sum(dym, axis=0, keepdims=True)
    dx = dym * gain
    m1 = jnp.sum(dx, axis=-1, keepdims=True) * inv_w
    m2 = jnp.sum(dx * xhat, axis=-1, keepdims=True) * inv_w
    return cm * (rstd * (dx - m1 - xhat * m2)), dg, ds


class Attn:
    def __init__(self, layer, refs, w, sems):
        w_in, w_out = refs
        d = w.shape[1]
        self.copies = [
            pltpu.make_async_copy(w_in.at[layer, :, pl.ds(b * d, d)], w.at[b], sems.at[b]) for b in range(3)
        ] + [pltpu.make_async_copy(w_out.at[layer], w.at[3], sems.at[3])]

    def start(self, order):
        for b in order:
            self.copies[b].start()

    def wait(self, b):
        self.copies[b].wait()


class Ffn:
    def __init__(self, layer, refs, w_up, w_down, sems):
        up, down = refs
        d = w_up.shape[0]
        self.blocks = w_up.shape[1] // d
        self.first = [b * d // UNIT_CHUNK for b in range(self.blocks)]
        self.copies = [(
            pltpu.make_async_copy(up.at[layer, :, pl.ds(b * d, d)], w_up.at[:, pl.ds(b * d, d)], sems.at[b, 0]),
            pltpu.make_async_copy(down.at[layer, pl.ds(b * d, d)], w_down.at[pl.ds(b * d, d)], sems.at[b, 1]),
        ) for b in range(self.blocks)]

    def start(self):
        for pair in self.copies:
            for copy in pair:
                copy.start()

    def wait(self, b):
        for copy in self.copies[b]:
            copy.wait()

    def before(self, c):
        for b in range(self.blocks):
            @pl.when(c == self.first[b])
            def _(b=b):
                self.wait(b)

    def drain(self, counts):
        most = jnp.maximum(counts[0], counts[1])
        for b in range(self.blocks):
            @pl.when(most <= self.first[b])
            def _(b=b):
                self.wait(b)


class Table:
    def __init__(self, subnet, items, width):
        segment = lax.axis_index("pipe") // (lax.axis_size("pipe") // 2)
        codes = [[subnet[k, segment * items + i] for k in range(4)] for i in range(items)]
        widths = [width * (4 + k) // 6 for k in range(3)]
        self.w = [width * (4 + c[0]) // 6 for c in codes]
        self.inv = [
            jnp.where(c[0] == 0, 1.0 / widths[0], jnp.where(c[0] == 1, 1.0 / widths[1], 1.0 / widths[2])) for c in codes]
        self.a = [HEAD_DIM * (HEADS * (4 + c[1]) // 6) for c in codes]
        self.u = [w * (6 + c[2]) // 2 for w, c in zip(self.w, codes)]
        self.skip = [c[3] for c in codes]
        self.pairs = [(a + LANES - 1) // LANES for a in self.a]
        self.chunks = [(u + UNIT_CHUNK - 1) // UNIT_CHUNK for u in self.u]


def fetch(src, dst, sem):
    copy = pltpu.make_async_copy(src, dst, sem)
    copy.start()
    return copy


def pick(i, values):
    return values[i] if isinstance(i, int) else jnp.where(i == 0, values[0], values[1])


def rows_of(i, frames):
    if isinstance(i, int):
        return pl.ds(i * frames, frames)
    return pl.ds(pl.multiple_of(i * frames, frames), frames)


def over_both(counts, body):
    n0, n1 = counts
    low, high = jnp.minimum(n0, n1), jnp.maximum(n0, n1)
    longer = (n1 > n0).astype(jnp.int32)

    def both(c, _):
        body((0, 1), c)
        return 0

    def one(c, _):
        body((longer,), c)
        return 0

    lax.fori_loop(0, low, both, 0)
    lax.fori_loop(low, high, one, 0)


def mask_rows(x, items, frames, tab):
    for i in range(items):
        rr = rows_of(i, frames)
        x[rr, :] = jnp.where(lane_mask(x.shape[1], tab.w[i]) > 0, x[rr, :], jnp.zeros((), x.dtype))


def half_mask(h):
    low = lax.broadcasted_iota(jnp.int32, (1, LANES), 1) < HEAD_DIM
    return low if h == 0 else jnp.logical_not(low)


def only(h, x):
    return jnp.where(half_mask(h), x, jnp.zeros_like(x))


def attn_front(layer, items, frames, tab, vec, buf, weights, sems, outs, hooks):
    w, x, qkv, pt, ob, r1 = buf
    wsem, sem, ptsem = sems
    qkv_o, pt_o, ob_o, r1_o = outs
    width = x.shape[1]
    npair = width // LANES
    p = Attn(layer, weights, w, wsem)
    p.start((0, 1, 2, 3))
    cms = [lane_mask(width, n) for n in tab.w]
    hms = [lane_mask(width, n) for n in tab.a]
    done = []
    for j in range(3):
        p.wait(j)
        accs = [dot_nn(x[rows_of(i, frames), :], w[j]) for i in range(items)]
        for i, acc in enumerate(accs):
            if j == 0:
                acc = acc + vec[layer, ROW_QB:ROW_QB + 1, :]
            qkv[j, rows_of(i, frames), :] = (acc * hms[i]).astype(BF)
        done.append(fetch(qkv.at[j], qkv_o.at[j], sem.at[j]))

    def store(c):
        return pltpu.make_async_copy(pt.at[:, pl.ds(2 * c, 2)], pt_o.at[:, pl.ds(2 * c, 2)], ptsem.at[c])

    def pair(c, _):
        for at, hook in hooks.items():
            @pl.when(c == at)
            def _(hook=hook):
                hook()

        lanes = pl.ds(pl.multiple_of(c * LANES, LANES), LANES)
        vts, ss = [], []
        for i in range(items):
            rr = rows_of(i, frames)
            q = qkv[0, rr, lanes] * jnp.asarray(HEAD_DIM ** -0.5, BF)
            k = qkv[1, rr, lanes]
            vts.append(qkv[2, rr, lanes].T)
            ss += [dot_nt(only(h, k), q) for h in (0, 1)]
        es = [jnp.exp(s - jnp.max(s, axis=0, keepdims=True)) for s in ss]
        pbs = [(e * (1.0 / jnp.sum(e, axis=0, keepdims=True))).astype(BF) for e in es]
        for i in range(items):
            mixed = []
            for h in (0, 1):
                pt[i, 2 * c + h] = pbs[2 * i + h]
                mixed.append(dot_nn(vts[i][h * HEAD_DIM:(h + 1) * HEAD_DIM], pbs[2 * i + h]))
            ob[rows_of(i, frames), lanes] = jnp.concatenate(mixed, axis=0).T.astype(BF)
        store(c).start()
        return 0

    lax.fori_loop(0, npair, pair, 0)
    done.append(fetch(ob, ob_o, sem.at[3]))
    p.wait(3)
    accs = [dot_nn(ob[rows_of(i, frames), :], w[3]) for i in range(items)]
    for i, acc in enumerate(accs):
        rr = rows_of(i, frames)
        r1[rr, :] = x[rr, :].astype(F32) + (acc + vec[layer, ROW_OB:ROW_OB + 1, :]) * cms[i]
    done.append(fetch(r1, r1_o, sem.at[4]))

    def finish():
        for c in range(npair):
            store(c).wait()
        for o in done:
            o.wait()

    return finish


def ffn_front(layer, last, items, frames, tab, vec, ub, buf, weights, sems, outs, hooks):
    w_up, w_down, r1, x, n1b, g, gp, acc = buf
    wsem, sem, gsem = sems
    n1b_o, g_o, gp_o, r2_o, out_o = outs
    width, units = w_up.shape
    nch = units // UNIT_CHUNK
    p = Ffn(layer, weights, w_up, w_down, wsem)
    p.start()
    cms = [lane_mask(width, n) for n in tab.w]
    for i in range(items):
        rr = rows_of(i, frames)
        xhat, _ = normed(r1[rr, :], cms[i], tab.inv[i])
        n1 = (xhat * vec[layer, ROW_G1:ROW_G1 + 1, :] + vec[layer, ROW_B1:ROW_B1 + 1, :]) * cms[i]
        n1b[rr, :] = n1.astype(BF)
        acc[rr, :] = n1 + vec[layer, ROW_DB:ROW_DB + 1, :] * cms[i]
    done = [fetch(n1b, n1b_o, sem.at[0])]

    def store(k, c):
        cols = pl.ds(pl.multiple_of(c * UNIT_CHUNK, UNIT_CHUNK), UNIT_CHUNK)
        ref, out = ((g, g_o), (gp, gp_o))[k]
        return pltpu.make_async_copy(ref.at[:, cols], out.at[:, cols], gsem.at[k, c])

    def chunk(c, _):
        for at, hook in hooks.items():
            @pl.when(c == at)
            def _(hook=hook):
                hook()

        p.before(c)
        cols = pl.ds(pl.multiple_of(c * UNIT_CHUNK, UNIT_CHUNK), UNIT_CHUNK)
        ids = lax.broadcasted_iota(jnp.int32, (1, UNIT_CHUNK), 1) + c * UNIT_CHUNK
        us = [dot_nn(n1b[rows_of(i, frames), :], w_up[:, cols]) for i in range(items)]
        gbs = []
        for i, u in enumerate(us):
            fm = (ids < tab.u[i]).astype(F32)
            u = (u + ub[layer, 0:1, cols]) * fm
            half = 0.5 * (1.0 + lax.erf(u * (0.5 ** 0.5)))
            gb = (u * half).astype(BF)
            g[rows_of(i, frames), cols] = gb
            gp[rows_of(i, frames), cols] = ((half + u * (jnp.exp(u * u * -0.5) * 0.3989422804014327)) * fm).astype(BF)
            gbs.append(gb)
        for i, gb in enumerate(gbs):
            acc[rows_of(i, frames), :] += dot_nn(gb, w_down[cols, :]) * cms[i]
        for k in (0, 1):
            store(k, c).start()
        return 0

    lax.fori_loop(0, nch, chunk, 0)
    done.append(fetch(acc, r2_o, sem.at[1]))
    for i in range(items):
        rr = rows_of(i, frames)
        xhat, _ = normed(acc[rr, :], cms[i], tab.inv[i])
        y = ((xhat * vec[layer, ROW_G2:ROW_G2 + 1, :] + vec[layer, ROW_B2:ROW_B2 + 1, :]) * cms[i]).astype(BF)
        if last:
            y = jnp.where(tab.skip[i] == 1, x[rr, :], y)
        x[rr, :] = y
    done.append(fetch(x, out_o, sem.at[2]))

    def finish():
        for c in range(nch):
            for k in (0, 1):
                store(k, c).wait()
        for o in done:
            o.wait()

    return finish


class Quarters:
    def __init__(self, stage, out, sems, first):
        self.stage, self.out, self.sems, self.first = stage, out, sems, first

    def copy(self, y, b):
        return pltpu.make_async_copy(self.stage.at[y, b], self.out.at[y, self.first + b], self.sems.at[y, b])

    def start(self, y, b):
        self.copy(y, b).start()

    def wait(self):
        for y in range(self.stage.shape[0]):
            for b in range(self.stage.shape[1]):
                self.copy(y, b).wait()


def ffn_bwd_kernel(layer, items, frames, last, first, subnet, vec, cot_any, dxn_any, r2_any, r1_any, gp_any, g_any, n1b_any,
                   *rest):
    (da_o, dr1_o, sums, grads, w_up, w_down, cot, dxn, r2, r1, gp, g, n1b, du, df, acc, da, stage, wsem, sem,
     gsem, qsem) = rest[(2 if last else 3):]
    width, units = w_up.shape
    tab = Table(subnet, items, width)
    nblk, nch = units // width, units // UNIT_CHUNK
    loads = [fetch(r2_any, r2, sem.at[0]), fetch(cot_any, cot, sem.at[1])]
    if not last:
        loads.append(fetch(dxn_any, dxn, sem.at[2]))
    p = Ffn(layer, rest[:2], w_up, w_down, wsem)
    p.start()

    def load_gp(c):
        cols = pl.ds(pl.multiple_of(c * UNIT_CHUNK, UNIT_CHUNK), UNIT_CHUNK)
        return pltpu.make_async_copy(gp_any.at[:, cols], gp.at[:, cols], gsem.at[c])

    for c in range(nch):
        load_gp(c).start()
    later = [fetch(r1_any, r1, sem.at[3]), fetch(n1b_any, n1b, sem.at[4]), fetch(g_any, g, sem.at[5])]
    sums[...] = jnp.zeros_like(sums)
    for o in loads:
        o.wait()
    for i in range(items):
        rr = rows_of(i, frames)
        cm = lane_mask(width, tab.w[i])
        if last:
            dy = jnp.where(tab.skip[i] == 1, 0.0, cot[rr, :].astype(F32))
        else:
            dy = jnp.where(tab.skip[i] == 1, cot[rr, :], dxn[rr, :]).astype(F32)
        xhat, rstd = normed(r2[rr, :], cm, tab.inv[i])
        dr2, dg, ds = norm_back(dy, xhat, rstd, vec[ROW_G2:ROW_G2 + 1, :], cm, tab.inv[i])
        dfb = dr2.astype(BF)
        df[rr, :] = dfb
        acc[rr, :] = dr2
        sums[ROW_G2:ROW_G2 + 1, 0:width] += dg
        sums[ROW_B2:ROW_B2 + 1, 0:width] += ds
        sums[ROW_DB:ROW_DB + 1, 0:width] += jnp.sum(dfb.astype(F32), axis=0, keepdims=True)

    def chunk(its, c):
        p.before(c)
        load_gp(c).wait()
        cols = pl.ds(pl.multiple_of(c * UNIT_CHUNK, UNIT_CHUNK), UNIT_CHUNK)
        dgs = [dot_nt(df[rows_of(i, frames), :], w_down[cols, :]) for i in its]
        dubs = []
        for i, dg in zip(its, dgs):
            dub = (dg * gp[rows_of(i, frames), cols].astype(F32)).astype(BF)
            du[rows_of(i, frames), cols] = dub
            sums[ROW_UB:ROW_UB + 1, cols] += jnp.sum(dub.astype(F32), axis=0, keepdims=True)
            dubs.append(dub)
        for i, dub in zip(its, dubs):
            acc[rows_of(i, frames), :] += dot_nt(dub, w_up[:, cols])

    over_both(tab.chunks, chunk)
    p.drain(tab.chunks)

    def drain(c, _):
        load_gp(c).wait()
        return 0

    lax.fori_loop(jnp.maximum(tab.chunks[0], tab.chunks[1]), nch, drain, 0)
    for i in range(items):
        def blank(c, _, i=i):
            cols = pl.ds(pl.multiple_of(c * UNIT_CHUNK, UNIT_CHUNK), UNIT_CHUNK)
            du[rows_of(i, frames), cols] = jnp.zeros((frames, UNIT_CHUNK), BF)
            return 0

        lax.fori_loop(tab.chunks[i], nch, blank, 0)
    for o in later:
        o.wait()
    quarters = Quarters(stage, grads, qsem, first)
    rows = stage.shape[3]

    def down_step(f, _):
        y, par = f // 2, f % 2
        for s in range(nblk // 2):
            lanes = pl.ds(pl.multiple_of(f * width + s * 2 * rows, LANES), 2 * rows)
            res = dot_tn(g[:, lanes], df[...]).astype(BF)
            for t in (0, 1):
                stage[y, 2 * s + t, par] = res[t * rows:(t + 1) * rows]

        @pl.when(par == 1)
        def _():
            for b in range(nblk):
                quarters.start(y, b)
        return 0

    lax.fori_loop(0, 4, down_step, 0)
    for i in range(items):
        rr = rows_of(i, frames)
        cm = lane_mask(width, tab.w[i])
        xhat, rstd = normed(r1[rr, :], cm, tab.inv[i])
        d1, dg, ds = norm_back(acc[rr, :], xhat, rstd, vec[ROW_G1:ROW_G1 + 1, :], cm, tab.inv[i])
        acc[rr, :] = d1
        dab = d1.astype(BF)
        da[rr, :] = dab
        sums[ROW_G1:ROW_G1 + 1, 0:width] += dg
        sums[ROW_B1:ROW_B1 + 1, 0:width] += ds
        sums[ROW_OB:ROW_OB + 1, 0:width] += jnp.sum(dab.astype(F32), axis=0, keepdims=True)
    outs = [fetch(acc, dr1_o, sem.at[6]), fetch(da, da_o, sem.at[7])]

    def up_step(j, _):
        cols = pl.ds(pl.multiple_of(j * width, LANES), width)
        for y in (0, 1):
            res = dot_tn(n1b[:, y * 2 * rows:(y + 1) * 2 * rows], du[:, cols]).astype(BF)
            for t in (0, 1):
                stage[y, nblk + j, t] = res[t * rows:(t + 1) * rows]
            quarters.start(y, nblk + j)
        return 0

    lax.fori_loop(0, nblk, up_step, 0)
    quarters.wait()
    for o in outs:
        o.wait()


ANY = pl.BlockSpec(memory_space=pl.ANY)
VM = pl.BlockSpec(memory_space=pltpu.VMEM)
SM = pl.BlockSpec(memory_space=pltpu.SMEM)
PARAMS = dict(vmem_limit_bytes=58 * 2 ** 20)


def cost(flops, nbytes):
    return pl.CostEstimate(flops=int(flops), bytes_accessed=int(nbytes), transcendentals=0)


def sds(shape, dtype):
    return jax.ShapeDtypeStruct(shape, dtype)


def run(kernel, name, subnet, vmem, hbm, outs, vmem_outs, scratch, sems, flops, nbytes, alias=None):
    return pl.pallas_call(
        kernel,
        out_shape=tuple(outs),
        in_specs=[SM] + [VM] * len(vmem) + [ANY] * len(hbm),
        out_specs=tuple(VM if k in vmem_outs else ANY for k in range(len(outs))),
        scratch_shapes=[pltpu.VMEM(s, d) for s, d in scratch] + [pltpu.SemaphoreType.DMA(s) for s in sems],
        input_output_aliases={} if alias is None else {len(vmem) + len(hbm): alias},
        compiler_params=pltpu.CompilerParams(**PARAMS),
        cost_estimate=cost(flops, nbytes),
        name=name,
    )(subnet, *vmem, *hbm)


def ffn_bwd(layer, last, first, blocks, subnet, cot, dxn, r2, r1, gp, g, n1b, vec, weights, grads, items):
    n, d = cot.shape
    ff = gp.shape[1]
    q, nb = d // 4, ff // d
    more = () if grads is None else (grads,)
    return run(
        functools.partial(ffn_bwd_kernel, layer, items, n // items, last, first), "ffn_bwd", subnet, (vec,),
        (cot, dxn, r2, r1, gp, g, n1b, *weights, *more),
        [sds((n, d), BF), sds((n, d), F32), sds((8, ff), F32), sds((2, blocks, 2, q, d), BF)], (2,),
        [((d, ff), BF), ((ff, d), BF), ((n, d), BF), ((n, d), BF), ((n, d), F32), ((n, d), F32), ((n, ff), BF),
         ((n, ff), BF), ((n, d), BF), ((n, ff), BF), ((n, d), BF), ((n, d), F32), ((n, d), BF),
         ((2, 2 * nb, 2, q, d), BF)],
        [(nb, 2), (8,), (ff // UNIT_CHUNK,), (2, 2 * nb)],
        10 * n * d * ff, 8 * d * ff + n * d * 40, None if grads is None else 3)


MESH = pl.DeviceIdType.MESH


def flip(axis, bit):
    return {axis: jnp.bitwise_xor(lax.axis_index(axis), 1 << bit)}


def greet(partners):
    barrier = pltpu.get_barrier_semaphore()
    for who in partners:
        pl.semaphore_signal(barrier, inc=1, device_id=who, device_id_type=MESH)
    pl.semaphore_wait(barrier, len(partners))


class Gather:
    def __init__(self, layers, shards, full, every, send_sem, recv_sem):
        self.layers, self.shards, self.full, self.every = layers, shards, full, every
        self.send_sem, self.recv_sem = send_sem, recv_sem
        self.f = lax.axis_index("fsdp")
        pipe = lax.axis_index("pipe")
        self.part = 2 * (pipe % 2) + (pipe // 2) % 2
        self.far = jnp.bitwise_xor(self.f, 2)
        self.who = {"c": flip("fsdp", 0), "y": flip("fsdp", 1), "x": flip("pipe", 0), "z": flip("pipe", 1)}
        self.rows, self.width = shards[1].shape[1:]
        self.chunks = [(l, kind) for l in range(layers) for kind in range(3)]
        self.direct = {n: (None, 1, 0)[n % 3] for n in range(len(self.chunks))}
        self.ids, self.began, self.arrived = {}, [], set()

    def at(self, ref, k, layer, row, nrows, col, ncols, quarter):
        base = 0 if quarter is None else pl.multiple_of(quarter * self.shards[k].shape[1], 8)
        return ref.at[layer, pl.ds(pl.multiple_of(base + row, 8), nrows), pl.ds(col, ncols)]

    def place(self, w, l):
        n = self.shards[w].shape[1]
        return self.full[w].at[l, pl.ds(pl.multiple_of(self.f * n, 8), n)]

    def regions(self, n, ab, k):
        kind = self.chunks[n][1]
        d, piece, half = self.width, self.rows // 4, self.rows // 2
        if kind == 0:
            if ab == 0:
                return [(0, piece * k, piece, 0, 2 * d)]
            return [(0, piece * k, piece, 2 * d, d), (1, piece * k, piece, 0, d)]
        row = (kind - 1) * half
        if ab == 0:
            return [(2, row, half, pl.multiple_of(k * d, LANES), d)]
        return [(3, k * self.rows + row, half, 0, d)]

    def copies(self, key):
        kind = key[0]
        if kind == "own":
            _, l, w = key
            pairs, who = [(self.shards[w].at[l], self.place(w, l))], "c"
        elif kind == "small":
            who = key[1]
            row = self.far if key[2] else self.f
            pairs = [(self.every.at[row], self.every.at[row])]
        else:
            _, n, ab, j = key
            l = self.chunks[n][0]
            k = jnp.bitwise_xor(self.part, j)
            who = kind
            pairs = []
            for w, row, nr, col, nc in self.regions(n, ab, k):
                if kind == "y":
                    src = self.at(self.shards[w], w, l, row, nr, col, nc, None)
                    dst = self.at(self.full[w], w, l, row, nr, col, nc, self.f)
                else:
                    src = dst = self.at(self.full[w], w, l, row, nr, col, nc, self.far)
                pairs.append((src, dst))
        out = []
        for m, (src, dst) in enumerate(pairs):
            sem = self.ids.setdefault((key, m), len(self.ids))
            out.append(pltpu.make_async_remote_copy(
                src_ref=src, dst_ref=dst, send_sem=self.send_sem.at[sem], recv_sem=self.recv_sem.at[sem],
                device_id=self.who[who], device_id_type=MESH))
        return out

    def start(self, *key):
        for c in self.copies(key):
            c.start()
        self.began.append(key)

    def landed(self, *key):
        if key not in self.arrived:
            for c in self.copies(key):
                c.wait_recv()
            self.arrived.add(key)

    def tick(self, t):
        count = len(self.chunks)
        if t < count:
            for ab in (0, 1):
                self.start("y", t, ab, 0)
            if self.direct[t] is not None:
                self.start("y", t, self.direct[t], 3)
        n = t - 3
        if 0 <= n < count:
            self.landed("x", n, 1, 0)
            self.landed("z", n, 0, 0)
            self.start("c", n, 1, 2)
            self.start("c", n, 0, 1)
            for ab, link in ((0, "z"), (1, "x")):
                if self.direct[n] != ab:
                    self.landed(link, n, ab, 2 if ab == 0 else 1)
                    self.start("c", n, ab, 3)
        n = t - 2
        if 0 <= n < count:
            self.landed("x", n, 0, 0)
            self.landed("z", n, 1, 0)
            if self.direct[n] != 0:
                self.start("z", n, 0, 2)
            if self.direct[n] != 1:
                self.start("x", n, 1, 1)
            if self.direct[n] is not None:
                self.landed("y", n, self.direct[n], 3)
                self.start("c", n, self.direct[n], 3)
            self.start("c", n, 0, 2)
            self.start("c", n, 1, 1)
        n = t - 1
        if 0 <= n < count:
            for ab in (0, 1):
                self.landed("y", n, ab, 0)
            for ab in (0, 1):
                self.start("x", n, ab, 0)
                self.start("z", n, ab, 0)
            for ab in (0, 1):
                self.start("c", n, ab, 0)

    def ready(self, n):
        for ab in (0, 1):
            for j in range(4):
                self.landed("c", n, ab, j)

    def drain(self):
        for key in self.began:
            for c in self.copies(key):
                c.wait_send()


def fore_kernel(layers, items, frames, subnet, *rest):
    smalls, (x_any, *shards) = rest[:8], rest[8:13]
    outs = rest[13:]
    full, (vec, ub, x1_o, out_o) = outs[:4], outs[4:8]
    kept = [outs[8 + 8 * l:16 + 8 * l] for l in range(layers)]
    scratch = outs[8 + 8 * layers:]
    every, own, (send_sem, recv_sem, local_sem) = scratch[0], scratch[1:5], scratch[5:8]
    w, x, qkv, pt, ob, r1, w_up, w_down, n1b, g, gp, acc = scratch[8:20]
    asem, fsem, xsem = scratch[20:23], scratch[23:26], scratch[26]
    width = x.shape[1]
    tab = Table(subnet, items, width)
    gat = Gather(layers, shards, full, every, send_sem, recv_sem)
    order = [(k, l) for l in range(layers) for k in range(4)]
    loads = [pltpu.make_async_copy(shards[k].at[l], own[k].at[l], local_sem.at[0, k, l]) for k, l in order]
    stores = [pltpu.make_async_copy(own[k].at[l], gat.place(k, l), local_sem.at[1, k, l]) for k, l in order]
    load_x = fetch(x_any, x, xsem.at[0])
    for c in loads:
        c.start()
    every[gat.f] = jnp.zeros(every.shape[1:], F32)
    for k, ref in enumerate(smalls):
        for l in range(layers):
            every[gat.f, l, k:k + 1, 0:ref.shape[1]] = ref[l:l + 1, :].astype(F32)
    greet(list(gat.who.values()))
    gat.start("small", "y", 0)
    gat.start("small", "c", 0)
    gat.tick(0)
    for c, d in zip(loads, stores):
        c.wait()
        d.start()
    gat.landed("small", "y", 0)
    gat.start("small", "c", 1)
    for k in range(4):
        gat.start("own", 0, k)
    load_x.wait()
    mask_rows(x, items, frames, tab)
    for t in (1, 2, 3):
        gat.tick(t)
    gat.landed("small", "c", 0)
    gat.landed("small", "c", 1)
    rows = gat.rows
    for q in range(4):
        for l in range(layers):
            vec[l, 0:7, q * rows:(q + 1) * rows] = every[q, l, 0:7, 0:rows]
            ub[l, :, q * width:(q + 1) * width] = every[q, l, 7:8, :]
    for c in stores:
        c.wait()
    for l in range(1, layers):
        for k in range(4):
            gat.start("own", l, k)

    last_tick = len(gat.chunks) + 2
    state = [4]

    def tick_to(t):
        while state[0] <= min(t, last_tick):
            gat.tick(state[0])
            state[0] += 1

    def hook_for(t):
        def hook():
            gat.tick(t)
        return hook

    def reserve():
        if state[0] > last_tick:
            return {}
        t = state[0]
        state[0] += 1
        return {3: hook_for(t)}

    pending = None
    for l in range(layers):
        tick_to(3 * l + 3)
        for k in (0, 1):
            gat.landed("own", l, k)
        gat.ready(3 * l)
        if pending is not None:
            pending[0]()
        hooks = reserve()
        end_a = attn_front(
            l, items, frames, tab, vec, (w, x, qkv, pt, ob, r1), full[:2], asem, kept[l][:4], hooks)
        tick_to(3 * l + 5)
        for k in (2, 3):
            gat.landed("own", l, k)
        gat.ready(3 * l + 1)
        gat.ready(3 * l + 2)
        if pending is not None:
            pending[1]()
        last = l == layers - 1
        hooks = reserve()
        end_f = ffn_front(
            l, last, items, frames, tab, vec, ub, (w_up, w_down, r1, x, n1b, g, gp, acc), full[2:], fsem,
            (*kept[l][4:], out_o if last else x1_o), hooks)
        pending = (end_a, end_f)
    pending[0]()
    pending[1]()
    gat.drain()


def fore(subnet, smalls, x, weights):
    layers = weights[0].shape[0]
    items, t, d = x.shape
    n = items * t
    ff = weights[2].shape[2]
    vm, dma = pltpu.VMEM, pltpu.SemaphoreType.DMA
    keep = [sds((3, n, d), BF), sds((items, HEADS, t, t), BF), sds((n, d), BF), sds((n, d), F32), sds((n, d), BF),
            sds((n, ff), BF), sds((n, ff), BF), sds((n, d), F32)]
    outs = [sds((layers, 4 * w.shape[1], w.shape[2]), BF) for w in weights] + [
        sds((layers, 8, d), F32), sds((layers, 1, ff), F32), sds((n, d), BF), sds((n, d), BF)] + keep * layers
    square = vm((n, d), BF)
    res = pl.pallas_call(
        functools.partial(fore_kernel, layers, items, t),
        out_shape=tuple(outs),
        in_specs=[SM] + [VM] * 8 + [ANY] * 5,
        out_specs=tuple(VM if k in (4, 5) else ANY for k in range(len(outs))),
        scratch_shapes=[
            vm((4, layers, 8, d), F32), *[vm(w.shape, BF) for w in weights], dma((200,)), dma((200,)), dma((2, 4, layers)),
            vm((4, d, d), BF), square, vm((3, n, d), BF), vm((items, HEADS, t, t), BF), square, vm((n, d), F32),
            vm((d, ff), BF), vm((ff, d), BF), square, vm((n, ff), BF), vm((n, ff), BF), vm((n, d), F32),
            dma((4,)), dma((5,)), dma((d // LANES,)), dma((ff // d, 2)), dma((3,)), dma((2, ff // UNIT_CHUNK)), dma((1,)),
        ],
        compiler_params=pltpu.CompilerParams(collective_id=0, has_side_effects=True, vmem_limit_bytes=60 * 2 ** 20),
        name="fore",
    )(subnet, *smalls, x.reshape(n, d), *weights)
    return res[:4], res[4], res[5], res[6], res[7], [res[8 + 8 * l:16 + 8 * l] for l in range(layers)]


class Reduce:
    LOC, RECV = 6, 4

    def __init__(self, count, bits, g, out, refs):
        self.count, self.bits, self.g, self.out = count, bits, g, out
        self.loc, self.rc, self.ry, self.rx, self.rz, self.fin, self.ss, self.rs, self.ls, self.os = refs
        f, pipe = lax.axis_index("fsdp"), lax.axis_index("pipe")
        self.c, self.y, x, z = f % 2, f // 2, pipe % 2, (pipe // 2) % 2
        rows = g.shape[3]
        half, quarter = rows // 2, rows // 4
        self.who = [flip("fsdp", 0), flip("fsdp", 1)] + [flip("pipe", b) for b in range(bits)]
        part = lambda at, n: pl.ds(pl.multiple_of(at, 16), n)
        self.my_half, self.their_half = part(x * half, half), part((1 - x) * half, half)
        self.mine, self.theirs = part(x * half + z * quarter, quarter), part(x * half + (1 - z) * quarter, quarter)
        self.n_red = 2 + bits
        self.total = self.n_red + 2
        self.slots = self.fin.shape[0]

    @staticmethod
    def scratch(bits, count, rows, d):
        vm, dma = pltpu.VMEM, pltpu.SemaphoreType.DMA
        n = bits + 4
        return [
            vm((Reduce.LOC, 2, rows, d), BF), vm((Reduce.RECV, 2, rows, d), BF), vm((Reduce.RECV, rows, d), BF),
            vm((Reduce.RECV, rows // 2, d), BF), vm((bits - 1, Reduce.RECV, rows // 4, d), BF), vm((n + 2, rows, d), BF),
            dma((n, count)), dma((n, count)), dma((count,)), dma((count,)),
        ]

    def load(self, p):
        return pltpu.make_async_copy(self.g.at[:, p, self.c], self.loc.at[p % self.LOC], self.ls.at[p])

    def store(self, p):
        return pltpu.make_async_copy(self.fin.at[p % self.slots], self.out.at[p], self.os.at[p])

    def move(self, k, p):
        loc, fin, r = self.loc.at[p % self.LOC], self.fin.at[p % self.slots], p % self.RECV
        if k == 0:
            src, dst, who = self.g.at[:, p, 1 - self.c], self.rc.at[r], 0
        elif k == 1:
            src, dst, who = loc.at[1 - self.y], self.ry.at[r], 1
        elif k == 2:
            src, dst, who = loc.at[self.y, self.their_half], self.rx.at[r], 2
        elif k == 3:
            src, dst, who = loc.at[self.y, self.theirs], self.rz.at[0, r], 3
        elif k < self.n_red:
            src, dst, who = fin.at[self.mine], self.rz.at[k - 3, r], k
        elif k == self.n_red:
            src, dst, who = fin.at[self.mine], fin.at[self.mine], 3
        else:
            src, dst, who = fin.at[self.my_half], fin.at[self.my_half], 2
        return pltpu.make_async_remote_copy(
            src_ref=src, dst_ref=dst, send_sem=self.ss.at[k, p], recv_sem=self.rs.at[k, p], device_id=self.who[who],
            device_id_type=MESH)

    def arrive(self, k, p):
        self.move(k, p).wait()
        s, f, r = p % self.LOC, p % self.slots, p % self.RECV
        if k == 0:
            self.load(p).wait()
            self.loc[s] = add_low(self.loc[s], self.rc[r])
        elif k == 1:
            self.loc[s, self.y] = add_low(self.loc[s, self.y], self.ry[r])
        elif k == 2:
            self.loc[s, self.y, self.my_half] = add_low(self.loc[s, self.y, self.my_half], self.rx[r])
        elif k == 3:
            self.fin[f, self.mine] = add_low(self.loc[s, self.y, self.mine], self.rz[0, r])
        elif k < self.n_red:
            self.fin[f, self.mine] = add_low(self.fin[f, self.mine], self.rz[k - 3, r])

    def begin(self):
        self.move(0, 0).start()
        self.load(0).start()

    def tick(self, t):
        @pl.when(t + 1 < self.count)
        def _():
            self.move(0, t + 1).start()
            self.load(t + 1).start()

        for k in range(self.total):
            p = t - k

            @pl.when(jnp.logical_and(p >= 0, p < self.count))
            def _(k=k, p=p):
                self.arrive(k, p)
                if k + 1 < self.total:
                    self.move(k + 1, p).start()
                else:
                    self.store(p).start()

        p = t - self.total

        @pl.when(jnp.logical_and(p >= 0, p < self.count))
        def _():
            self.store(p).wait()

    def ticks(self):
        return self.count + self.total


def add_low(a, b):
    return (a.astype(F32) + b.astype(F32)).astype(BF)


class SumAll:
    def __init__(self, who, total, recv, ss, rs):
        self.who, self.total, self.recv, self.ss, self.rs = who, total, recv, ss, rs

    def move(self, k):
        return pltpu.make_async_remote_copy(
            src_ref=self.total, dst_ref=self.recv.at[k], send_sem=self.ss.at[k], recv_sem=self.rs.at[k],
            device_id=self.who[k], device_id_type=MESH)

    def step(self, k):
        for j in range(len(self.who) + 1):
            @pl.when(k == j)
            def _(j=j):
                if j > 0:
                    self.move(j - 1).wait()
                    self.total[...] = self.total[...] + self.recv[j - 1]
                if j < len(self.who):
                    self.move(j).start()


def attn_back(layer, items, frames, tab, src, buf, weights, sems, first, grads, tick, t0, dx_out):
    qkv_any, pt_any, x_any, ob_any = src
    w, da, dr1, qkv, pt, x, ob, do, dqkv, dx, stage = buf
    wsem, sem, ptsem, qsem = sems
    width = da.shape[1]
    npair = width // LANES
    ring = pt.shape[0]
    p = Attn(layer, weights, w, wsem)
    p.start((3, 0, 1, 2))

    def block(ref, j):
        return ref.at[:, pl.ds(pl.multiple_of(j * width, LANES), width)]

    loads = [fetch(qkv_any.at[j], block(qkv, j), sem.at[3 + j]) for j in range(3)]

    def load_pt(c):
        return pltpu.make_async_copy(pt_any.at[:, pl.ds(2 * c, 2)], pt.at[c % ring], ptsem.at[c])

    for c in range(ring - 1):
        load_pt(c).start()
    later = [fetch(ob_any, ob, sem.at[0]), fetch(x_any, x, sem.at[1])]
    p.wait(3)
    dos = [dot_nt(da[rows_of(i, frames), :], w[3]) for i in range(items)]
    for i, d in enumerate(dos):
        do[rows_of(i, frames), :] = d.astype(BF)
    for o in loads:
        o.wait()
    scale = HEAD_DIM ** -0.5
    qsums = []

    def pair(c, _):
        @pl.when(c % 3 == 0)
        def _():
            tick(t0 + c // 3)

        lanes = pl.ds(pl.multiple_of(c * LANES, LANES), LANES)
        ids = lax.broadcasted_iota(jnp.int32, (1, LANES), 1) + c * LANES
        load_pt(c).wait()

        @pl.when(c + ring - 1 < npair)
        def _():
            load_pt(c + ring - 1).start()

        rr = [rows_of(i, frames) for i in range(items)]
        at = [pl.ds(pl.multiple_of(j * width + c * LANES, LANES), LANES) for j in range(3)]
        q = [qkv[r, at[0]] for r in rr]
        k = [qkv[r, at[1]] for r in rr]
        v = [qkv[r, at[2]] for r in rr]
        dob = [do[r, lanes] for r in rr]
        kt = [a.T for a in k]
        heads = [(n, h) for n in range(items) for h in (0, 1)]
        pbs = [pt[c % ring, n, h] for n, h in heads]
        dps = [dot_nt(only(h, v[n]), dob[n]) for n, h in heads]
        dvs = [dot_nn(pb, dob[n]) for pb, (n, h) in zip(pbs, heads)]
        tmps = [pb.astype(F32) * dp for pb, dp in zip(pbs, dps)]
        dss = [(t - pb.astype(F32) * jnp.sum(t, axis=0, keepdims=True)).astype(BF) for t, pb in zip(tmps, pbs)]
        dks = [dot_nn(ds, q[n]) for ds, (n, h) in zip(dss, heads)]
        dqs = [dot_nn(kt[n][h * HEAD_DIM:(h + 1) * HEAD_DIM], ds) for ds, (n, h) in zip(dss, heads)]
        for n in range(items):
            on = ids < tab.a[n]
            put = lambda v, s: jnp.where(on, v * s, 0.0).astype(BF)
            dqkv[rr[n], at[0]] = put(jnp.concatenate(dqs[2 * n:2 * n + 2], axis=0).T, scale)
            dqkv[rr[n], at[1]] = put(jnp.where(half_mask(0), dks[2 * n], dks[2 * n + 1]), scale)
            dqkv[rr[n], at[2]] = put(jnp.where(half_mask(0), dvs[2 * n], dvs[2 * n + 1]), 1.0)
        return 0

    lax.fori_loop(0, npair, pair, 0)
    t0 = t0 + (npair + 2) // 3
    tick(t0)
    q_sum = jnp.sum(dqkv[:, 0:width].astype(F32), axis=0, keepdims=True)
    for o in later:
        o.wait()
    if layer == 0:
        mask_rows(x, items, frames, tab)
    quarters = Quarters(stage, grads, qsem, first)
    rows = stage.shape[3]

    def step(lhs, rhs, b):
        for y in (0, 1):
            res = dot_tn(lhs[:, y * 2 * rows:(y + 1) * 2 * rows], rhs).astype(BF)
            for t in (0, 1):
                stage[y, b, t] = res[t * rows:(t + 1) * rows]
            quarters.start(y, b)

    def in_step(j, _):
        step(x, block(dqkv, j)[...], j)
        return 0

    lax.fori_loop(0, 3, in_step, 0)
    tick(t0 + 1)
    step(ob, da[...], 3)
    for j in range(3):
        p.wait(j)

    def back_step(j, _):
        adds = [dot_nt(block(dqkv, j)[rows_of(i, frames), :], w[j]) for i in range(items)]
        for i, add in enumerate(adds):
            dr1[rows_of(i, frames), :] += add
        return 0

    lax.fori_loop(0, 3, back_step, 0)
    for i in range(items):
        rr = rows_of(i, frames)
        dx[rr, :] = (dr1[rr, :] * lane_mask(width, tab.w[i])).astype(BF)
    if dx_out is not None:
        fetch(dx, dx_out, sem.at[2])
    quarters.wait()
    tick(t0 + 2)
    return t0 + 3, q_sum


def ffn_back(layer, items, frames, tab, vec, src, buf, weights, sems, first, grads, tick, t0, sums):
    cot_any, r2_any, r1_any, gp_any, g_any, n1b_any = src
    w_up, w_down, cot, dxn, r, du, g, n1b, df, acc, da, stage = buf
    wsem, sem, gsem, qsem = sems
    width, units = w_up.shape
    nblk, nch = units // width, units // UNIT_CHUNK
    p = Ffn(layer, weights, w_up, w_down, wsem)
    p.start()
    loads = [fetch(r2_any, r, sem.at[0]), fetch(cot_any, cot, sem.at[1])]

    def load_gp(c):
        cols = pl.ds(pl.multiple_of(c * UNIT_CHUNK, UNIT_CHUNK), UNIT_CHUNK)
        return pltpu.make_async_copy(gp_any.at[:, cols], du.at[:, cols], gsem.at[c])

    for c in range(nch):
        load_gp(c).start()
    later = [fetch(n1b_any, n1b, sem.at[3]), fetch(g_any, g, sem.at[4])]
    for o in loads:
        o.wait()
    for i in range(items):
        rr = rows_of(i, frames)
        cm = lane_mask(width, tab.w[i])
        dy = jnp.where(tab.skip[i] == 1, cot[rr, :], dxn[rr, :]).astype(F32)
        xhat, rstd = normed(r[rr, :], cm, tab.inv[i])
        dr2, dg, ds = norm_back(dy, xhat, rstd, vec[layer, ROW_G2:ROW_G2 + 1, :], cm, tab.inv[i])
        dfb = dr2.astype(BF)
        df[rr, :] = dfb
        acc[rr, :] = dr2
        sums[ROW_G2:ROW_G2 + 1, 0:width] += dg
        sums[ROW_B2:ROW_B2 + 1, 0:width] += ds
        sums[ROW_DB:ROW_DB + 1, 0:width] += jnp.sum(dfb.astype(F32), axis=0, keepdims=True)
    load_r1 = fetch(r1_any, r, sem.at[2])
    tick(t0)

    def chunk(c):
        p.before(c)
        load_gp(c).wait()
        cols = pl.ds(pl.multiple_of(c * UNIT_CHUNK, UNIT_CHUNK), UNIT_CHUNK)
        dgs = [dot_nt(df[rows_of(i, frames), :], w_down[cols, :]) for i in range(items)]
        dubs = []
        for i, dg in enumerate(dgs):
            dub = (dg * du[rows_of(i, frames), cols].astype(F32)).astype(BF)
            du[rows_of(i, frames), cols] = dub
            sums[ROW_UB:ROW_UB + 1, cols] += jnp.sum(dub.astype(F32), axis=0, keepdims=True)
            dubs.append(dub)
        for i, dub in enumerate(dubs):
            acc[rows_of(i, frames), :] += dot_nt(dub, w_up[:, cols])

    def one(c, _):
        @pl.when(jnp.logical_and(c % 3 == 0, c > 0))
        def _():
            tick(t0 + c // 3)

        chunk(c)
        return 0

    lax.fori_loop(0, nch, one, 0)
    t0 = t0 + (nch + 2) // 3
    tick(t0)
    for o in later:
        o.wait()
    rows = stage.shape[3]
    down = Quarters(stage, grads, qsem.at[0], first)
    up = Quarters(stage, grads, qsem.at[1], first + nblk)

    def down_step(f, _):
        y, par = f // 2, f % 2
        for s in range(nblk // 2):
            lanes = pl.ds(pl.multiple_of(f * width + s * 2 * rows, LANES), 2 * rows)
            res = dot_tn(g[:, lanes], df[...]).astype(BF)
            for t in (0, 1):
                stage[y, 2 * s + t, par] = res[t * rows:(t + 1) * rows]
        return 0

    lax.fori_loop(0, 4, down_step, 0)
    for y in (0, 1):
        for b in range(nblk):
            down.start(y, b)
    tick(t0 + 1)
    load_r1.wait()
    for i in range(items):
        rr = rows_of(i, frames)
        cm = lane_mask(width, tab.w[i])
        xhat, rstd = normed(r[rr, :], cm, tab.inv[i])
        d1, dg, ds = norm_back(acc[rr, :], xhat, rstd, vec[layer, ROW_G1:ROW_G1 + 1, :], cm, tab.inv[i])
        acc[rr, :] = d1
        dab = d1.astype(BF)
        da[rr, :] = dab
        sums[ROW_G1:ROW_G1 + 1, 0:width] += dg
        sums[ROW_B1:ROW_B1 + 1, 0:width] += ds
        sums[ROW_OB:ROW_OB + 1, 0:width] += jnp.sum(dab.astype(F32), axis=0, keepdims=True)
    down.wait()
    tick(t0 + 2)

    def up_step(j, _):
        cols = pl.ds(pl.multiple_of(j * width, LANES), width)
        for y in (0, 1):
            res = dot_tn(n1b[:, y * 2 * rows:(y + 1) * 2 * rows], du[:, cols]).astype(BF)
            for t in (0, 1):
                stage[y, j, t] = res[t * rows:(t + 1) * rows]
            up.start(y, j)
        return 0

    lax.fori_loop(0, nblk, up_step, 0)
    up.wait()
    tick(t0 + 3)
    return t0 + 4


def back_kernel(items, frames, bits, blocks, subnet, vec, s_top, da_any, dr1_any, cot_any, *rest):
    top, bottom, mid, weights = rest[:4], rest[4:8], rest[8:13], rest[13:17]
    (dx_o, grads, out, total, w_up, w, da, dr1, pt, x, ob, do, dx, r, du, g, stage, srecv) = rest[18:36]
    asem, bsem, fsem = rest[36:40], rest[40:44], rest[44:48]
    red = Reduce(2 * blocks, bits, grads, out, rest[48:58])
    s_send, s_recv, isem = rest[58:]
    width = da.shape[1]
    tab = Table(subnet, items, width)
    loads = [fetch(da_any, da, isem.at[0]), fetch(dr1_any, dr1, isem.at[1])]
    greet(red.who)
    red.begin()
    total[1] = s_top[...]
    total[0] = jnp.zeros(total.shape[1:], F32)
    nb = w_up.shape[1] // width
    w_att, w_ffn = weights[:2], weights[2:]
    for o in loads:
        o.wait()
    buf = (w, da, dr1, du, pt, x, ob, do, g, dx, stage)
    t, q_sum = attn_back(1, items, frames, tab, top, buf, w_att, asem, 2 * nb, grads, red.tick, 0, None)
    total[1, ROW_QB:ROW_QB + 1, 0:width] = q_sum
    w_down = w.reshape(nb * width, width)
    buf_f = (w_up, w_down, x, dx, r, du, g, ob, do, dr1, da, stage)
    t = ffn_back(0, items, frames, tab, vec, (cot_any,) + tuple(mid), buf_f, w_ffn, fsem, blocks, grads, red.tick, t, total.at[0])
    t, q_sum = attn_back(0, items, frames, tab, bottom, buf, w_att, bsem, blocks + 2 * nb, grads, red.tick, t, dx_o)
    total[0, ROW_QB:ROW_QB + 1, 0:width] = q_sum
    small = SumAll(red.who, total, srecv, s_send, s_recv)

    def rest_of(n, _):
        red.tick(n)
        small.step(n - t)
        return 0

    lax.fori_loop(t, red.ticks(), rest_of, 0)
    pltpu.make_async_copy(dx, dx_o, bsem[1].at[2]).wait()


def back(subnet, vec, s_top, da, dr1, cot, top, bottom, mid, weights, grads, items):
    bits = 0
    while (1 << bits) < lax.axis_size("pipe"):
        bits += 1
    n, d = cot.shape
    ff = mid[2].shape[1]
    t = n // items
    rows, nb = d // 4, ff // d
    blocks = 2 * nb + 4
    small = (2,) + s_top.shape
    vm, dma = pltpu.VMEM, pltpu.SemaphoreType.DMA
    square = vm((n, d), BF)
    hbm = (da, dr1, cot, *top, *bottom, *mid, *weights, grads)
    asems = [dma((4,)), dma((6,)), dma((d // LANES,)), dma((2, 4))]
    return pl.pallas_call(
        functools.partial(back_kernel, items, t, bits, blocks),
        out_shape=(sds((n, d), BF), sds(grads.shape, BF), sds((2 * blocks, rows, d), BF), sds(small, F32)),
        in_specs=[SM, VM, VM] + [ANY] * len(hbm),
        out_specs=(ANY, ANY, ANY, VM),
        scratch_shapes=[
            vm((d, ff), BF), vm((4, d, d), BF), square, vm((n, d), F32), vm((3, items, 2, t, t), BF),
            square, square, square, square, vm((n, d), F32), vm((n, ff), BF), vm((n, ff), BF),
            vm((2, 4, 2, rows, d), BF), vm((2 + bits,) + small, F32),
            *asems, *asems, dma((nb, 2)), dma((5,)), dma((ff // UNIT_CHUNK,)), dma((2, 2, nb)),
            *Reduce.scratch(bits, 2 * blocks, rows, d), dma((2 + bits,)), dma((2 + bits,)), dma((2,)),
        ],
        input_output_aliases={2 + len(hbm): 1},
        compiler_params=pltpu.CompilerParams(collective_id=1, has_side_effects=True, vmem_limit_bytes=60 * 2 ** 20),
        name="back",
    )(subnet, vec, s_top, *hbm)


def finish_kernel(layers, red, total, g_in, g_out, g_up, g_down, *rest):
    vecs, (bf, f32, sem_in, sem_out) = rest[:8], rest[8:]
    f = lax.axis_index("fsdp")
    blocks = bf.shape[0]
    rows, d = bf.shape[1:]
    per = blocks // layers
    nb = (per - 4) // 2

    def target(l, k):
        if k < nb:
            return g_down.at[l, pl.ds(k * rows, rows)]
        if k < 2 * nb:
            return g_up.at[l, :, pl.ds((k - nb) * d, d)]
        if k < 2 * nb + 3:
            return g_in.at[l, :, pl.ds((k - 2 * nb) * d, d)]
        return g_out.at[l]

    loads = [pltpu.make_async_copy(red.at[p], bf.at[p], sem_in.at[p]) for p in range(blocks)]
    stores = [pltpu.make_async_copy(f32.at[p], target(layers - 1 - p // per, p % per), sem_out.at[p]) for p in range(blocks)]
    for c in loads:
        c.start()
    for q in range(4):
        @pl.when(f == q)
        def _(q=q):
            for l in range(layers):
                for k in range(7):
                    vecs[k][l:l + 1, :] = total[l, k:k + 1, q * rows:(q + 1) * rows]
                vecs[7][l:l + 1, :] = total[l, 7:8, q * d:(q + 1) * d]
    for p in range(blocks):
        loads[p].wait()
        f32[p] = bf[p].astype(F32)
        stores[p].start()
    for c in stores:
        c.wait()


def finish(red, total):
    blocks, rows, d = red.shape
    layers = total.shape[0]
    nb = (blocks // layers - 4) // 2
    return pl.pallas_call(
        functools.partial(finish_kernel, layers),
        out_shape=(sds((layers, rows, 3 * d), F32), sds((layers, rows, d), F32), sds((layers, rows, nb * d), F32),
                   sds((layers, nb * rows, d), F32)) + (sds((layers, rows), F32),) * 7 + (sds((layers, d), F32),),
        in_specs=[ANY, VM],
        out_specs=(ANY,) * 4 + (VM,) * 8,
        scratch_shapes=[pltpu.VMEM(red.shape, BF), pltpu.VMEM(red.shape, F32), pltpu.SemaphoreType.DMA((blocks,)),
                        pltpu.SemaphoreType.DMA((blocks,))],
        compiler_params=pltpu.CompilerParams(**PARAMS),
        name="finish",
    )(red, total)


def local(
    frames_in, attn_in, q_bias, attn_out, out_bias, norm1_gain, norm1_bias, ffn_up, up_bias, ffn_down, down_bias,
    norm2_gain, norm2_bias, subnet, out_cotangent,
):
    items, frames, width = frames_in.shape
    ff = ffn_up.shape[2]
    layers = attn_in.shape[0]
    nb = ff // width
    smalls = (q_bias, out_bias, norm1_gain, norm1_bias, down_bias, norm2_gain, norm2_bias, up_bias)
    n = items * frames
    weights, vec, ub, x1, layer_out, kept = fore(subnet, smalls, frames_in, (attn_in, attn_out, ffn_up, ffn_down))
    layer_out = layer_out.reshape(frames_in.shape)
    cot = out_cotangent.reshape(n, width)
    qkv1, pt1, ob1, r1, n1b, g, gp, r2 = kept[1]
    da, dr1, s_top, grads = ffn_bwd(
        1, True, 0, 2 * (2 * nb + 4), subnet, cot, cot, r2, r1, gp, g, n1b, vec[1], weights[2:], None, items)
    x0 = frames_in.reshape(n, width)
    qkv0, pt0, ob0, r1, n1b, g, gp, r2 = kept[0]
    dx, _, red, total = back(
        subnet, vec, s_top, da, dr1, cot, (qkv1, pt1, x1, ob1), (qkv0, pt0, x0, ob0), (r2, r1, gp, g, n1b), weights, grads,
        items)
    dx = dx.reshape(frames_in.shape)
    g_in, g_out, g_up, g_down, g_qb, g_ob, g_g1, g_b1, g_db, g_g2, g_b2, g_ub = finish(red, total)
    return (layer_out, dx, g_in, g_qb, g_out, g_ob, g_g1, g_b1, g_up, g_ub, g_down, g_db, g_g2, g_b2)


def solution(mesh):
    rows3 = P(None, "fsdp", None)
    rows2 = P(None, "fsdp")
    item = P(("pipe", "fsdp"), None, None)
    weights = (rows3, rows2, rows3, rows2, rows2, rows2, rows3, rows2, rows3, rows2, rows2, rows2)
    return jax.shard_map(
        local, mesh=mesh, in_specs=(item,) + weights + (P(), item), out_specs=(item, item) + weights, check_vma=False,
    )
```

```python
import functools

import jax
import jax.numpy as jnp
from jax import lax
from jax.experimental import pallas as pl
from jax.experimental.pallas import tpu as pltpu
from jax.sharding import PartitionSpec as P

HEADS = 12
HEAD_DIM = 64
EPSILON = 1e-05
LANES = 128
UNIT_CHUNK = 512
BF = jnp.bfloat16
F32 = jnp.float32

ROW_QB, ROW_OB, ROW_G1, ROW_B1, ROW_DB, ROW_G2, ROW_B2, ROW_UB = 0, 1, 2, 3, 4, 5, 6, 7

def dot_nn(a, b):
    return lax.dot_general(a, b, (((1,), (0,)), ((), ())), preferred_element_type=F32)


def dot_nt(a, b):
    return lax.dot_general(a, b, (((1,), (1,)), ((), ())), preferred_element_type=F32)


def dot_tn(a, b):
    return lax.dot_general(a, b, (((0,), (0,)), ((), ())), preferred_element_type=F32)


def lane_mask(width, count):
    return (lax.broadcasted_iota(jnp.int32, (1, width), 1) < count).astype(F32)


def normed(rows, cm, inv_w):
    mean = jnp.sum(rows * cm, axis=-1, keepdims=True) * inv_w
    centered = (rows - mean) * cm
    var = jnp.sum(centered * centered, axis=-1, keepdims=True) * inv_w
    rstd = lax.rsqrt(var + EPSILON)
    return centered * rstd, rstd


def norm_back(dy, xhat, rstd, gain, cm, inv_w):
    dym = dy * cm
    dg = jnp.sum(dym * xhat, axis=0, keepdims=True)
    ds = jnp.sum(dym, axis=0, keepdims=True)
    dx = dym * gain
    m1 = jnp.sum(dx, axis=-1, keepdims=True) * inv_w
    m2 = jnp.sum(dx * xhat, axis=-1, keepdims=True) * inv_w
    return cm * (rstd * (dx - m1 - xhat * m2)), dg, ds


class Attn:
    def __init__(self, layer, refs, w, sems):
        w_in, w_out = refs
        d = w.shape[1]
        self.copies = [
            pltpu.make_async_copy(w_in.at[layer, :, pl.ds(b * d, d)], w.at[b], sems.at[b]) for b in range(3)
        ] + [pltpu.make_async_copy(w_out.at[layer], w.at[3], sems.at[3])]

    def start(self, order):
        for b in order:
            self.copies[b].start()

    def wait(self, b):
        self.copies[b].wait()


class Ffn:
    def __init__(self, layer, refs, w_up, w_down, sems):
        up, down = refs
        d = w_up.shape[0]
        self.blocks = w_up.shape[1] // d
        self.first = [b * d // UNIT_CHUNK for b in range(self.blocks)]
        self.copies = [(
            pltpu.make_async_copy(up.at[layer, :, pl.ds(b * d, d)], w_up.at[:, pl.ds(b * d, d)], sems.at[b, 0]),
            pltpu.make_async_copy(down.at[layer, pl.ds(b * d, d)], w_down.at[pl.ds(b * d, d)], sems.at[b, 1]),
        ) for b in range(self.blocks)]

    def start(self):
        for pair in self.copies:
            for copy in pair:
                copy.start()

    def wait(self, b):
        for copy in self.copies[b]:
            copy.wait()

    def before(self, c):
        for b in range(self.blocks):
            @pl.when(c == self.first[b])
            def _(b=b):
                self.wait(b)

    def drain(self, counts):
        most = jnp.maximum(counts[0], counts[1])
        for b in range(self.blocks):
            @pl.when(most <= self.first[b])
            def _(b=b):
                self.wait(b)


class Table:
    def __init__(self, subnet, items, width):
        segment = lax.axis_index("pipe") // (lax.axis_size("pipe") // 2)
        codes = [[subnet[k, segment * items + i] for k in range(4)] for i in range(items)]
        widths = [width * (4 + k) // 6 for k in range(3)]
        self.w = [width * (4 + c[0]) // 6 for c in codes]
        self.inv = [
            jnp.where(c[0] == 0, 1.0 / widths[0], jnp.where(c[0] == 1, 1.0 / widths[1], 1.0 / widths[2])) for c in codes]
        self.a = [HEAD_DIM * (HEADS * (4 + c[1]) // 6) for c in codes]
        self.u = [w * (6 + c[2]) // 2 for w, c in zip(self.w, codes)]
        self.skip = [c[3] for c in codes]
        self.pairs = [(a + LANES - 1) // LANES for a in self.a]
        self.chunks = [(u + UNIT_CHUNK - 1) // UNIT_CHUNK for u in self.u]


def fetch(src, dst, sem):
    copy = pltpu.make_async_copy(src, dst, sem)
    copy.start()
    return copy


def rows_of(i, frames):
    if isinstance(i, int):
        return pl.ds(i * frames, frames)
    return pl.ds(pl.multiple_of(i * frames, frames), frames)


def mask_rows(x, items, frames, tab):
    for i in range(items):
        rr = rows_of(i, frames)
        x[rr, :] = jnp.where(lane_mask(x.shape[1], tab.w[i]) > 0, x[rr, :], jnp.zeros((), x.dtype))


def half_mask(h):
    low = lax.broadcasted_iota(jnp.int32, (1, LANES), 1) < HEAD_DIM
    return low if h == 0 else jnp.logical_not(low)


def only(h, x):
    return jnp.where(half_mask(h), x, jnp.zeros_like(x))


def attn_front(layer, items, frames, tab, vec, buf, weights, sems, outs, hooks):
    w, x, qkv, pt, ob, r1 = buf
    wsem, sem, ptsem = sems
    qkv_o, pt_o, ob_o, r1_o = outs
    width = x.shape[1]
    npair = width // LANES
    p = Attn(layer, weights, w, wsem)
    p.start((0, 1, 2, 3))
    cms = [lane_mask(width, n) for n in tab.w]
    hms = [lane_mask(width, n) for n in tab.a]
    done = []
    for j in range(3):
        p.wait(j)
        accs = [dot_nn(x[rows_of(i, frames), :], w[j]) for i in range(items)]
        for i, acc in enumerate(accs):
            if j == 0:
                acc = acc + vec[layer, ROW_QB:ROW_QB + 1, :]
            qkv[j, rows_of(i, frames), :] = (acc * hms[i]).astype(BF)
        done.append(fetch(qkv.at[j], qkv_o.at[j], sem.at[j]))

    def store(c):
        return pltpu.make_async_copy(pt.at[:, pl.ds(2 * c, 2)], pt_o.at[:, pl.ds(2 * c, 2)], ptsem.at[c])

    def pair(c, _):
        for at, hook in hooks.items():
            @pl.when(c == at)
            def _(hook=hook):
                hook()

        lanes = pl.ds(pl.multiple_of(c * LANES, LANES), LANES)
        vts, ss = [], []
        for i in range(items):
            rr = rows_of(i, frames)
            q = qkv[0, rr, lanes] * jnp.asarray(HEAD_DIM ** -0.5, BF)
            k = qkv[1, rr, lanes]
            vts.append(qkv[2, rr, lanes].T)
            ss += [dot_nt(only(h, k), q) for h in (0, 1)]
        es = [jnp.exp(s - jnp.max(s, axis=0, keepdims=True)) for s in ss]
        pbs = [(e * (1.0 / jnp.sum(e, axis=0, keepdims=True))).astype(BF) for e in es]
        for i in range(items):
            mixed = []
            for h in (0, 1):
                pt[i, 2 * c + h] = pbs[2 * i + h]
                mixed.append(dot_nn(vts[i][h * HEAD_DIM:(h + 1) * HEAD_DIM], pbs[2 * i + h]))
            ob[rows_of(i, frames), lanes] = jnp.concatenate(mixed, axis=0).T.astype(BF)
        store(c).start()
        return 0

    lax.fori_loop(0, npair, pair, 0)
    done.append(fetch(ob, ob_o, sem.at[3]))
    p.wait(3)
    accs = [dot_nn(ob[rows_of(i, frames), :], w[3]) for i in range(items)]
    for i, acc in enumerate(accs):
        rr = rows_of(i, frames)
        r1[rr, :] = x[rr, :].astype(F32) + (acc + vec[layer, ROW_OB:ROW_OB + 1, :]) * cms[i]
    done.append(fetch(r1, r1_o, sem.at[4]))

    def finish():
        for c in range(npair):
            store(c).wait()
        for o in done:
            o.wait()

    return finish


def ffn_front(layer, last, items, frames, tab, vec, ub, buf, weights, sems, outs, hooks):
    w_up, w_down, r1, x, n1b, g, gp, acc = buf
    wsem, sem, gsem = sems
    n1b_o, g_o, gp_o, r2_o, out_o = outs
    width, units = w_up.shape
    nch = units // UNIT_CHUNK
    p = Ffn(layer, weights, w_up, w_down, wsem)
    p.start()
    cms = [lane_mask(width, n) for n in tab.w]
    for i in range(items):
        rr = rows_of(i, frames)
        xhat, _ = normed(r1[rr, :], cms[i], tab.inv[i])
        n1 = (xhat * vec[layer, ROW_G1:ROW_G1 + 1, :] + vec[layer, ROW_B1:ROW_B1 + 1, :]) * cms[i]
        n1b[rr, :] = n1.astype(BF)
        acc[rr, :] = n1 + vec[layer, ROW_DB:ROW_DB + 1, :] * cms[i]
    done = [fetch(n1b, n1b_o, sem.at[0])]

    def store(k, c):
        cols = pl.ds(pl.multiple_of(c * UNIT_CHUNK, UNIT_CHUNK), UNIT_CHUNK)
        ref, out = ((g, g_o), (gp, gp_o))[k]
        return pltpu.make_async_copy(ref.at[:, cols], out.at[:, cols], gsem.at[k, c])

    def chunk(c, _):
        for at, hook in hooks.items():
            @pl.when(c == at)
            def _(hook=hook):
                hook()

        p.before(c)
        cols = pl.ds(pl.multiple_of(c * UNIT_CHUNK, UNIT_CHUNK), UNIT_CHUNK)
        ids = lax.broadcasted_iota(jnp.int32, (1, UNIT_CHUNK), 1) + c * UNIT_CHUNK
        us = [dot_nn(n1b[rows_of(i, frames), :], w_up[:, cols]) for i in range(items)]
        gbs = []
        for i, u in enumerate(us):
            fm = (ids < tab.u[i]).astype(F32)
            u = (u + ub[layer, 0:1, cols]) * fm
            half = 0.5 * (1.0 + lax.erf(u * (0.5 ** 0.5)))
            gb = (u * half).astype(BF)
            g[rows_of(i, frames), cols] = gb
            gp[rows_of(i, frames), cols] = ((half + u * (jnp.exp(u * u * -0.5) * 0.3989422804014327)) * fm).astype(BF)
            gbs.append(gb)
        for i, gb in enumerate(gbs):
            acc[rows_of(i, frames), :] += dot_nn(gb, w_down[cols, :]) * cms[i]
        for k in (0, 1):
            store(k, c).start()
        return 0

    lax.fori_loop(0, nch, chunk, 0)
    done.append(fetch(acc, r2_o, sem.at[1]))
    for i in range(items):
        rr = rows_of(i, frames)
        xhat, _ = normed(acc[rr, :], cms[i], tab.inv[i])
        y = ((xhat * vec[layer, ROW_G2:ROW_G2 + 1, :] + vec[layer, ROW_B2:ROW_B2 + 1, :]) * cms[i]).astype(BF)
        if last:
            y = jnp.where(tab.skip[i] == 1, x[rr, :], y)
        x[rr, :] = y
    done.append(fetch(x, out_o, sem.at[2]))

    def finish():
        for c in range(nch):
            for k in (0, 1):
                store(k, c).wait()
        for o in done:
            o.wait()

    return finish


class Quarters:
    def __init__(self, stage, out, sems, first):
        self.stage, self.out, self.sems, self.first = stage, out, sems, first

    def copy(self, y, b):
        return pltpu.make_async_copy(self.stage.at[y, b], self.out.at[y, self.first + b], self.sems.at[y, b])

    def start(self, y, b):
        self.copy(y, b).start()

    def wait_block(self, b):
        for y in range(self.stage.shape[0]):
            self.copy(y, b).wait()

    def wait(self):
        for b in range(self.stage.shape[1]):
            self.wait_block(b)


ANY = pl.BlockSpec(memory_space=pl.ANY)
VM = pl.BlockSpec(memory_space=pltpu.VMEM)
SM = pl.BlockSpec(memory_space=pltpu.SMEM)
PARAMS = dict(vmem_limit_bytes=58 * 2 ** 20)


def cost(flops, nbytes):
    return pl.CostEstimate(flops=int(flops), bytes_accessed=int(nbytes), transcendentals=0)


def sds(shape, dtype):
    return jax.ShapeDtypeStruct(shape, dtype)


MESH = pl.DeviceIdType.MESH


def flip(axis, bit):
    return {axis: jnp.bitwise_xor(lax.axis_index(axis), 1 << bit)}


def greet(partners):
    barrier = pltpu.get_barrier_semaphore()
    for who in partners:
        pl.semaphore_signal(barrier, inc=1, device_id=who, device_id_type=MESH)
    return lambda: pl.semaphore_wait(barrier, len(partners))


class Gather:
    def __init__(self, layers, shards, full, every, send_sem, recv_sem):
        self.layers, self.shards, self.full, self.every = layers, shards, full, every
        self.send_sem, self.recv_sem = send_sem, recv_sem
        self.f = lax.axis_index("fsdp")
        pipe = lax.axis_index("pipe")
        self.part = 2 * (pipe % 2) + (pipe // 2) % 2
        self.far = jnp.bitwise_xor(self.f, 2)
        self.who = {"c": flip("fsdp", 0), "y": flip("fsdp", 1), "x": flip("pipe", 0), "z": flip("pipe", 1)}
        self.rows, self.width = shards[1].shape[1:]
        piece, half = self.rows // 4, self.rows // 2
        self.chunks = []
        for l in range(layers):
            if l == 0:
                self.chunks += [(l, 0, 0, piece // 2), (l, 0, piece // 2, piece // 2)]
            else:
                self.chunks += [(l, 0, 0, piece)]
            self.chunks += [(l, 1, 0, half), (l, 1, half, half)]
        self.of = lambda l, kind: [n for n, c in enumerate(self.chunks) if c[0] == l and (c[1] > 0) == (kind > 0)]
        self.direct = {n: (None, 1, 0)[n % 3] for n in range(len(self.chunks))}
        self.direct[1] = None
        self.ids, self.began, self.arrived = {}, [], set()

    def at(self, ref, k, layer, row, nrows, col, ncols, quarter):
        base = 0 if quarter is None else pl.multiple_of(quarter * self.shards[k].shape[1], 8)
        return ref.at[layer, pl.ds(pl.multiple_of(base + row, 8), nrows), pl.ds(col, ncols)]

    def place(self, w, l):
        n = self.shards[w].shape[1]
        return self.full[w].at[l, pl.ds(pl.multiple_of(self.f * n, 8), n)]

    def regions(self, n, ab, k):
        _, kind, start, count = self.chunks[n]
        d, piece = self.width, self.rows // 4
        if kind == 0:
            if ab == 0:
                return [(0, piece * k + start, count, 0, 2 * d)]
            return [(0, piece * k + start, count, 2 * d, d), (1, piece * k + start, count, 0, d)]
        if ab == 0:
            return [(2, start, count, pl.multiple_of(k * d, LANES), d)]
        return [(3, k * self.rows + start, count, 0, d)]

    def copies(self, key):
        kind = key[0]
        if kind == "own":
            _, l, w = key
            pairs, who = [(self.shards[w].at[l], self.place(w, l))], "c"
        elif kind == "small":
            who = key[1]
            row = self.far if key[2] else self.f
            pairs = [(self.every.at[row], self.every.at[row])]
        else:
            _, n, ab, j = key
            l = self.chunks[n][0]
            k = jnp.bitwise_xor(self.part, j)
            who = kind
            pairs = []
            for w, row, nr, col, nc in self.regions(n, ab, k):
                if kind == "y":
                    src = self.at(self.shards[w], w, l, row, nr, col, nc, None)
                    dst = self.at(self.full[w], w, l, row, nr, col, nc, self.f)
                else:
                    src = dst = self.at(self.full[w], w, l, row, nr, col, nc, self.far)
                pairs.append((src, dst))
        out = []
        for m, (src, dst) in enumerate(pairs):
            sem = self.ids.setdefault((key, m), len(self.ids))
            out.append(pltpu.make_async_remote_copy(
                src_ref=src, dst_ref=dst, send_sem=self.send_sem.at[sem], recv_sem=self.recv_sem.at[sem],
                device_id=self.who[who], device_id_type=MESH))
        return out

    def start(self, *key):
        for c in self.copies(key):
            c.start()
        self.began.append(key)

    def landed(self, *key):
        if key not in self.arrived:
            for c in self.copies(key):
                c.wait_recv()
            self.arrived.add(key)

    def step(self, k, n):
        if k == 0:
            for ab in (0, 1):
                self.start("y", n, ab, 0)
            if self.direct[n] is not None:
                self.start("y", n, self.direct[n], 3)
        elif k == 1:
            for ab in (0, 1):
                self.landed("y", n, ab, 0)
            for ab in (0, 1):
                self.start("x", n, ab, 0)
                self.start("z", n, ab, 0)
            for ab in (0, 1):
                self.start("c", n, ab, 0)
        elif k == 2:
            self.landed("x", n, 0, 0)
            self.landed("z", n, 1, 0)
            if self.direct[n] != 0:
                self.start("z", n, 0, 2)
            if self.direct[n] != 1:
                self.start("x", n, 1, 1)
            if self.direct[n] is not None:
                self.landed("y", n, self.direct[n], 3)
                self.start("c", n, self.direct[n], 3)
            self.start("c", n, 0, 2)
            self.start("c", n, 1, 1)
        else:
            self.landed("x", n, 1, 0)
            self.landed("z", n, 0, 0)
            self.start("c", n, 1, 2)
            self.start("c", n, 0, 1)
            for ab, link in ((0, "z"), (1, "x")):
                if self.direct[n] != ab:
                    self.landed(link, n, ab, 2 if ab == 0 else 1)
                    self.start("c", n, ab, 3)

    def ready(self, n):
        for ab in (0, 1):
            for j in range(4):
                self.landed("c", n, ab, j)

    def drain(self):
        for key in self.began:
            for c in self.copies(key):
                c.wait_send()


def fore_kernel(layers, items, frames, subnet, *rest):
    smalls, (x_any, *shards) = rest[:8], rest[8:13]
    outs = rest[13:]
    full, (vec, ub, x1_o, out_o) = outs[:4], outs[4:8]
    kept = [outs[8 + 8 * l:16 + 8 * l] for l in range(layers)]
    scratch = outs[8 + 8 * layers:]
    every, own, (send_sem, recv_sem, local_sem) = scratch[0], scratch[1:5], scratch[5:8]
    w, x, qkv, pt, ob, r1, w_up, w_down, n1b, g, gp, acc = scratch[8:20]
    asem, fsem, xsem = scratch[20:23], scratch[23:26], scratch[26]
    width = x.shape[1]
    tab = Table(subnet, items, width)
    gat = Gather(layers, shards, full, every, send_sem, recv_sem)
    order = [(k, l) for l in range(layers) for k in range(4)]
    loads = [pltpu.make_async_copy(shards[k].at[l], own[k].at[l], local_sem.at[0, k, l]) for k, l in order]
    stores = [pltpu.make_async_copy(own[k].at[l], gat.place(k, l), local_sem.at[1, k, l]) for k, l in order]
    met = greet(list(gat.who.values()))
    load_x = fetch(x_any, x, xsem.at[0])
    for c in loads:
        c.start()
    every[gat.f] = jnp.zeros(every.shape[1:], F32)
    for k, ref in enumerate(smalls):
        for l in range(layers):
            every[gat.f, l, k:k + 1, 0:ref.shape[1]] = ref[l:l + 1, :].astype(F32)
    met()
    gat.start("small", "y", 0)
    gat.start("small", "c", 0)
    step = gat.step
    before = [(0, 1), (1, 0), (0, 2), (2, 0), (1, 1), (0, 3), (3, 0), (2, 1), (1, 2), (0, 4), (3, 1), (2, 2), (1, 3)]
    inside = [
        [{3: [(0, 5), (3, 2), (2, 3), (1, 4)]}, {3: [(3, 4), (2, 5), (1, 6)]}],
        [{3: [(3, 5), (2, 6)]}, {}],
    ]
    after = [[[(0, 6), (3, 3), (2, 4), (1, 5)], []], [[(3, 6)], []]]
    step(0, 0)
    for c, d in zip(loads, stores):
        c.wait()
        d.start()
    gat.landed("small", "y", 0)
    gat.start("small", "c", 1)
    for k in range(4):
        gat.start("own", 0, k)
    load_x.wait()
    mask_rows(x, items, frames, tab)
    for one in before:
        step(*one)
    gat.landed("small", "c", 0)
    gat.landed("small", "c", 1)
    rows = gat.rows
    for q in range(4):
        for l in range(layers):
            vec[l, 0:7, q * rows:(q + 1) * rows] = every[q, l, 0:7, 0:rows]
            ub[l, :, q * width:(q + 1) * width] = every[q, l, 7:8, :]
    for c in stores:
        c.wait()
    for l in range(1, layers):
        for k in range(4):
            gat.start("own", l, k)

    def hooks(l, k):
        def at(steps):
            return lambda: [step(*one) for one in steps] and None
        return {c: at(steps) for c, steps in inside[l][k].items()}

    def need(l, kind):
        for k in ((2, 3) if kind else (0, 1)):
            gat.landed("own", l, k)
        for n in gat.of(l, kind):
            gat.ready(n)

    pending = None
    for l in range(layers):
        need(l, 0)
        if pending is not None:
            pending[0]()
        end_a = attn_front(
            l, items, frames, tab, vec, (w, x, qkv, pt, ob, r1), full[:2], asem, kept[l][:4], hooks(l, 0))
        for one in after[l][0]:
            step(*one)
        need(l, 1)
        if pending is not None:
            pending[1]()
        last = l == layers - 1
        end_f = ffn_front(
            l, last, items, frames, tab, vec, ub, (w_up, w_down, r1, x, n1b, g, gp, acc), full[2:], fsem,
            (*kept[l][4:], out_o if last else x1_o), hooks(l, 1))
        for one in after[l][1]:
            step(*one)
        pending = (end_a, end_f)
    pending[0]()
    pending[1]()
    gat.drain()


def fore(subnet, smalls, x, weights):
    layers = weights[0].shape[0]
    items, t, d = x.shape
    n = items * t
    ff = weights[2].shape[2]
    vm, dma = pltpu.VMEM, pltpu.SemaphoreType.DMA
    keep = [sds((3, n, d), BF), sds((items, HEADS, t, t), BF), sds((n, d), BF), sds((n, d), F32), sds((n, d), BF),
            sds((n, ff), BF), sds((n, ff), BF), sds((n, d), F32)]
    outs = [sds((layers, 4 * w.shape[1], w.shape[2]), BF) for w in weights] + [
        sds((layers, 8, d), F32), sds((layers, 1, ff), F32), sds((n, d), BF), sds((n, d), BF)] + keep * layers
    square = vm((n, d), BF)
    res = pl.pallas_call(
        functools.partial(fore_kernel, layers, items, t),
        out_shape=tuple(outs),
        in_specs=[SM] + [VM] * 8 + [ANY] * 5,
        out_specs=tuple(VM if k in (4, 5) else ANY for k in range(len(outs))),
        scratch_shapes=[
            vm((4, layers, 8, d), F32), *[vm(w.shape, BF) for w in weights], dma((200,)), dma((200,)), dma((2, 4, layers)),
            vm((4, d, d), BF), square, vm((3, n, d), BF), vm((items, HEADS, t, t), BF), square, vm((n, d), F32),
            vm((d, ff), BF), vm((ff, d), BF), square, vm((n, ff), BF), vm((n, ff), BF), vm((n, d), F32),
            dma((4,)), dma((5,)), dma((d // LANES,)), dma((ff // d, 2)), dma((3,)), dma((2, ff // UNIT_CHUNK)), dma((1,)),
        ],
        compiler_params=pltpu.CompilerParams(collective_id=0, has_side_effects=True, vmem_limit_bytes=60 * 2 ** 20),
        name="fore",
    )(subnet, *smalls, x.reshape(n, d), *weights)
    return res[:4], res[4], res[5], res[6], res[7], [res[8 + 8 * l:16 + 8 * l] for l in range(layers)]


def when(cond):
    if isinstance(cond, bool):
        return lambda f: f() if cond else None
    return pl.when(cond)


def both(a, b):
    return a and b if isinstance(a, bool) else jnp.logical_and(a, b)


class Reduce:
    LOC, RECV = 6, 6

    def __init__(self, count, bits, g, out, refs):
        self.count, self.bits, self.g, self.out = count, bits, g, out
        self.loc, self.rc, self.ry, self.rx, self.rz, self.fin, self.ss, self.rs, self.ls, self.os = refs
        f, pipe = lax.axis_index("fsdp"), lax.axis_index("pipe")
        self.c, self.y, x, z = f % 2, f // 2, pipe % 2, (pipe // 2) % 2
        rows = g.shape[3]
        half, quarter = rows // 2, rows // 4
        self.who = [flip("fsdp", 0), flip("fsdp", 1)] + [flip("pipe", b) for b in range(bits)]
        part = lambda at, n: pl.ds(pl.multiple_of(at, 16), n)
        self.my_half, self.their_half = part(x * half, half), part((1 - x) * half, half)
        self.mine, self.theirs = part(x * half + z * quarter, quarter), part(x * half + (1 - z) * quarter, quarter)
        self.n_red = 2 + bits
        self.total = self.n_red + 2
        self.slots = self.fin.shape[0]

    @staticmethod
    def scratch(bits, count, rows, d):
        vm, dma = pltpu.VMEM, pltpu.SemaphoreType.DMA
        n = bits + 4
        return [
            vm((Reduce.LOC, 2, rows, d), BF), vm((Reduce.RECV, 2, rows, d), BF), vm((Reduce.RECV, rows, d), BF),
            vm((Reduce.RECV, rows // 2, d), BF), vm((bits - 1, Reduce.RECV, rows // 4, d), BF), vm((n + 2, rows, d), BF),
            dma((n, count)), dma((n, count)), dma((count,)), dma((count,)),
        ]

    def load(self, p):
        return pltpu.make_async_copy(self.g.at[:, p, self.c], self.loc.at[p % self.LOC], self.ls.at[p])

    def store(self, p):
        return pltpu.make_async_copy(self.fin.at[p % self.slots], self.out.at[p], self.os.at[p])

    def move(self, k, p):
        loc, fin, r = self.loc.at[p % self.LOC], self.fin.at[p % self.slots], p % self.RECV
        if k == 0:
            src, dst, who = self.g.at[:, p, 1 - self.c], self.rc.at[r], 0
        elif k == 1:
            src, dst, who = loc.at[1 - self.y], self.ry.at[r], 1
        elif k == 2:
            src, dst, who = loc.at[self.y, self.their_half], self.rx.at[r], 2
        elif k == 3:
            src, dst, who = loc.at[self.y, self.theirs], self.rz.at[0, r], 3
        elif k < self.n_red:
            src, dst, who = fin.at[self.mine], self.rz.at[k - 3, r], k
        elif k == self.n_red:
            src, dst, who = fin.at[self.mine], fin.at[self.mine], 3
        else:
            src, dst, who = fin.at[self.my_half], fin.at[self.my_half], 2
        return pltpu.make_async_remote_copy(
            src_ref=src, dst_ref=dst, send_sem=self.ss.at[k, p], recv_sem=self.rs.at[k, p], device_id=self.who[who],
            device_id_type=MESH)

    def arrive(self, k, p):
        self.move(k, p).wait()
        s, f, r = p % self.LOC, p % self.slots, p % self.RECV
        if k == 0:
            self.load(p).wait()
            self.loc[s] = add_low(self.loc[s], self.rc[r])
        elif k == 1:
            self.loc[s, self.y] = add_low(self.loc[s, self.y], self.ry[r])
        elif k == 2:
            self.loc[s, self.y, self.my_half] = add_low(self.loc[s, self.y, self.my_half], self.rx[r])
        elif k == 3:
            self.fin[f, self.mine] = add_low(self.loc[s, self.y, self.mine], self.rz[0, r])
        elif k < self.n_red:
            self.fin[f, self.mine] = add_low(self.fin[f, self.mine], self.rz[k - 3, r])

    def begin(self):
        self.move(0, 0).start()
        self.load(0).start()

    def tick(self, t):
        @when(t + 1 < self.count)
        def _():
            self.move(0, t + 1).start()
            self.load(t + 1).start()

        for k in range(self.total):
            p = t - k - min(k, 1)

            @when(both(p >= 0, p < self.count))
            def _(k=k, p=p):
                self.arrive(k, p)
                if k + 1 < self.total:
                    self.move(k + 1, p).start()
                else:
                    self.store(p).start()

        p = t - self.total - 1

        @when(both(p >= 0, p < self.count))
        def _():
            self.store(p).wait()

    def ticks(self):
        return self.count + self.total + 1


def add_low(a, b):
    return a + b


class SumAll:
    def __init__(self, who, total, recv, ss, rs):
        self.who, self.total, self.recv, self.ss, self.rs = who, total, recv, ss, rs

    def move(self, k):
        return pltpu.make_async_remote_copy(
            src_ref=self.total, dst_ref=self.recv.at[k], send_sem=self.ss.at[k], recv_sem=self.rs.at[k],
            device_id=self.who[k], device_id_type=MESH)

    def step(self, k):
        for j in range(len(self.who) + 1):
            @pl.when(k == j)
            def _(j=j):
                if j > 0:
                    self.move(j - 1).wait()
                    self.total[...] = self.total[...] + self.recv[j - 1]
                if j < len(self.who):
                    self.move(j).start()


def attn_back(layer, items, frames, tab, src, buf, weights, sems, first, grads, tick, dx_out):
    qkv_any, pt_any, x_any, ob_any = src
    w, da, dr1, qkv, pt, x, ob, do, dqkv, dx, stage = buf
    wsem, sem, ptsem, qsem = sems
    width = da.shape[1]
    npair = width // LANES
    ring = pt.shape[0]
    p = Attn(layer, weights, w, wsem)
    p.start((3, 0, 1, 2))

    def block(ref, j):
        return ref.at[:, pl.ds(pl.multiple_of(j * width, LANES), width)]

    loads = [fetch(qkv_any.at[j], block(qkv, j), sem.at[3 + j]) for j in range(3)]

    def load_pt(c):
        return pltpu.make_async_copy(pt_any.at[:, pl.ds(2 * c, 2)], pt.at[c % ring], ptsem.at[c])

    for c in range(ring - 1):
        load_pt(c).start()
    later = [fetch(ob_any, ob, sem.at[0]), fetch(x_any, x, sem.at[1])]
    p.wait(3)
    dos = [dot_nt(da[rows_of(i, frames), :], w[3]) for i in range(items)]
    for i, d in enumerate(dos):
        do[rows_of(i, frames), :] = d.astype(BF)
    for o in loads:
        o.wait()
    scale = HEAD_DIM ** -0.5
    qsums = []

    def pair(c, _):
        for at in (0, 3):
            @pl.when(c == at)
            def _():
                tick()

        lanes = pl.ds(pl.multiple_of(c * LANES, LANES), LANES)
        ids = lax.broadcasted_iota(jnp.int32, (1, LANES), 1) + c * LANES
        load_pt(c).wait()

        @pl.when(c + ring - 1 < npair)
        def _():
            load_pt(c + ring - 1).start()

        rr = [rows_of(i, frames) for i in range(items)]
        at = [pl.ds(pl.multiple_of(j * width + c * LANES, LANES), LANES) for j in range(3)]
        q = [qkv[r, at[0]] for r in rr]
        k = [qkv[r, at[1]] for r in rr]
        v = [qkv[r, at[2]] for r in rr]
        dob = [do[r, lanes] for r in rr]
        kt = [a.T for a in k]
        heads = [(n, h) for n in range(items) for h in (0, 1)]
        pbs = [pt[c % ring, n, h] for n, h in heads]
        dps = [dot_nt(only(h, v[n]), dob[n]) for n, h in heads]
        dvs = [dot_nn(pb, dob[n]) for pb, (n, h) in zip(pbs, heads)]
        tmps = [pb.astype(F32) * dp for pb, dp in zip(pbs, dps)]
        dss = [(t - pb.astype(F32) * jnp.sum(t, axis=0, keepdims=True)).astype(BF) for t, pb in zip(tmps, pbs)]
        dks = [dot_nn(ds, q[n]) for ds, (n, h) in zip(dss, heads)]
        dqs = [dot_nn(kt[n][h * HEAD_DIM:(h + 1) * HEAD_DIM], ds) for ds, (n, h) in zip(dss, heads)]
        for n in range(items):
            on = ids < tab.a[n]
            put = lambda v, s: jnp.where(on, v * s, 0.0).astype(BF)
            dqkv[rr[n], at[0]] = put(jnp.concatenate(dqs[2 * n:2 * n + 2], axis=0).T, scale)
            dqkv[rr[n], at[1]] = put(jnp.where(half_mask(0), dks[2 * n], dks[2 * n + 1]), scale)
            dqkv[rr[n], at[2]] = put(jnp.where(half_mask(0), dvs[2 * n], dvs[2 * n + 1]), 1.0)
        return 0

    lax.fori_loop(0, npair, pair, 0)
    tick()
    q_sum = jnp.sum(dqkv[:, 0:width].astype(F32), axis=0, keepdims=True)
    for o in later:
        o.wait()
    if layer == 0:
        mask_rows(x, items, frames, tab)
    quarters = Quarters(stage, grads, qsem, first)
    rows = stage.shape[3]

    def step(lhs, rhs, b):
        for y in (0, 1):
            res = dot_tn(lhs[:, y * 2 * rows:(y + 1) * 2 * rows], rhs).astype(BF)
            for t in (0, 1):
                stage[y, b, t] = res[t * rows:(t + 1) * rows]
            quarters.start(y, b)

    def in_step(j, _):
        step(x, block(dqkv, j)[...], j)
        return 0

    lax.fori_loop(0, 3, in_step, 0)
    step(ob, da[...], 3)
    quarters.wait()
    tick()
    for j in range(3):
        p.wait(j)

    def back_step(j, _):
        adds = [dot_nt(block(dqkv, j)[rows_of(i, frames), :], w[j]) for i in range(items)]
        for i, add in enumerate(adds):
            dr1[rows_of(i, frames), :] += add
        return 0

    lax.fori_loop(0, 3, back_step, 0)
    for i in range(items):
        rr = rows_of(i, frames)
        dx[rr, :] = (dr1[rr, :] * lane_mask(width, tab.w[i])).astype(BF)
    if dx_out is not None:
        fetch(dx, dx_out, sem.at[2])
    return q_sum


def ffn_back(layer, last, items, frames, tab, vec, src, buf, weights, sems, first, grads, hooks, sums):
    cot_any, r2_any, r1_any, gp_any, g_any, n1b_any = src
    w_up, w_down, cot, dxn, r, du, g, n1b, df, acc, da, stage = buf
    wsem, sem, gsem, qsem = sems
    width, units = w_up.shape
    nblk, nch = units // width, units // UNIT_CHUNK
    rows = stage.shape[3]
    down = Quarters(stage, grads, qsem.at[0], first)
    up = Quarters(stage, grads, qsem.at[1], first + nblk)
    loads = [fetch(r2_any, r, sem.at[0]), fetch(cot_any, cot, sem.at[1])]
    load_g = fetch(g_any, g, sem.at[4])
    p = Ffn(layer, weights, w_up, w_down, wsem)
    p.start()

    def load_gp(c):
        cols = pl.ds(pl.multiple_of(c * UNIT_CHUNK, UNIT_CHUNK), UNIT_CHUNK)
        return pltpu.make_async_copy(gp_any.at[:, cols], du.at[:, cols], gsem.at[c])

    for c in range(nch):
        load_gp(c).start()
    load_n1b = fetch(n1b_any, n1b, sem.at[3])
    for o in loads:
        o.wait()
    for i in range(items):
        rr = rows_of(i, frames)
        cm = lane_mask(width, tab.w[i])
        if last:
            dy = jnp.where(tab.skip[i] == 1, 0.0, cot[rr, :].astype(F32))
        else:
            dy = jnp.where(tab.skip[i] == 1, cot[rr, :], dxn[rr, :]).astype(F32)
        xhat, rstd = normed(r[rr, :], cm, tab.inv[i])
        dr2, dg, ds = norm_back(dy, xhat, rstd, vec[layer, ROW_G2:ROW_G2 + 1, :], cm, tab.inv[i])
        dfb = dr2.astype(BF)
        df[rr, :] = dfb
        acc[rr, :] = dr2
        sums[ROW_G2:ROW_G2 + 1, 0:width] += dg
        sums[ROW_B2:ROW_B2 + 1, 0:width] += ds
        sums[ROW_DB:ROW_DB + 1, 0:width] += jnp.sum(dfb.astype(F32), axis=0, keepdims=True)
    load_r1 = fetch(r1_any, r, sem.at[2])
    hooks["norm"]()
    load_g.wait()

    for s in range(nblk // 2):
        def down_step(f, _, s=s):
            y, par = f // 2, f % 2
            lanes = pl.ds(pl.multiple_of(f * width + s * 2 * rows, LANES), 2 * rows)
            res = dot_tn(g[:, lanes], df[...]).astype(BF)
            for t in (0, 1):
                stage[y, 2 * s + t, par] = res[t * rows:(t + 1) * rows]
            return 0

        lax.fori_loop(0, 4, down_step, 0)
        for b in (2 * s, 2 * s + 1):
            for y in (0, 1):
                down.start(y, b)
        if s == 0:
            down.wait_block(0)
            hooks["first"]()
    down.wait_block(1)
    hooks["down"]()

    def chunk(c, _):
        for at in (1, 4):
            @pl.when(c == at)
            def _(at=at):
                if at == 1:
                    for b in range(2, nblk):
                        down.wait_block(b)
                hooks["mid"]()

        p.before(c)
        load_gp(c).wait()
        cols = pl.ds(pl.multiple_of(c * UNIT_CHUNK, UNIT_CHUNK), UNIT_CHUNK)
        dgs = [dot_nt(df[rows_of(i, frames), :], w_down[cols, :]) for i in range(items)]
        dubs = []
        for i, dg in enumerate(dgs):
            dub = (dg * du[rows_of(i, frames), cols].astype(F32)).astype(BF)
            du[rows_of(i, frames), cols] = dub
            sums[ROW_UB:ROW_UB + 1, cols] += jnp.sum(dub.astype(F32), axis=0, keepdims=True)
            dubs.append(dub)
        for i, dub in enumerate(dubs):
            acc[rows_of(i, frames), :] += dot_nt(dub, w_up[:, cols])
        return 0

    lax.fori_loop(0, nch, chunk, 0)
    hooks["chunks"]()
    load_r1.wait()
    for i in range(items):
        rr = rows_of(i, frames)
        cm = lane_mask(width, tab.w[i])
        xhat, rstd = normed(r[rr, :], cm, tab.inv[i])
        d1, dg, ds = norm_back(acc[rr, :], xhat, rstd, vec[layer, ROW_G1:ROW_G1 + 1, :], cm, tab.inv[i])
        acc[rr, :] = d1
        dab = d1.astype(BF)
        da[rr, :] = dab
        sums[ROW_G1:ROW_G1 + 1, 0:width] += dg
        sums[ROW_B1:ROW_B1 + 1, 0:width] += ds
        sums[ROW_OB:ROW_OB + 1, 0:width] += jnp.sum(dab.astype(F32), axis=0, keepdims=True)
    hooks["norm1"]()
    load_n1b.wait()

    def up_step(j, _):
        cols = pl.ds(pl.multiple_of(j * width, LANES), width)
        for y in (0, 1):
            res = dot_tn(n1b[:, y * 2 * rows:(y + 1) * 2 * rows], du[:, cols]).astype(BF)
            for t in (0, 1):
                stage[y, j, t] = res[t * rows:(t + 1) * rows]
            up.start(y, j)
        return 0

    lax.fori_loop(0, nblk, up_step, 0)
    up.wait()
    hooks["up"]()


def back_kernel(items, frames, bits, blocks, subnet, vec, cot_any, x0_any, x1_any, *rest):
    kept, weights = (rest[:8], rest[8:16]), rest[16:20]
    (dx_o, grads, out, total, w_up, w, da, dr1, pt, x, ob, do, dx, r, du, g, stage, srecv) = rest[20:38]
    asem, bsem, fsem, gsem = rest[38:42], rest[42:46], rest[46:50], rest[50:54]
    red = Reduce(2 * blocks, bits, grads, out, rest[54:64])
    s_send, s_recv = rest[64:]
    width = da.shape[1]
    tab = Table(subnet, items, width)
    met = greet(red.who)
    total[...] = jnp.zeros_like(total)
    nb = w_up.shape[1] // width
    w_att, w_ffn = weights[:2], weights[2:]
    count = [0]

    def tick():
        red.tick(count[0])
        count[0] += 1

    def begin():
        met()
        red.begin()

    nothing = lambda: None
    att = lambda l: (kept[l][0], kept[l][1], (x0_any, x1_any)[l], kept[l][2])
    ffn = lambda l: (cot_any, kept[l][7], kept[l][3], kept[l][6], kept[l][5], kept[l][4])
    buf = (w, da, dr1, du, pt, x, ob, do, g, dx, stage)
    buf_f = (w_up, w.reshape(nb * width, width), x, dx, r, du, g, ob, do, dr1, da, stage)
    ffn_back(1, True, items, frames, tab, vec, ffn(1), buf_f, w_ffn, fsem, 0, grads,
             dict(norm=nothing, first=begin, down=tick, mid=tick, chunks=nothing, norm1=nothing, up=tick), total.at[1])
    total[1, ROW_QB:ROW_QB + 1, 0:width] = attn_back(
        1, items, frames, tab, att(1), buf, w_att, asem, 2 * nb, grads, tick, None)
    ffn_back(0, False, items, frames, tab, vec, ffn(0), buf_f, w_ffn, gsem, blocks, grads,
             dict(norm=tick, first=nothing, down=nothing, mid=tick, chunks=tick, norm1=tick, up=tick), total.at[0])
    total[0, ROW_QB:ROW_QB + 1, 0:width] = attn_back(
        0, items, frames, tab, att(0), buf, w_att, bsem, blocks + 2 * nb, grads, tick, dx_o)
    small = SumAll(red.who, total, srecv, s_send, s_recv)
    t = count[0]

    def rest_of(n, _):
        red.tick(n)
        small.step(n - t)
        return 0

    lax.fori_loop(t, red.ticks(), rest_of, 0)
    pltpu.make_async_copy(dx, dx_o, bsem[1].at[2]).wait()


def back(subnet, vec, cot, x0, x1, kept, weights):
    bits = 0
    while (1 << bits) < lax.axis_size("pipe"):
        bits += 1
    n, d = cot.shape
    items, _, t, _ = kept[0][1].shape
    ff = kept[0][5].shape[1]
    rows, nb = d // 4, ff // d
    blocks = 2 * nb + 4
    small = (2, 8, ff)
    vm, dma = pltpu.VMEM, pltpu.SemaphoreType.DMA
    square = vm((n, d), BF)
    hbm = (cot, x0, x1, *kept[0], *kept[1], *weights)
    asems = [dma((4,)), dma((6,)), dma((d // LANES,)), dma((2, 4))]
    fsems = [dma((nb, 2)), dma((5,)), dma((ff // UNIT_CHUNK,)), dma((2, 2, nb))]
    return pl.pallas_call(
        functools.partial(back_kernel, items, t, bits, blocks),
        out_shape=(sds((n, d), BF), sds((2, 2 * blocks, 2, rows, d), BF), sds((2 * blocks, rows, d), BF), sds(small, F32)),
        in_specs=[SM, VM] + [ANY] * len(hbm),
        out_specs=(ANY, ANY, ANY, VM),
        scratch_shapes=[
            vm((d, ff), BF), vm((4, d, d), BF), square, vm((n, d), F32), vm((3, items, 2, t, t), BF),
            square, square, square, square, vm((n, d), F32), vm((n, ff), BF), vm((n, ff), BF),
            vm((2, 4, 2, rows, d), BF), vm((2 + bits,) + small, F32),
            *asems, *asems, *fsems, *fsems, *Reduce.scratch(bits, 2 * blocks, rows, d), dma((2 + bits,)), dma((2 + bits,)),
        ],
        compiler_params=pltpu.CompilerParams(collective_id=1, has_side_effects=True, vmem_limit_bytes=60 * 2 ** 20),
        name="back",
    )(subnet, vec, *hbm)


def finish_kernel(layers, red, rows_a, rows_b, total, g_in, g_out, g_up, g_down, *rest):
    vecs, passed, (bf, f32, keep, sem_in, sem_out, sem_rows) = rest[:8], rest[8:10], rest[10:]
    f = lax.axis_index("fsdp")
    blocks = bf.shape[0]
    rows, d = bf.shape[1:]
    per = blocks // layers
    nb = (per - 4) // 2

    def target(l, k):
        if k < nb:
            return g_down.at[l, pl.ds(k * rows, rows)]
        if k < 2 * nb:
            return g_up.at[l, :, pl.ds((k - nb) * d, d)]
        if k < 2 * nb + 3:
            return g_in.at[l, :, pl.ds((k - 2 * nb) * d, d)]
        return g_out.at[l]

    loads = [pltpu.make_async_copy(red.at[p], bf.at[p], sem_in.at[p]) for p in range(blocks)]
    stores = [pltpu.make_async_copy(f32.at[p], target(layers - 1 - p // per, p % per), sem_out.at[p]) for p in range(blocks)]
    rows_in = [pltpu.make_async_copy(a, keep.at[k], sem_rows.at[0, k]) for k, a in enumerate((rows_a, rows_b))]
    rows_out = [pltpu.make_async_copy(keep.at[k], a, sem_rows.at[1, k]) for k, a in enumerate(passed)]
    for c in rows_in + loads:
        c.start()
    for came, goes in zip(rows_in, rows_out):
        came.wait()
        goes.start()
    for q in range(4):
        @pl.when(f == q)
        def _(q=q):
            for l in range(layers):
                for k in range(7):
                    vecs[k][l:l + 1, :] = total[l, k:k + 1, q * rows:(q + 1) * rows]
                vecs[7][l:l + 1, :] = total[l, 7:8, q * d:(q + 1) * d]
    for p in range(blocks):
        loads[p].wait()
        f32[p] = bf[p].astype(F32)
        stores[p].start()
    for c in stores + rows_out:
        c.wait()


def finish(red, rows_a, rows_b, total):
    blocks, rows, d = red.shape
    layers = total.shape[0]
    nb = (blocks // layers - 4) // 2
    return pl.pallas_call(
        functools.partial(finish_kernel, layers),
        out_shape=(sds((layers, rows, 3 * d), F32), sds((layers, rows, d), F32), sds((layers, rows, nb * d), F32),
                   sds((layers, nb * rows, d), F32)) + (sds((layers, rows), F32),) * 7 + (sds((layers, d), F32),)
        + (sds(rows_a.shape, BF), sds(rows_b.shape, BF)),
        in_specs=[ANY, ANY, ANY, VM],
        out_specs=(ANY,) * 4 + (VM,) * 8 + (ANY, ANY),
        scratch_shapes=[pltpu.VMEM(red.shape, BF), pltpu.VMEM(red.shape, F32), pltpu.VMEM((2,) + rows_a.shape, BF),
                        pltpu.SemaphoreType.DMA((blocks,)), pltpu.SemaphoreType.DMA((blocks,)),
                        pltpu.SemaphoreType.DMA((2, 2))],
        compiler_params=pltpu.CompilerParams(**PARAMS),
        name="finish",
    )(red, rows_a, rows_b, total)


def local(
    frames_in, attn_in, q_bias, attn_out, out_bias, norm1_gain, norm1_bias, ffn_up, up_bias, ffn_down, down_bias,
    norm2_gain, norm2_bias, subnet, out_cotangent,
):
    items, frames, width = frames_in.shape
    ff = ffn_up.shape[2]
    layers = attn_in.shape[0]
    nb = ff // width
    smalls = (q_bias, out_bias, norm1_gain, norm1_bias, down_bias, norm2_gain, norm2_bias, up_bias)
    n = items * frames
    weights, vec, ub, x1, layer_out, kept = fore(subnet, smalls, frames_in, (attn_in, attn_out, ffn_up, ffn_down))
    cot = out_cotangent.reshape(n, width)
    dx, _, red, total = back(subnet, vec, cot, frames_in.reshape(n, width), x1, kept, weights)
    g_in, g_out, g_up, g_down, g_qb, g_ob, g_g1, g_b1, g_db, g_g2, g_b2, g_ub, layer_out, dx = finish(
        red, layer_out, dx, total)
    return (layer_out.reshape(frames_in.shape), dx.reshape(frames_in.shape), g_in, g_qb, g_out, g_ob, g_g1, g_b1, g_up, g_ub, g_down, g_db, g_g2, g_b2)


def solution(mesh):
    rows3 = P(None, "fsdp", None)
    rows2 = P(None, "fsdp")
    item = P(("pipe", "fsdp"), None, None)
    weights = (rows3, rows2, rows3, rows2, rows2, rows2, rows3, rows2, rows3, rows2, rows2, rows2)
    return jax.shard_map(
        local, mesh=mesh, in_specs=(item,) + weights + (P(), item), out_specs=(item, item) + weights, check_vma=False,
    )
```

```python
import functools

import jax
import jax.numpy as jnp
from jax import lax
from jax.experimental import pallas as pl
from jax.experimental.pallas import tpu as pltpu
from jax.sharding import PartitionSpec as P

HEADS = 12
HEAD_DIM = 64
EPSILON = 1e-05
LANES = 128
UNIT_CHUNK = 512
FRONT_CHUNK = 768
BF = jnp.bfloat16
F32 = jnp.float32

ROW_QB, ROW_OB, ROW_G1, ROW_B1, ROW_DB, ROW_G2, ROW_B2, ROW_UB = 0, 1, 2, 3, 4, 5, 6, 7

def dot_nn(a, b):
    return lax.dot_general(a, b, (((1,), (0,)), ((), ())), preferred_element_type=F32)


def dot_nt(a, b):
    return lax.dot_general(a, b, (((1,), (1,)), ((), ())), preferred_element_type=F32)


def dot_tn(a, b):
    return lax.dot_general(a, b, (((0,), (0,)), ((), ())), preferred_element_type=F32)


def lane_mask(width, count):
    return (lax.broadcasted_iota(jnp.int32, (1, width), 1) < count).astype(F32)


def normed(rows, cm, inv_w):
    mean = jnp.sum(rows * cm, axis=-1, keepdims=True) * inv_w
    centered = (rows - mean) * cm
    var = jnp.sum(centered * centered, axis=-1, keepdims=True) * inv_w
    rstd = lax.rsqrt(var + EPSILON)
    return centered * rstd, rstd


def norm_back(dy, xhat, rstd, gain, cm, inv_w):
    dym = dy * cm
    dg = jnp.sum(dym * xhat, axis=0, keepdims=True)
    ds = jnp.sum(dym, axis=0, keepdims=True)
    dx = dym * gain
    m1 = jnp.sum(dx, axis=-1, keepdims=True) * inv_w
    m2 = jnp.sum(dx * xhat, axis=-1, keepdims=True) * inv_w
    return cm * (rstd * (dx - m1 - xhat * m2)), dg, ds


class Attn:
    def __init__(self, layer, refs, w, sems):
        w_in, w_out = refs
        d = w.shape[1]
        self.copies = [
            pltpu.make_async_copy(w_in.at[layer, :, pl.ds(b * d, d)], w.at[b], sems.at[b]) for b in range(3)
        ] + [pltpu.make_async_copy(w_out.at[layer], w.at[3], sems.at[3])]

    def start(self, order):
        for b in order:
            self.copies[b].start()

    def wait(self, b):
        self.copies[b].wait()


class Ffn:
    def __init__(self, layer, refs, w_up, w_down, sems, chunk):
        up, down = refs
        d = w_up.shape[0]
        self.blocks = w_up.shape[1] // d
        self.first = [b * d // chunk for b in range(self.blocks)]
        self.copies = [(
            pltpu.make_async_copy(up.at[layer, :, pl.ds(b * d, d)], w_up.at[:, pl.ds(b * d, d)], sems.at[b, 0]),
            pltpu.make_async_copy(down.at[layer, pl.ds(b * d, d)], w_down.at[pl.ds(b * d, d)], sems.at[b, 1]),
        ) for b in range(self.blocks)]

    def start(self):
        for pair in self.copies:
            for copy in pair:
                copy.start()

    def wait(self, b):
        for copy in self.copies[b]:
            copy.wait()

    def before(self, c):
        for b in range(self.blocks):
            @pl.when(c == self.first[b])
            def _(b=b):
                self.wait(b)

    def drain(self, counts):
        most = jnp.maximum(counts[0], counts[1])
        for b in range(self.blocks):
            @pl.when(most <= self.first[b])
            def _(b=b):
                self.wait(b)


class Table:
    def __init__(self, subnet, items, width):
        segment = lax.axis_index("pipe") // (lax.axis_size("pipe") // 2)
        codes = [[subnet[k, segment * items + i] for k in range(4)] for i in range(items)]
        widths = [width * (4 + k) // 6 for k in range(3)]
        self.w = [width * (4 + c[0]) // 6 for c in codes]
        self.inv = [
            jnp.where(c[0] == 0, 1.0 / widths[0], jnp.where(c[0] == 1, 1.0 / widths[1], 1.0 / widths[2])) for c in codes]
        self.a = [HEAD_DIM * (HEADS * (4 + c[1]) // 6) for c in codes]
        self.u = [w * (6 + c[2]) // 2 for w, c in zip(self.w, codes)]
        self.skip = [c[3] for c in codes]
        self.pairs = [(a + LANES - 1) // LANES for a in self.a]
        self.chunks = [(u + UNIT_CHUNK - 1) // UNIT_CHUNK for u in self.u]


def fetch(src, dst, sem):
    copy = pltpu.make_async_copy(src, dst, sem)
    copy.start()
    return copy


def rows_of(i, frames):
    if isinstance(i, int):
        return pl.ds(i * frames, frames)
    return pl.ds(pl.multiple_of(i * frames, frames), frames)


def mask_rows(x, items, frames, tab):
    for i in range(items):
        rr = rows_of(i, frames)
        x[rr, :] = jnp.where(lane_mask(x.shape[1], tab.w[i]) > 0, x[rr, :], jnp.zeros((), x.dtype))


def half_mask(h):
    low = lax.broadcasted_iota(jnp.int32, (1, LANES), 1) < HEAD_DIM
    return low if h == 0 else jnp.logical_not(low)


def only(h, x):
    return jnp.where(half_mask(h), x, jnp.zeros_like(x))


def attn_front(layer, items, frames, tab, vec, buf, weights, sems, outs, hooks):
    w, x, qkv, pt, ob, r1 = buf
    wsem, sem, ptsem = sems
    qkv_o, pt_o, ob_o, r1_o = outs
    width = x.shape[1]
    npair = width // LANES
    p = Attn(layer, weights, w, wsem)
    p.start((0, 1, 2, 3))
    cms = [lane_mask(width, n) for n in tab.w]
    hms = [lane_mask(width, n) for n in tab.a]
    done = []
    for j in range(3):
        p.wait(j)
        accs = [dot_nn(x[rows_of(i, frames), :], w[j]) for i in range(items)]
        for i, acc in enumerate(accs):
            if j == 0:
                acc = acc + vec[layer, ROW_QB:ROW_QB + 1, :]
            qkv[j, rows_of(i, frames), :] = (acc * hms[i]).astype(BF)
        done.append(fetch(qkv.at[j], qkv_o.at[j], sem.at[j]))

    def store(c):
        return pltpu.make_async_copy(pt.at[:, pl.ds(2 * c, 2)], pt_o.at[:, pl.ds(2 * c, 2)], ptsem.at[c])

    def pair(c, _):
        for at, hook in hooks.items():
            @pl.when(c == at)
            def _(hook=hook):
                hook()

        lanes = pl.ds(pl.multiple_of(c * LANES, LANES), LANES)
        vts, ss = [], []
        for i in range(items):
            rr = rows_of(i, frames)
            q = qkv[0, rr, lanes] * jnp.asarray(HEAD_DIM ** -0.5, BF)
            k = qkv[1, rr, lanes]
            vts.append(qkv[2, rr, lanes].T)
            ss += [dot_nt(only(h, k), q) for h in (0, 1)]
        es = [jnp.exp(s - jnp.max(s, axis=0, keepdims=True)) for s in ss]
        pbs = [(e * (1.0 / jnp.sum(e, axis=0, keepdims=True))).astype(BF) for e in es]
        for i in range(items):
            mixed = []
            for h in (0, 1):
                pt[i, 2 * c + h] = pbs[2 * i + h]
                mixed.append(dot_nn(vts[i][h * HEAD_DIM:(h + 1) * HEAD_DIM], pbs[2 * i + h]))
            ob[rows_of(i, frames), lanes] = jnp.concatenate(mixed, axis=0).T.astype(BF)
        store(c).start()
        return 0

    lax.fori_loop(0, npair, pair, 0)
    done.append(fetch(ob, ob_o, sem.at[3]))
    p.wait(3)
    accs = [dot_nn(ob[rows_of(i, frames), :], w[3]) for i in range(items)]
    for i, acc in enumerate(accs):
        rr = rows_of(i, frames)
        r1[rr, :] = x[rr, :].astype(F32) + (acc + vec[layer, ROW_OB:ROW_OB + 1, :]) * cms[i]
    done.append(fetch(r1, r1_o, sem.at[4]))

    def finish():
        for c in range(npair):
            store(c).wait()
        for o in done:
            o.wait()

    return finish


def ffn_front(layer, last, items, frames, tab, vec, ub, buf, weights, sems, outs, hooks):
    w_up, w_down, r1, x, n1b, g, gp, acc = buf
    wsem, sem, gsem = sems
    n1b_o, g_o, gp_o, r2_o, out_o = outs
    width, units = w_up.shape
    nch = units // FRONT_CHUNK
    p = Ffn(layer, weights, w_up, w_down, wsem, FRONT_CHUNK)
    p.start()
    cms = [lane_mask(width, n) for n in tab.w]
    for i in range(items):
        rr = rows_of(i, frames)
        xhat, _ = normed(r1[rr, :], cms[i], tab.inv[i])
        n1 = (xhat * vec[layer, ROW_G1:ROW_G1 + 1, :] + vec[layer, ROW_B1:ROW_B1 + 1, :]) * cms[i]
        n1b[rr, :] = n1.astype(BF)
        acc[rr, :] = n1 + vec[layer, ROW_DB:ROW_DB + 1, :] * cms[i]
    done = [fetch(n1b, n1b_o, sem.at[0])]

    def store(k, c):
        cols = pl.ds(pl.multiple_of(c * FRONT_CHUNK, FRONT_CHUNK), FRONT_CHUNK)
        ref, out = ((g, g_o), (gp, gp_o))[k]
        return pltpu.make_async_copy(ref.at[:, cols], out.at[:, cols], gsem.at[k, c])

    def chunk(c, _):
        for at, hook in hooks.items():
            @pl.when(c == at)
            def _(hook=hook):
                hook()

        p.before(c)
        cols = pl.ds(pl.multiple_of(c * FRONT_CHUNK, FRONT_CHUNK), FRONT_CHUNK)
        ids = lax.broadcasted_iota(jnp.int32, (1, FRONT_CHUNK), 1) + c * FRONT_CHUNK
        us = [dot_nn(n1b[rows_of(i, frames), :], w_up[:, cols]) for i in range(items)]
        gbs = []
        for i, u in enumerate(us):
            fm = (ids < tab.u[i]).astype(F32)
            u = (u + ub[layer, 0:1, cols]) * fm
            half = 0.5 * (1.0 + lax.erf(u * (0.5 ** 0.5)))
            gb = (u * half).astype(BF)
            g[rows_of(i, frames), cols] = gb
            gp[rows_of(i, frames), cols] = ((half + u * (jnp.exp(u * u * -0.5) * 0.3989422804014327)) * fm).astype(BF)
            gbs.append(gb)
        for i, gb in enumerate(gbs):
            acc[rows_of(i, frames), :] += dot_nn(gb, w_down[cols, :]) * cms[i]
        for k in (0, 1):
            store(k, c).start()
        return 0

    lax.fori_loop(0, nch, chunk, 0)
    done.append(fetch(acc, r2_o, sem.at[1]))
    for i in range(items):
        rr = rows_of(i, frames)
        xhat, _ = normed(acc[rr, :], cms[i], tab.inv[i])
        y = ((xhat * vec[layer, ROW_G2:ROW_G2 + 1, :] + vec[layer, ROW_B2:ROW_B2 + 1, :]) * cms[i]).astype(BF)
        if last:
            y = jnp.where(tab.skip[i] == 1, x[rr, :], y)
        x[rr, :] = y
    done.append(fetch(x, out_o, sem.at[2]))

    def finish():
        for c in range(nch):
            for k in (0, 1):
                store(k, c).wait()
        for o in done:
            o.wait()

    return finish


class Quarters:
    def __init__(self, stage, out, sems, first):
        self.stage, self.out, self.sems, self.first = stage, out, sems, first

    def copy(self, y, b):
        return pltpu.make_async_copy(self.stage.at[y, b], self.out.at[y, self.first + b], self.sems.at[y, b])

    def start(self, y, b):
        self.copy(y, b).start()

    def wait_block(self, b):
        for y in range(self.stage.shape[0]):
            self.copy(y, b).wait()

    def wait(self):
        for b in range(self.stage.shape[1]):
            self.wait_block(b)


ANY = pl.BlockSpec(memory_space=pl.ANY)
VM = pl.BlockSpec(memory_space=pltpu.VMEM)
SM = pl.BlockSpec(memory_space=pltpu.SMEM)
PARAMS = dict(vmem_limit_bytes=58 * 2 ** 20)


def cost(flops, nbytes):
    return pl.CostEstimate(flops=int(flops), bytes_accessed=int(nbytes), transcendentals=0)


def sds(shape, dtype):
    return jax.ShapeDtypeStruct(shape, dtype)


MESH = pl.DeviceIdType.MESH


def flip(axis, bit):
    return {axis: jnp.bitwise_xor(lax.axis_index(axis), 1 << bit)}


def greet(partners):
    barrier = pltpu.get_barrier_semaphore()
    for who in partners:
        pl.semaphore_signal(barrier, inc=1, device_id=who, device_id_type=MESH)
    return lambda: pl.semaphore_wait(barrier, len(partners))


class Gather:
    def __init__(self, layers, shards, full, every, send_sem, recv_sem):
        self.layers, self.shards, self.full, self.every = layers, shards, full, every
        self.send_sem, self.recv_sem = send_sem, recv_sem
        self.f = lax.axis_index("fsdp")
        pipe = lax.axis_index("pipe")
        self.part = 2 * (pipe % 2) + (pipe // 2) % 2
        self.far = jnp.bitwise_xor(self.f, 2)
        self.who = {"c": flip("fsdp", 0), "y": flip("fsdp", 1), "x": flip("pipe", 0), "z": flip("pipe", 1)}
        self.rows, self.width = shards[1].shape[1:]
        piece, half = self.rows // 4, self.rows // 2
        self.chunks = []
        for l in range(layers):
            if l == 0:
                self.chunks += [(l, 0, 0, piece // 2), (l, 0, piece // 2, piece // 2)]
            else:
                self.chunks += [(l, 0, 0, piece)]
            self.chunks += [(l, 1, 0, half), (l, 1, half, half)]
        self.of = lambda l, kind: [n for n, c in enumerate(self.chunks) if c[0] == l and (c[1] > 0) == (kind > 0)]
        self.direct = {n: (None, 1, 0)[n % 3] for n in range(len(self.chunks))}
        self.direct[1] = None
        self.ids, self.began, self.arrived = {}, [], set()

    def at(self, ref, k, layer, row, nrows, col, ncols, quarter):
        base = 0 if quarter is None else pl.multiple_of(quarter * self.shards[k].shape[1], 8)
        return ref.at[layer, pl.ds(pl.multiple_of(base + row, 8), nrows), pl.ds(col, ncols)]

    def place(self, w, l):
        n = self.shards[w].shape[1]
        return self.full[w].at[l, pl.ds(pl.multiple_of(self.f * n, 8), n)]

    def regions(self, n, ab, k):
        _, kind, start, count = self.chunks[n]
        d, piece = self.width, self.rows // 4
        if kind == 0:
            if ab == 0:
                return [(0, piece * k + start, count, 0, 2 * d)]
            return [(0, piece * k + start, count, 2 * d, d), (1, piece * k + start, count, 0, d)]
        if ab == 0:
            return [(2, start, count, pl.multiple_of(k * d, LANES), d)]
        return [(3, k * self.rows + start, count, 0, d)]

    def copies(self, key):
        kind = key[0]
        if kind == "own":
            _, l, w = key
            pairs, who = [(self.shards[w].at[l], self.place(w, l))], "c"
        elif kind == "small":
            who = key[1]
            row = self.far if key[2] else self.f
            pairs = [(self.every.at[row], self.every.at[row])]
        else:
            _, n, ab, j = key
            l = self.chunks[n][0]
            k = jnp.bitwise_xor(self.part, j)
            who = kind
            pairs = []
            for w, row, nr, col, nc in self.regions(n, ab, k):
                if kind == "y":
                    src = self.at(self.shards[w], w, l, row, nr, col, nc, None)
                    dst = self.at(self.full[w], w, l, row, nr, col, nc, self.f)
                else:
                    src = dst = self.at(self.full[w], w, l, row, nr, col, nc, self.far)
                pairs.append((src, dst))
        out = []
        for m, (src, dst) in enumerate(pairs):
            sem = self.ids.setdefault((key, m), len(self.ids))
            out.append(pltpu.make_async_remote_copy(
                src_ref=src, dst_ref=dst, send_sem=self.send_sem.at[sem], recv_sem=self.recv_sem.at[sem],
                device_id=self.who[who], device_id_type=MESH))
        return out

    def start(self, *key):
        for c in self.copies(key):
            c.start()
        self.began.append(key)

    def landed(self, *key):
        if key not in self.arrived:
            for c in self.copies(key):
                c.wait_recv()
            self.arrived.add(key)

    def step(self, k, n):
        if k == 0:
            for ab in (0, 1):
                self.start("y", n, ab, 0)
            if self.direct[n] is not None:
                self.start("y", n, self.direct[n], 3)
        elif k == 1:
            for ab in (0, 1):
                self.landed("y", n, ab, 0)
            for ab in (0, 1):
                self.start("x", n, ab, 0)
                self.start("z", n, ab, 0)
            for ab in (0, 1):
                self.start("c", n, ab, 0)
        elif k == 2:
            self.landed("x", n, 0, 0)
            self.landed("z", n, 1, 0)
            if self.direct[n] != 0:
                self.start("z", n, 0, 2)
            if self.direct[n] != 1:
                self.start("x", n, 1, 1)
            if self.direct[n] is not None:
                self.landed("y", n, self.direct[n], 3)
                self.start("c", n, self.direct[n], 3)
            self.start("c", n, 0, 2)
            self.start("c", n, 1, 1)
        else:
            self.landed("x", n, 1, 0)
            self.landed("z", n, 0, 0)
            self.start("c", n, 1, 2)
            self.start("c", n, 0, 1)
            for ab, link in ((0, "z"), (1, "x")):
                if self.direct[n] != ab:
                    self.landed(link, n, ab, 2 if ab == 0 else 1)
                    self.start("c", n, ab, 3)

    def ready(self, n):
        for ab in (0, 1):
            for j in range(4):
                self.landed("c", n, ab, j)

    def drain(self):
        for key in self.began:
            for c in self.copies(key):
                c.wait_send()


def fore_kernel(layers, items, frames, subnet, *rest):
    smalls, (x_any, *shards) = rest[:8], rest[8:13]
    outs = rest[13:]
    full, (vec, ub, x1_o, out_o) = outs[:4], outs[4:8]
    kept = [outs[8 + 8 * l:16 + 8 * l] for l in range(layers)]
    scratch = outs[8 + 8 * layers:]
    every, own, (send_sem, recv_sem, local_sem) = scratch[0], scratch[1:5], scratch[5:8]
    w, x, qkv, pt, ob, r1, w_up, w_down, n1b, g, gp, acc = scratch[8:20]
    asem, fsem, xsem = scratch[20:23], scratch[23:26], scratch[26]
    width = x.shape[1]
    tab = Table(subnet, items, width)
    gat = Gather(layers, shards, full, every, send_sem, recv_sem)
    order = [(k, l) for l in range(layers) for k in range(4)]
    loads = [pltpu.make_async_copy(shards[k].at[l], own[k].at[l], local_sem.at[0, k, l]) for k, l in order]
    stores = [pltpu.make_async_copy(own[k].at[l], gat.place(k, l), local_sem.at[1, k, l]) for k, l in order]
    met = greet(list(gat.who.values()))
    load_x = fetch(x_any, x, xsem.at[0])
    for c in loads:
        c.start()
    every[gat.f] = jnp.zeros(every.shape[1:], F32)
    for k, ref in enumerate(smalls):
        for l in range(layers):
            every[gat.f, l, k:k + 1, 0:ref.shape[1]] = ref[l:l + 1, :].astype(F32)
    met()
    gat.start("small", "y", 0)
    gat.start("small", "c", 0)
    step = gat.step
    before = [(0, 1), (1, 0), (0, 2), (2, 0), (1, 1), (0, 3), (3, 0), (2, 1), (1, 2), (0, 4), (3, 1), (2, 2), (1, 3)]
    inside = [
        [{3: [(0, 5), (3, 2), (2, 3), (1, 4)]}, {2: [(3, 4), (2, 5), (1, 6)]}],
        [{3: [(3, 5), (2, 6)]}, {}],
    ]
    after = [[[(0, 6), (3, 3), (2, 4), (1, 5)], []], [[(3, 6)], []]]
    step(0, 0)
    for c, d in zip(loads, stores):
        c.wait()
        d.start()
    gat.landed("small", "y", 0)
    gat.start("small", "c", 1)
    for k in range(4):
        gat.start("own", 0, k)
    load_x.wait()
    mask_rows(x, items, frames, tab)
    for one in before:
        step(*one)
    gat.landed("small", "c", 0)
    gat.landed("small", "c", 1)
    rows = gat.rows
    for q in range(4):
        for l in range(layers):
            vec[l, 0:7, q * rows:(q + 1) * rows] = every[q, l, 0:7, 0:rows]
            ub[l, :, q * width:(q + 1) * width] = every[q, l, 7:8, :]
    for c in stores:
        c.wait()
    for l in range(1, layers):
        for k in range(4):
            gat.start("own", l, k)

    def hooks(l, k):
        def at(steps):
            return lambda: [step(*one) for one in steps] and None
        return {c: at(steps) for c, steps in inside[l][k].items()}

    def need(l, kind):
        for k in ((2, 3) if kind else (0, 1)):
            gat.landed("own", l, k)
        for n in gat.of(l, kind):
            gat.ready(n)

    pending = None
    for l in range(layers):
        need(l, 0)
        if pending is not None:
            pending[0]()
        end_a = attn_front(
            l, items, frames, tab, vec, (w, x, qkv, pt, ob, r1), full[:2], asem, kept[l][:4], hooks(l, 0))
        for one in after[l][0]:
            step(*one)
        need(l, 1)
        if pending is not None:
            pending[1]()
        last = l == layers - 1
        end_f = ffn_front(
            l, last, items, frames, tab, vec, ub, (w_up, w_down, r1, x, n1b, g, gp, acc), full[2:], fsem,
            (*kept[l][4:], out_o if last else x1_o), hooks(l, 1))
        for one in after[l][1]:
            step(*one)
        pending = (end_a, end_f)
    pending[0]()
    pending[1]()
    gat.drain()


def fore(subnet, smalls, x, weights):
    layers = weights[0].shape[0]
    items, t, d = x.shape
    n = items * t
    ff = weights[2].shape[2]
    vm, dma = pltpu.VMEM, pltpu.SemaphoreType.DMA
    keep = [sds((3, n, d), BF), sds((items, HEADS, t, t), BF), sds((n, d), BF), sds((n, d), F32), sds((n, d), BF),
            sds((n, ff), BF), sds((n, ff), BF), sds((n, d), F32)]
    outs = [sds((layers, 4 * w.shape[1], w.shape[2]), BF) for w in weights] + [
        sds((layers, 8, d), F32), sds((layers, 1, ff), F32), sds((n, d), BF), sds((n, d), BF)] + keep * layers
    square = vm((n, d), BF)
    res = pl.pallas_call(
        functools.partial(fore_kernel, layers, items, t),
        out_shape=tuple(outs),
        in_specs=[SM] + [VM] * 8 + [ANY] * 5,
        out_specs=tuple(VM if k in (4, 5) else ANY for k in range(len(outs))),
        scratch_shapes=[
            vm((4, layers, 8, d), F32), *[vm(w.shape, BF) for w in weights], dma((200,)), dma((200,)), dma((2, 4, layers)),
            vm((4, d, d), BF), square, vm((3, n, d), BF), vm((items, HEADS, t, t), BF), square, vm((n, d), F32),
            vm((d, ff), BF), vm((ff, d), BF), square, vm((n, ff), BF), vm((n, ff), BF), vm((n, d), F32),
            dma((4,)), dma((5,)), dma((d // LANES,)), dma((ff // d, 2)), dma((3,)), dma((2, ff // FRONT_CHUNK)), dma((1,)),
        ],
        compiler_params=pltpu.CompilerParams(collective_id=0, has_side_effects=True, vmem_limit_bytes=60 * 2 ** 20),
        name="fore",
    )(subnet, *smalls, x.reshape(n, d), *weights)
    return res[:4], res[4], res[5], res[6], res[7], [res[8 + 8 * l:16 + 8 * l] for l in range(layers)]


def when(cond):
    if isinstance(cond, bool):
        return lambda f: f() if cond else None
    return pl.when(cond)


def both(a, b):
    return a and b if isinstance(a, bool) else jnp.logical_and(a, b)


class Reduce:
    LOC, RECV = 6, 6

    def __init__(self, count, bits, g, out, refs):
        self.count, self.bits, self.g, self.out = count, bits, g, out
        self.loc, self.rc, self.ry, self.rx, self.rz, self.fin, self.ss, self.rs, self.ls, self.os = refs
        f, pipe = lax.axis_index("fsdp"), lax.axis_index("pipe")
        self.c, self.y, x, z = f % 2, f // 2, pipe % 2, (pipe // 2) % 2
        rows = g.shape[3]
        half, quarter = rows // 2, rows // 4
        self.who = [flip("fsdp", 0), flip("fsdp", 1)] + [flip("pipe", b) for b in range(bits)]
        part = lambda at, n: pl.ds(pl.multiple_of(at, 16), n)
        self.my_half, self.their_half = part(x * half, half), part((1 - x) * half, half)
        self.mine, self.theirs = part(x * half + z * quarter, quarter), part(x * half + (1 - z) * quarter, quarter)
        self.n_red = 2 + bits
        self.total = self.n_red + 2
        self.slots = self.fin.shape[0]

    @staticmethod
    def scratch(bits, count, rows, d):
        vm, dma = pltpu.VMEM, pltpu.SemaphoreType.DMA
        n = bits + 4
        return [
            vm((Reduce.LOC, 2, rows, d), BF), vm((Reduce.RECV, 2, rows, d), BF), vm((Reduce.RECV, rows, d), BF),
            vm((Reduce.RECV, rows // 2, d), BF), vm((bits - 1, Reduce.RECV, rows // 4, d), BF), vm((n + 2, rows, d), BF),
            dma((n, count)), dma((n, count)), dma((count,)), dma((count,)),
        ]

    def load(self, p):
        return pltpu.make_async_copy(self.g.at[:, p, self.c], self.loc.at[p % self.LOC], self.ls.at[p])

    def store(self, p):
        return pltpu.make_async_copy(self.fin.at[p % self.slots], self.out.at[p], self.os.at[p])

    def move(self, k, p):
        loc, fin, r = self.loc.at[p % self.LOC], self.fin.at[p % self.slots], p % self.RECV
        if k == 0:
            src, dst, who = self.g.at[:, p, 1 - self.c], self.rc.at[r], 0
        elif k == 1:
            src, dst, who = loc.at[1 - self.y], self.ry.at[r], 1
        elif k == 2:
            src, dst, who = loc.at[self.y, self.their_half], self.rx.at[r], 2
        elif k == 3:
            src, dst, who = loc.at[self.y, self.theirs], self.rz.at[0, r], 3
        elif k < self.n_red:
            src, dst, who = fin.at[self.mine], self.rz.at[k - 3, r], k
        elif k == self.n_red:
            src, dst, who = fin.at[self.mine], fin.at[self.mine], 3
        else:
            src, dst, who = fin.at[self.my_half], fin.at[self.my_half], 2
        return pltpu.make_async_remote_copy(
            src_ref=src, dst_ref=dst, send_sem=self.ss.at[k, p], recv_sem=self.rs.at[k, p], device_id=self.who[who],
            device_id_type=MESH)

    def arrive(self, k, p):
        self.move(k, p).wait()
        s, f, r = p % self.LOC, p % self.slots, p % self.RECV
        if k == 0:
            self.load(p).wait()
            self.loc[s] = add_low(self.loc[s], self.rc[r])
        elif k == 1:
            self.loc[s, self.y] = add_low(self.loc[s, self.y], self.ry[r])
        elif k == 2:
            self.loc[s, self.y, self.my_half] = add_low(self.loc[s, self.y, self.my_half], self.rx[r])
        elif k == 3:
            self.fin[f, self.mine] = add_low(self.loc[s, self.y, self.mine], self.rz[0, r])
        elif k < self.n_red:
            self.fin[f, self.mine] = add_low(self.fin[f, self.mine], self.rz[k - 3, r])

    def begin(self):
        self.move(0, 0).start()
        self.load(0).start()

    def tick(self, t):
        @when(t + 1 < self.count)
        def _():
            self.move(0, t + 1).start()
            self.load(t + 1).start()

        for k in range(self.total):
            p = t - k - min(k, 1)

            @when(both(p >= 0, p < self.count))
            def _(k=k, p=p):
                self.arrive(k, p)
                if k + 1 < self.total:
                    self.move(k + 1, p).start()
                else:
                    self.store(p).start()

        p = t - self.total - 1

        @when(both(p >= 0, p < self.count))
        def _():
            self.store(p).wait()

    def ticks(self):
        return self.count + self.total + 1


def add_low(a, b):
    return a + b


class SumAll:
    def __init__(self, who, total, recv, ss, rs):
        self.who, self.total, self.recv, self.ss, self.rs = who, total, recv, ss, rs

    def move(self, k):
        return pltpu.make_async_remote_copy(
            src_ref=self.total, dst_ref=self.recv.at[k], send_sem=self.ss.at[k], recv_sem=self.rs.at[k],
            device_id=self.who[k], device_id_type=MESH)

    def step(self, k):
        for j in range(len(self.who) + 1):
            @pl.when(k == j)
            def _(j=j):
                if j > 0:
                    self.move(j - 1).wait()
                    self.total[...] = self.total[...] + self.recv[j - 1]
                if j < len(self.who):
                    self.move(j).start()


def attn_back(layer, items, frames, tab, src, buf, weights, sems, first, grads, tick, dx_out):
    qkv_any, pt_any, x_any, ob_any = src
    w, da, dr1, qkv, pt, x, ob, do, dqkv, dx, stage = buf
    wsem, sem, ptsem, qsem = sems
    width = da.shape[1]
    npair = width // LANES
    ring = pt.shape[0]
    p = Attn(layer, weights, w, wsem)
    p.start((3, 0, 1, 2))

    def block(ref, j):
        return ref.at[:, pl.ds(pl.multiple_of(j * width, LANES), width)]

    loads = [fetch(qkv_any.at[j], block(qkv, j), sem.at[3 + j]) for j in range(3)]

    def load_pt(c):
        return pltpu.make_async_copy(pt_any.at[:, pl.ds(2 * c, 2)], pt.at[c % ring], ptsem.at[c])

    for c in range(ring - 1):
        load_pt(c).start()
    later = [fetch(ob_any, ob, sem.at[0]), fetch(x_any, x, sem.at[1])]
    p.wait(3)
    dos = [dot_nt(da[rows_of(i, frames), :], w[3]) for i in range(items)]
    for i, d in enumerate(dos):
        do[rows_of(i, frames), :] = d.astype(BF)
    for o in loads:
        o.wait()
    scale = HEAD_DIM ** -0.5
    qsums = []

    def pair(c, _):
        for at in (0, 3):
            @pl.when(c == at)
            def _():
                tick()

        lanes = pl.ds(pl.multiple_of(c * LANES, LANES), LANES)
        ids = lax.broadcasted_iota(jnp.int32, (1, LANES), 1) + c * LANES
        load_pt(c).wait()

        @pl.when(c + ring - 1 < npair)
        def _():
            load_pt(c + ring - 1).start()

        rr = [rows_of(i, frames) for i in range(items)]
        at = [pl.ds(pl.multiple_of(j * width + c * LANES, LANES), LANES) for j in range(3)]
        q = [qkv[r, at[0]] for r in rr]
        k = [qkv[r, at[1]] for r in rr]
        v = [qkv[r, at[2]] for r in rr]
        dob = [do[r, lanes] for r in rr]
        kt = [a.T for a in k]
        heads = [(n, h) for n in range(items) for h in (0, 1)]
        pbs = [pt[c % ring, n, h] for n, h in heads]
        dps = [dot_nt(only(h, v[n]), dob[n]) for n, h in heads]
        dvs = [dot_nn(pb, dob[n]) for pb, (n, h) in zip(pbs, heads)]
        tmps = [pb.astype(F32) * dp for pb, dp in zip(pbs, dps)]
        dss = [(t - pb.astype(F32) * jnp.sum(t, axis=0, keepdims=True)).astype(BF) for t, pb in zip(tmps, pbs)]
        dks = [dot_nn(ds, q[n]) for ds, (n, h) in zip(dss, heads)]
        dqs = [dot_nn(kt[n][h * HEAD_DIM:(h + 1) * HEAD_DIM], ds) for ds, (n, h) in zip(dss, heads)]
        for n in range(items):
            on = ids < tab.a[n]
            put = lambda v, s: jnp.where(on, v * s, 0.0).astype(BF)
            dqkv[rr[n], at[0]] = put(jnp.concatenate(dqs[2 * n:2 * n + 2], axis=0).T, scale)
            dqkv[rr[n], at[1]] = put(jnp.where(half_mask(0), dks[2 * n], dks[2 * n + 1]), scale)
            dqkv[rr[n], at[2]] = put(jnp.where(half_mask(0), dvs[2 * n], dvs[2 * n + 1]), 1.0)
        return 0

    lax.fori_loop(0, npair, pair, 0)
    tick()
    q_sum = jnp.sum(dqkv[:, 0:width].astype(F32), axis=0, keepdims=True)
    for o in later:
        o.wait()
    if layer == 0:
        mask_rows(x, items, frames, tab)
    quarters = Quarters(stage, grads, qsem, first)
    rows = stage.shape[3]

    def step(lhs, rhs, b):
        for y in (0, 1):
            res = dot_tn(lhs[:, y * 2 * rows:(y + 1) * 2 * rows], rhs).astype(BF)
            for t in (0, 1):
                stage[y, b, t] = res[t * rows:(t + 1) * rows]
            quarters.start(y, b)

    def in_step(j, _):
        step(x, block(dqkv, j)[...], j)
        return 0

    lax.fori_loop(0, 3, in_step, 0)
    step(ob, da[...], 3)
    quarters.wait()
    tick()
    for j in range(3):
        p.wait(j)

    def back_step(j, _):
        adds = [dot_nt(block(dqkv, j)[rows_of(i, frames), :], w[j]) for i in range(items)]
        for i, add in enumerate(adds):
            dr1[rows_of(i, frames), :] += add
        return 0

    lax.fori_loop(0, 3, back_step, 0)
    for i in range(items):
        rr = rows_of(i, frames)
        dx[rr, :] = (dr1[rr, :] * lane_mask(width, tab.w[i])).astype(BF)
    if dx_out is not None:
        fetch(dx, dx_out, sem.at[2])
    return q_sum


def ffn_back(layer, last, items, frames, tab, vec, src, buf, weights, sems, first, grads, hooks, sums):
    cot_any, r2_any, r1_any, gp_any, g_any, n1b_any = src
    w_up, w_down, cot, dxn, r, du, g, n1b, df, acc, da, stage = buf
    wsem, sem, gsem, qsem = sems
    width, units = w_up.shape
    nblk, nch = units // width, units // UNIT_CHUNK
    rows = stage.shape[3]
    down = Quarters(stage, grads, qsem.at[0], first)
    up = Quarters(stage, grads, qsem.at[1], first + nblk)
    loads = [fetch(r2_any, r, sem.at[0]), fetch(cot_any, cot, sem.at[1])]
    load_g = fetch(g_any, g, sem.at[4])
    p = Ffn(layer, weights, w_up, w_down, wsem, UNIT_CHUNK)
    p.start()

    def load_gp(c):
        cols = pl.ds(pl.multiple_of(c * UNIT_CHUNK, UNIT_CHUNK), UNIT_CHUNK)
        return pltpu.make_async_copy(gp_any.at[:, cols], du.at[:, cols], gsem.at[c])

    for c in range(nch):
        load_gp(c).start()
    load_n1b = fetch(n1b_any, n1b, sem.at[3])
    for o in loads:
        o.wait()
    for i in range(items):
        rr = rows_of(i, frames)
        cm = lane_mask(width, tab.w[i])
        if last:
            dy = jnp.where(tab.skip[i] == 1, 0.0, cot[rr, :].astype(F32))
        else:
            dy = jnp.where(tab.skip[i] == 1, cot[rr, :], dxn[rr, :]).astype(F32)
        xhat, rstd = normed(r[rr, :], cm, tab.inv[i])
        dr2, dg, ds = norm_back(dy, xhat, rstd, vec[layer, ROW_G2:ROW_G2 + 1, :], cm, tab.inv[i])
        dfb = dr2.astype(BF)
        df[rr, :] = dfb
        acc[rr, :] = dr2
        sums[ROW_G2:ROW_G2 + 1, 0:width] += dg
        sums[ROW_B2:ROW_B2 + 1, 0:width] += ds
        sums[ROW_DB:ROW_DB + 1, 0:width] += jnp.sum(dfb.astype(F32), axis=0, keepdims=True)
    load_r1 = fetch(r1_any, r, sem.at[2])
    hooks["norm"]()
    load_g.wait()

    for s in range(nblk // 2):
        def down_step(f, _, s=s):
            y, par = f // 2, f % 2
            lanes = pl.ds(pl.multiple_of(f * width + s * 2 * rows, LANES), 2 * rows)
            res = dot_tn(g[:, lanes], df[...]).astype(BF)
            for t in (0, 1):
                stage[y, 2 * s + t, par] = res[t * rows:(t + 1) * rows]
            return 0

        lax.fori_loop(0, 4, down_step, 0)
        for b in (2 * s, 2 * s + 1):
            for y in (0, 1):
                down.start(y, b)
        if s == 0:
            down.wait_block(0)
            hooks["first"]()
    down.wait_block(1)
    hooks["down"]()

    def chunk(c, _):
        for at in (1, 4):
            @pl.when(c == at)
            def _(at=at):
                if at == 1:
                    for b in range(2, nblk):
                        down.wait_block(b)
                hooks["mid"]()

        p.before(c)
        load_gp(c).wait()
        cols = pl.ds(pl.multiple_of(c * UNIT_CHUNK, UNIT_CHUNK), UNIT_CHUNK)
        dgs = [dot_nt(df[rows_of(i, frames), :], w_down[cols, :]) for i in range(items)]
        dubs = []
        for i, dg in enumerate(dgs):
            dub = (dg * du[rows_of(i, frames), cols].astype(F32)).astype(BF)
            du[rows_of(i, frames), cols] = dub
            sums[ROW_UB:ROW_UB + 1, cols] += jnp.sum(dub.astype(F32), axis=0, keepdims=True)
            dubs.append(dub)
        for i, dub in enumerate(dubs):
            acc[rows_of(i, frames), :] += dot_nt(dub, w_up[:, cols])
        return 0

    lax.fori_loop(0, nch, chunk, 0)
    hooks["chunks"]()
    load_r1.wait()
    for i in range(items):
        rr = rows_of(i, frames)
        cm = lane_mask(width, tab.w[i])
        xhat, rstd = normed(r[rr, :], cm, tab.inv[i])
        d1, dg, ds = norm_back(acc[rr, :], xhat, rstd, vec[layer, ROW_G1:ROW_G1 + 1, :], cm, tab.inv[i])
        acc[rr, :] = d1
        dab = d1.astype(BF)
        da[rr, :] = dab
        sums[ROW_G1:ROW_G1 + 1, 0:width] += dg
        sums[ROW_B1:ROW_B1 + 1, 0:width] += ds
        sums[ROW_OB:ROW_OB + 1, 0:width] += jnp.sum(dab.astype(F32), axis=0, keepdims=True)
    hooks["norm1"]()
    load_n1b.wait()

    def up_step(j, _):
        cols = pl.ds(pl.multiple_of(j * width, LANES), width)
        for y in (0, 1):
            res = dot_tn(n1b[:, y * 2 * rows:(y + 1) * 2 * rows], du[:, cols]).astype(BF)
            for t in (0, 1):
                stage[y, j, t] = res[t * rows:(t + 1) * rows]
            up.start(y, j)
        return 0

    lax.fori_loop(0, nblk, up_step, 0)
    up.wait()
    hooks["up"]()


def back_kernel(items, frames, bits, blocks, subnet, vec, cot_any, x0_any, x1_any, *rest):
    kept, weights = (rest[:8], rest[8:16]), rest[16:20]
    (dx_o, grads, out, total, w_up, w, da, dr1, pt, x, ob, do, dx, r, du, g, stage, srecv) = rest[20:38]
    asem, bsem, fsem, gsem = rest[38:42], rest[42:46], rest[46:50], rest[50:54]
    red = Reduce(2 * blocks, bits, grads, out, rest[54:64])
    s_send, s_recv = rest[64:]
    width = da.shape[1]
    tab = Table(subnet, items, width)
    met = greet(red.who)
    total[...] = jnp.zeros_like(total)
    nb = w_up.shape[1] // width
    w_att, w_ffn = weights[:2], weights[2:]
    count = [0]

    def tick():
        red.tick(count[0])
        count[0] += 1

    def begin():
        met()
        red.begin()

    nothing = lambda: None
    att = lambda l: (kept[l][0], kept[l][1], (x0_any, x1_any)[l], kept[l][2])
    ffn = lambda l: (cot_any, kept[l][7], kept[l][3], kept[l][6], kept[l][5], kept[l][4])
    buf = (w, da, dr1, du, pt, x, ob, do, g, dx, stage)
    buf_f = (w_up, w.reshape(nb * width, width), x, dx, r, du, g, ob, do, dr1, da, stage)
    ffn_back(1, True, items, frames, tab, vec, ffn(1), buf_f, w_ffn, fsem, 0, grads,
             dict(norm=nothing, first=begin, down=tick, mid=tick, chunks=nothing, norm1=nothing, up=tick), total.at[1])
    total[1, ROW_QB:ROW_QB + 1, 0:width] = attn_back(
        1, items, frames, tab, att(1), buf, w_att, asem, 2 * nb, grads, tick, None)
    ffn_back(0, False, items, frames, tab, vec, ffn(0), buf_f, w_ffn, gsem, blocks, grads,
             dict(norm=tick, first=nothing, down=nothing, mid=tick, chunks=tick, norm1=tick, up=tick), total.at[0])
    total[0, ROW_QB:ROW_QB + 1, 0:width] = attn_back(
        0, items, frames, tab, att(0), buf, w_att, bsem, blocks + 2 * nb, grads, tick, dx_o)
    small = SumAll(red.who, total, srecv, s_send, s_recv)
    t = count[0]

    def rest_of(n, _):
        red.tick(n)
        small.step(n - t)
        return 0

    lax.fori_loop(t, red.ticks(), rest_of, 0)
    pltpu.make_async_copy(dx, dx_o, bsem[1].at[2]).wait()


def back(subnet, vec, cot, x0, x1, kept, weights):
    bits = 0
    while (1 << bits) < lax.axis_size("pipe"):
        bits += 1
    n, d = cot.shape
    items, _, t, _ = kept[0][1].shape
    ff = kept[0][5].shape[1]
    rows, nb = d // 4, ff // d
    blocks = 2 * nb + 4
    small = (2, 8, ff)
    vm, dma = pltpu.VMEM, pltpu.SemaphoreType.DMA
    square = vm((n, d), BF)
    hbm = (cot, x0, x1, *kept[0], *kept[1], *weights)
    asems = [dma((4,)), dma((6,)), dma((d // LANES,)), dma((2, 4))]
    fsems = [dma((nb, 2)), dma((5,)), dma((ff // UNIT_CHUNK,)), dma((2, 2, nb))]
    return pl.pallas_call(
        functools.partial(back_kernel, items, t, bits, blocks),
        out_shape=(sds((n, d), BF), sds((2, 2 * blocks, 2, rows, d), BF), sds((2 * blocks, rows, d), BF), sds(small, F32)),
        in_specs=[SM, VM] + [ANY] * len(hbm),
        out_specs=(ANY, ANY, ANY, VM),
        scratch_shapes=[
            vm((d, ff), BF), vm((4, d, d), BF), square, vm((n, d), F32), vm((3, items, 2, t, t), BF),
            square, square, square, square, vm((n, d), F32), vm((n, ff), BF), vm((n, ff), BF),
            vm((2, 4, 2, rows, d), BF), vm((2 + bits,) + small, F32),
            *asems, *asems, *fsems, *fsems, *Reduce.scratch(bits, 2 * blocks, rows, d), dma((2 + bits,)), dma((2 + bits,)),
        ],
        compiler_params=pltpu.CompilerParams(collective_id=1, has_side_effects=True, vmem_limit_bytes=60 * 2 ** 20),
        name="back",
    )(subnet, vec, *hbm)


def finish_kernel(layers, red, rows_a, rows_b, total, g_in, g_out, g_up, g_down, *rest):
    vecs, passed, (bf, f32, keep, sem_in, sem_out, sem_rows) = rest[:8], rest[8:10], rest[10:]
    f = lax.axis_index("fsdp")
    blocks = bf.shape[0]
    rows, d = bf.shape[1:]
    per = blocks // layers
    nb = (per - 4) // 2

    def target(l, k):
        if k < nb:
            return g_down.at[l, pl.ds(k * rows, rows)]
        if k < 2 * nb:
            return g_up.at[l, :, pl.ds((k - nb) * d, d)]
        if k < 2 * nb + 3:
            return g_in.at[l, :, pl.ds((k - 2 * nb) * d, d)]
        return g_out.at[l]

    loads = [pltpu.make_async_copy(red.at[p], bf.at[p], sem_in.at[p]) for p in range(blocks)]
    stores = [pltpu.make_async_copy(f32.at[p], target(layers - 1 - p // per, p % per), sem_out.at[p]) for p in range(blocks)]
    rows_in = [pltpu.make_async_copy(a, keep.at[k], sem_rows.at[0, k]) for k, a in enumerate((rows_a, rows_b))]
    rows_out = [pltpu.make_async_copy(keep.at[k], a, sem_rows.at[1, k]) for k, a in enumerate(passed)]
    for c in rows_in + loads:
        c.start()
    for came, goes in zip(rows_in, rows_out):
        came.wait()
        goes.start()
    for q in range(4):
        @pl.when(f == q)
        def _(q=q):
            for l in range(layers):
                for k in range(7):
                    vecs[k][l:l + 1, :] = total[l, k:k + 1, q * rows:(q + 1) * rows]
                vecs[7][l:l + 1, :] = total[l, 7:8, q * d:(q + 1) * d]
    for p in range(blocks):
        loads[p].wait()
        f32[p] = bf[p].astype(F32)
        stores[p].start()
    for c in stores + rows_out:
        c.wait()


def finish(red, rows_a, rows_b, total):
    blocks, rows, d = red.shape
    layers = total.shape[0]
    nb = (blocks // layers - 4) // 2
    return pl.pallas_call(
        functools.partial(finish_kernel, layers),
        out_shape=(sds((layers, rows, 3 * d), F32), sds((layers, rows, d), F32), sds((layers, rows, nb * d), F32),
                   sds((layers, nb * rows, d), F32)) + (sds((layers, rows), F32),) * 7 + (sds((layers, d), F32),)
        + (sds(rows_a.shape, BF), sds(rows_b.shape, BF)),
        in_specs=[ANY, ANY, ANY, VM],
        out_specs=(ANY,) * 4 + (VM,) * 8 + (ANY, ANY),
        scratch_shapes=[pltpu.VMEM(red.shape, BF), pltpu.VMEM(red.shape, F32), pltpu.VMEM((2,) + rows_a.shape, BF),
                        pltpu.SemaphoreType.DMA((blocks,)), pltpu.SemaphoreType.DMA((blocks,)),
                        pltpu.SemaphoreType.DMA((2, 2))],
        compiler_params=pltpu.CompilerParams(**PARAMS),
        name="finish",
    )(red, rows_a, rows_b, total)


def local(
    frames_in, attn_in, q_bias, attn_out, out_bias, norm1_gain, norm1_bias, ffn_up, up_bias, ffn_down, down_bias,
    norm2_gain, norm2_bias, subnet, out_cotangent,
):
    items, frames, width = frames_in.shape
    ff = ffn_up.shape[2]
    layers = attn_in.shape[0]
    nb = ff // width
    smalls = (q_bias, out_bias, norm1_gain, norm1_bias, down_bias, norm2_gain, norm2_bias, up_bias)
    n = items * frames
    weights, vec, ub, x1, layer_out, kept = fore(subnet, smalls, frames_in, (attn_in, attn_out, ffn_up, ffn_down))
    cot = out_cotangent.reshape(n, width)
    dx, _, red, total = back(subnet, vec, cot, frames_in.reshape(n, width), x1, kept, weights)
    g_in, g_out, g_up, g_down, g_qb, g_ob, g_g1, g_b1, g_db, g_g2, g_b2, g_ub, layer_out, dx = finish(
        red, layer_out, dx, total)
    return (layer_out.reshape(frames_in.shape), dx.reshape(frames_in.shape), g_in, g_qb, g_out, g_ob, g_g1, g_b1, g_up, g_ub, g_down, g_db, g_g2, g_b2)


def solution(mesh):
    rows3 = P(None, "fsdp", None)
    rows2 = P(None, "fsdp")
    item = P(("pipe", "fsdp"), None, None)
    weights = (rows3, rows2, rows3, rows2, rows2, rows2, rows3, rows2, rows3, rows2, rows2, rows2)
    return jax.shard_map(
        local, mesh=mesh, in_specs=(item,) + weights + (P(), item), out_specs=(item, item) + weights, check_vma=False,
    )
```
